32 devices in a mesh: dp: 8 (over z, y), tensor: 4 (over x, core).
Axes of the slice: x: 2, y: 2, z: 4, core: 2. Of those that a mesh axis runs over, the one named last changes fastest.
Arguments:
- tokens: bfloat16 [16384, 768], P(('dp', 'tensor')), may hold values from -12 to 12
- grad_out: bfloat16 [16384, 768], P(('dp', 'tensor')), may hold values from -6 to 6
- lengths: int32 [32], P('dp'), may hold values from 204 to 512, as said below
- segment_ids: int32 [32, 512], P('dp'), may hold values from 0 to 3, never falling along the last dimension, each value on 1 to 256 neighbouring positions
- query_weight: bfloat16 [768, 768], P(None, 'tensor'), may hold values from -0.21875 to 0.21875
- query_bias: bfloat16 [768], P('tensor'), may hold values from -3 to 3
- key_weight: bfloat16 [768, 768], P(None, 'tensor'), may hold values from -0.21875 to 0.21875
- value_weight: bfloat16 [768, 768], P(None, 'tensor'), may hold values from -0.21875 to 0.21875
- value_bias: bfloat16 [768], P('tensor'), may hold values from -3 to 3
- mixer_weight: bfloat16 [768, 768], P('tensor'), may hold values from -0.625 to 0.625
- mixer_bias: bfloat16 [768], replicated, may hold values from -3 to 3
- first_gain: bfloat16 [768], replicated, may hold values from 0.5 to 1.5
- first_shift: bfloat16 [768], replicated, may hold values from -2 to 2
- inner_weight: bfloat16 [768, 3072], P(None, 'tensor'), may hold values from -0.21875 to 0.21875
- inner_bias: bfloat16 [3072], P('tensor'), may hold values from -3 to 3
- outer_weight: bfloat16 [3072, 768], P('tensor'), may hold values from -0.109375 to 0.109375
- outer_bias: bfloat16 [768], replicated, may hold values from -2 to 2
- second_gain: bfloat16 [768], replicated, may hold values from 0.5 to 1.5
- second_shift: bfloat16 [768], replicated, may hold values from -2 to 2
Outputs:
- layer_out: bfloat16 [16384, 768], P(('dp', 'tensor'))
- tokens_grad: float32 [16384, 768], P(('dp', 'tensor'))
- query_weight_grad: float32 [768, 768], P(None, 'tensor')
- query_bias_grad: float32 [768], P('tensor')
- key_weight_grad: float32 [768, 768], P(None, 'tensor')
- value_weight_grad: float32 [768, 768], P(None, 'tensor')
- value_bias_grad: float32 [768], P('tensor')
- mixer_weight_grad: float32 [768, 768], P('tensor')
- mixer_bias_grad: float32 [768], replicated
- first_gain_grad: float32 [768], replicated
- first_shift_grad: float32 [768], replicated
- inner_weight_grad: float32 [768, 3072], P(None, 'tensor')
- inner_bias_grad: float32 [3072], P('tensor')
- outer_weight_grad: float32 [3072, 768], P('tensor')
- outer_bias_grad: float32 [768], replicated
- second_gain_grad: float32 [768], replicated
- second_shift_grad: float32 [768], replicated
- statistics: float32 [3], replicated
The draws below stay inside these ranges and needn't reach their ends.
Inputs may be any that keep to these rules, and one draw needn't show every extreme that they name: `lengths`: the first sequence holds (1024) // 5 tokens and the last is full. `segment_ids`: never fall along a sequence; a segment holds at most 256 rows.
All inputs are finite; a program needn't handle non-finite values.
Results may differ from the reference program's by a relative error of at most 0.018.
Values may be sent and summed in bfloat16 or wider, within the bound.
No kernel may reach another device: no remote copies, remote signals or barrier semaphores. Data moves between devices by JAX's collectives and lax.ppermute only.
A program may use at most 128 MiB of HBM per device.

```python
import math
import jax
import jax.numpy as jnp
import numpy as np
from jax import lax

D = 768
HEADS = 12
HEAD_DIM = 64
FF = 3072
L = 512
SEQS = 32
TOKENS = 16384


def draw_tokens(key, part):
    row_order = jnp.arange(TOKENS, dtype=jnp.float32) / TOKENS
    scale_rows = 0.75 + 1.25 * row_order
    base_draw = jax.random.truncated_normal(key, -6.0, 6.0, (TOKENS, D), jnp.float32)
    return (base_draw * scale_rows[:, None]).astype(jnp.bfloat16)


def draw_lengths(key, part):
    seq_index = jnp.arange(SEQS, dtype=jnp.int32)
    lowest = 2 * L // 5 + 3 * L * seq_index // (5 * SEQS)
    jitter = jax.random.randint(key, (SEQS,), 0, L // 10 + 1, dtype=jnp.int32)
    drawn = jnp.minimum(lowest + jitter, L)
    drawn = jnp.where(seq_index == 0, 2 * L // 5, drawn)
    return jnp.where(seq_index == SEQS - 1, L, drawn).astype(jnp.int32)


def block_scale(key, dims, split, low, top_value):
    gain, own = 1.0, jax.random.fold_in(key, 6)
    for axis_at, parts in split:
        steps = jnp.exp(jax.random.uniform(jax.random.fold_in(own, axis_at), (parts,), jnp.float32, low / len(split), top_value / len(split)))
        gain = gain * jnp.repeat(steps, dims[axis_at] // parts).reshape([-1 if axis == axis_at else 1 for axis in range(len(dims))])
    return gain


def split_up(count, total, most, skew):
    loads = [(1 << 20) // math.isqrt(grade ** skew) + 1 for grade in range(2, count + 1)]
    spare, holding = total - most - (count - 1), [1] * (count - 1)
    while spare > 0:
        candidates = [i for i in range(count - 1) if holding[i] < most]
        mass, budget = sum([loads[i] for i in candidates]), spare
        for i in candidates:
            more = min(most - holding[i], max(1, budget * loads[i] // mass), spare)
            holding[i] = holding[i] + more
            spare = spare - more
    return np.array([most] + holding)


def uneven(rng, amount, total, most, skew):
    if amount == 2:
        one = jax.random.randint(rng, (), max(1, total - most), min(most, total - 1) + 1)
        return jnp.stack([one, total - one])
    sizes = jnp.asarray(split_up(amount, total, most, skew), jnp.int32)
    twos = (amount - 1) // 2
    giver, taker = sizes[1:1 + 2 * twos:2], sizes[2:2 + 2 * twos:2]
    room = jnp.minimum(giver - 1, most - taker)
    passed = jax.random.randint(jax.random.fold_in(rng, 1), (twos,), 0, 1 << 20) % (room + 1)
    sizes = sizes.at[1:1 + 2 * twos:2].set(giver - passed).at[2:2 + 2 * twos:2].set(taker + passed)
    return sizes[jax.random.permutation(jax.random.fold_in(rng, 2), amount)]


def noise(stream_key, dims, spread, limit, cuts=(), held_as=jnp.bfloat16):
    gain = block_scale(stream_key, dims, cuts, -0.22, 0.18) if cuts else 1.0
    entries = jax.random.normal(stream_key, dims, jnp.float32) * spread * gain
    return jnp.minimum(jnp.maximum(entries, -limit), limit).astype(held_as)


def setup_inputs(seed: int = 0) -> dict:
    key_list = jax.random.split(jax.random.key(seed), 20)
    tokens = draw_tokens(jax.random.fold_in(key_list[19], 71), 0)
    grad_out = noise(key_list[1], (TOKENS, D), 1.0, 6.0, ((0, 32),))
    lengths = draw_lengths(jax.random.fold_in(key_list[19], 71), 0)
    segment_ids = jax.vmap(lambda own: jnp.searchsorted(jnp.cumsum(uneven(own, 4, L, L // 2, 0)), jnp.arange(L), side="right"))(jax.random.split(key_list[3], SEQS)).reshape((SEQS, L)).astype(jnp.int32)
    query_weight = noise(key_list[4], (D, D), D ** -0.5, 0.21875, ((1, 4),))
    query_bias = noise(key_list[5], (D,), 0.5, 3.0, ((0, 4),))
    key_weight = noise(key_list[6], (D, D), D ** -0.5, 0.21875, ((1, 4),))
    value_weight = noise(key_list[7], (D, D), D ** -0.5, 0.21875, ((1, 4),))
    value_bias = noise(key_list[8], (D,), 0.5, 3.0, ((0, 4),))
    mixer_weight = noise(key_list[9], (D, D), (D // 8) ** -0.5, 0.625, ((0, 4),))
    mixer_bias = noise(key_list[10], (D,), 0.5, 3.0)
    first_gain = jnp.clip(1.0 + 0.1 * jax.random.normal(key_list[11], (D,), jnp.float32), 0.5, 1.5).astype(jnp.bfloat16)
    first_shift = noise(key_list[12], (D,), 0.3, 2.0)
    inner_weight = noise(key_list[13], (D, FF), D ** -0.5, 0.21875, ((1, 4),))
    inner_bias = noise(key_list[14], (FF,), 0.5, 3.0, ((0, 4),))
    outer_weight = noise(key_list[15], (FF, D), FF ** -0.5, 0.109375, ((0, 4),))
    outer_bias = noise(key_list[16], (D,), 0.3, 2.0)
    second_gain = jnp.clip(1.0 + 0.1 * jax.random.normal(key_list[17], (D,), jnp.float32), 0.5, 1.5).astype(jnp.bfloat16)
    second_shift = noise(key_list[18], (D,), 0.3, 2.0)
    return {"tokens": tokens, "grad_out": grad_out, "lengths": lengths, "segment_ids": segment_ids, "query_weight": query_weight, "query_bias": query_bias, "key_weight": key_weight, "value_weight": value_weight, "value_bias": value_bias, "mixer_weight": mixer_weight, "mixer_bias": mixer_bias, "first_gain": first_gain, "first_shift": first_shift, "inner_weight": inner_weight, "inner_bias": inner_bias, "outer_weight": outer_weight, "outer_bias": outer_bias, "second_gain": second_gain, "second_shift": second_shift}


eps_norm = 1e-06
highest = lax.Precision.HIGHEST

@jax.custom_vjp
def low(v):
    return lax.optimization_barrier(v.astype(jnp.bfloat16)).astype(jnp.float32)

@jax.custom_vjp
def low_back(v):
    return v

def low_keep(v):
    return (low(v), None)

def low_pass(kept, grad):
    return (grad,)

def back_keep(v):
    return (v, None)

def back_low(kept, grad):
    return (low(grad),)
low.defvjp(low_keep, low_pass)
low_back.defvjp(back_keep, back_low)

def matmul(left_side, right_side):
    return jnp.dot(left_side, right_side, precision=highest, preferred_element_type=jnp.float32)

def layer_norm(token_rows, norm_gain, norm_shift):
    center = token_rows - lax.optimization_barrier(jnp.mean(token_rows, axis=-1, keepdims=True))
    inverse = lax.rsqrt(lax.optimization_barrier(jnp.mean(center * center, axis=-1, keepdims=True)) + eps_norm)
    return center * inverse * norm_gain + norm_shift

def allowed_pairs(segment_row, seq_length):
    position = jnp.arange(L, dtype=jnp.int32)
    same_doc = segment_row[:, None] == segment_row[None, :]
    live_key = position[None, :] < seq_length
    return same_doc & live_key | (position[:, None] == position[None, :])

def attend_packed(packed):
    queries, key_rows, values, segment_row, seq_length = packed
    raw_scores = low_back(jnp.einsum('qhd,khd->hqk', queries, key_rows, precision=highest))
    scores = jnp.where(allowed_pairs(segment_row, seq_length)[None], raw_scores * float(HEAD_DIM) ** (-0.5), -1e+30)
    softmax_out = jax.nn.softmax(scores, axis=-1)
    return jnp.einsum('hqk,khd->qhd', low(softmax_out), values, precision=highest)

def forward(params, token_rows, segments, block_lengths):
    query_weight, query_bias, key_weight, value_weight, value_bias, mixer_weight, mixer_bias, first_gain, first_shift, inner_weight, inner_bias, outer_weight, outer_bias, second_gain, second_shift = params
    seq_count = segments.shape[0]
    queries = low(low_back(matmul(token_rows, query_weight)) + query_bias)
    key_rows = low(low_back(matmul(token_rows, key_weight)))
    values = low(low_back(matmul(token_rows, value_weight)) + value_bias)
    head_shape = (seq_count, L, HEADS, HEAD_DIM)
    attended = lax.map(jax.checkpoint(attend_packed), (queries.reshape(head_shape), key_rows.reshape(head_shape), values.reshape(head_shape), segments, block_lengths))
    attended = low_back(low(attended.reshape(seq_count * L, D)))
    attn_branch = low_back(matmul(attended, mixer_weight)) + mixer_bias
    normed_one = layer_norm(token_rows + attn_branch, first_gain, first_shift)
    inner_pre = low_back(matmul(low(normed_one), inner_weight)) + inner_bias
    activated = low(jax.nn.gelu(inner_pre, approximate=False))
    ffn_branch = low_back(matmul(activated, outer_weight)) + outer_bias
    result = layer_norm(normed_one + ffn_branch, second_gain, second_shift)
    return (result, (attn_branch, ffn_branch))

def reference(tokens, grad_out, lengths, segment_ids, query_weight, query_bias, key_weight, value_weight, value_bias, mixer_weight, mixer_bias, first_gain, first_shift, inner_weight, inner_bias, outer_weight, outer_bias, second_gain, second_shift):
    params = tuple((weight_arg.astype(jnp.float32) for weight_arg in (query_weight, query_bias, key_weight, value_weight, value_bias, mixer_weight, mixer_bias, first_gain, first_shift, inner_weight, inner_bias, outer_weight, outer_bias, second_gain, second_shift)))
    group_size = math.gcd(SEQS, 8)
    blocks = SEQS // group_size
    rows_all = tokens.astype(jnp.float32).reshape(blocks, group_size * L, D)
    cotangents = grad_out.astype(jnp.float32).reshape(blocks, group_size * L, D)
    segments_all = segment_ids.reshape(blocks, group_size, L)
    lengths_all = lengths.reshape(blocks, group_size)

    def scan_step(carried, inputs):
        totals, stat_sums = carried
        token_rows, cotangent, segments, block_lengths = inputs
        result, pullback, branches = jax.vjp(lambda param_set, row_set: forward(param_set, row_set, segments, block_lengths), params, token_rows, has_aux=True)
        param_grads, rows_grad = pullback(cotangent)
        position = jnp.arange(L, dtype=jnp.int32)
        valid_rows = (position[None, :] < block_lengths[:, None]).reshape(group_size * L).astype(jnp.float32)
        stat_terms = jnp.stack([jnp.sum(valid_rows * lax.optimization_barrier(jnp.sum(token_rows * token_rows, axis=-1))), jnp.sum(valid_rows * lax.optimization_barrier(jnp.sum(branches[0] * branches[0], axis=-1))), jnp.sum(valid_rows * lax.optimization_barrier(jnp.sum(branches[1] * branches[1], axis=-1))), jnp.sum(valid_rows)])
        totals = jax.tree.map(lambda first_term, second_term: first_term + second_term, totals, param_grads)
        return ((totals, stat_sums + stat_terms), (result.astype(jnp.bfloat16), rows_grad))
    initial = (jax.tree.map(jnp.zeros_like, params), jnp.zeros((4,), jnp.float32))
    (totals, stat_sums), (outputs, row_grads) = lax.scan(scan_step, initial, (rows_all, cotangents, segments_all, lengths_all))
    statistics = jnp.sqrt(stat_sums[:3] / (stat_sums[3] * D))
    return (outputs.reshape(TOKENS, D), row_grads.reshape(TOKENS, D), totals[0], totals[1], totals[2], totals[3], totals[4], totals[5], totals[6], totals[7], totals[8], totals[9], totals[10], totals[11], totals[12], totals[13], totals[14], statistics)
```

```python
import jax
import jax.numpy as jnp
from jax import lax
from jax.experimental import pallas as pl
from jax.experimental.pallas import tpu as pltpu
from jax.sharding import PartitionSpec as P

D = 768
HEAD_DIM = 64
L = 512

eps_norm = 1e-06
root_half = 0.7071067811865476
inv_root_tau = 0.3989422804014327
low_type = jnp.bfloat16
wide = jnp.float32
NN = (((1,), (0,)), ((), ()))
NT = (((1,), (1,)), ((), ()))
TN = (((0,), (0,)), ((), ()))


def product(left, right, dims):
    return lax.dot_general(left, right, dims, preferred_element_type=wide)


def layer_norm(token_rows, norm_gain, norm_shift):
    center = token_rows - jnp.mean(token_rows, axis=-1, keepdims=True)
    inverse = lax.rsqrt(jnp.mean(center * center, axis=-1, keepdims=True) + eps_norm)
    normed = center * inverse
    return (normed * norm_gain + norm_shift, normed, inverse)


def norm_backward(incoming, normed, inverse, norm_gain):
    scaled = incoming * norm_gain
    middle = jnp.mean(scaled, axis=-1, keepdims=True)
    along = jnp.mean(scaled * normed, axis=-1, keepdims=True)
    return inverse * (scaled - middle - normed * along)


def attend_forward(tokens, projection, owner_column, owner_row):
    width = projection.shape[0] // 3 // HEAD_DIM * HEAD_DIM
    heads = width // HEAD_DIM

    def kernel(tokens_ref, projection_ref, column_ref, row_ref, qkv_ref, attended_ref, probs_ref, mask):
        bias = projection_ref[3 * width : 3 * width + 1, : 3 * width].astype(wide)
        qkv_ref[...] = (
            product(tokens_ref[...], projection_ref[: 3 * width, :], NT) + bias
        ).astype(low_type)
        row = lax.broadcasted_iota(jnp.int32, (L, L), 0)
        column = lax.broadcasted_iota(jnp.int32, (L, L), 1)
        allowed = (column_ref[...] == row_ref[...]) | (row == column)
        mask[...] = jnp.where(allowed, 0.0, -1e30)
        for head in range(heads):
            at = head * HEAD_DIM
            queries = qkv_ref[:, at : at + HEAD_DIM] * jnp.asarray(HEAD_DIM**-0.5, low_type)
            key_rows = qkv_ref[:, width + at : width + at + HEAD_DIM]
            values = qkv_ref[:, 2 * width + at : 2 * width + at + HEAD_DIM]
            scores = product(queries, key_rows, NT) + mask[...]
            highest = jnp.max(scores, axis=-1, keepdims=True)
            expanded = jnp.exp(scores - highest)
            row_total = jnp.sum(expanded, axis=-1, keepdims=True)
            probs = (expanded * (1.0 / row_total)).astype(low_type)
            probs_ref[head] = probs
            attended_ref[:, at : at + HEAD_DIM] = product(probs, values, NN).astype(low_type)

    return pl.pallas_call(
        kernel,
        out_shape=(
            jax.ShapeDtypeStruct((L, 3 * width), low_type),
            jax.ShapeDtypeStruct((L, width), low_type),
            jax.ShapeDtypeStruct((heads, L, L), low_type),
        ),
        scratch_shapes=[pltpu.VMEM((L, L), wide)],
        cost_estimate=pl.CostEstimate(
            flops=9 * L * D * width, transcendentals=heads * L * L, bytes_accessed=16000000
        ),
        name="attend_forward",
    )(tokens, projection, owner_column, owner_row)


def attend_backward(branch_low, mixer, qkv, attended, probs):
    width = attended.shape[1]
    heads = width // HEAD_DIM

    def kernel(branch_ref, mixer_ref, qkv_ref, attended_ref, probs_ref, grad_ref):
        attended_grad = product(branch_ref[...], mixer_ref[:width, :], NT).astype(low_type)
        for head in range(heads):
            at = head * HEAD_DIM
            queries = qkv_ref[:, at : at + HEAD_DIM] * jnp.asarray(HEAD_DIM**-0.5, low_type)
            key_rows = qkv_ref[:, width + at : width + at + HEAD_DIM]
            values = qkv_ref[:, 2 * width + at : 2 * width + at + HEAD_DIM]
            grad = attended_grad[:, at : at + HEAD_DIM]
            along = attended_ref[:, at : at + HEAD_DIM].astype(wide) * grad.astype(wide)
            row_dot = jnp.sum(along, axis=-1, keepdims=True)
            probs = probs_ref[head]
            probs_grad = product(grad, values, NT)
            scores_grad = (probs.astype(wide) * (probs_grad - row_dot)).astype(low_type)
            grad_ref[:, at : at + HEAD_DIM] = (
                product(scores_grad, key_rows, NN) * (HEAD_DIM**-0.5)
            ).astype(low_type)
            grad_ref[:, width + at : width + at + HEAD_DIM] = product(
                scores_grad, queries, TN
            ).astype(low_type)
            grad_ref[:, 2 * width + at : 2 * width + at + HEAD_DIM] = product(
                probs, grad, TN
            ).astype(low_type)

    return pl.pallas_call(
        kernel,
        out_shape=jax.ShapeDtypeStruct((L, 3 * width), low_type),
        cost_estimate=pl.CostEstimate(
            flops=9 * L * D * width, transcendentals=0, bytes_accessed=16000000
        ),
        name="attend_backward",
    )(branch_low, mixer, qkv, attended, probs)


def inner_forward(normed_low, weights, start):
    block = L // 2
    rows = weights.shape[0]

    def kernel(normed_ref, weights_ref, activated_ref, slope_ref):
        inner_pre = product(
            normed_ref[...], weights_ref[start : start + D, :], NN
        ) + weights_ref[start + D : start + D + 1, :].astype(wide)
        below = 0.5 * (1.0 + lax.erf(inner_pre * root_half))
        density = jnp.exp(-0.5 * inner_pre * inner_pre) * inv_root_tau
        activated_ref[...] = (inner_pre * below).astype(low_type)
        slope_ref[...] = (below + inner_pre * density).astype(low_type)

    return pl.pallas_call(
        kernel,
        grid=(L // block,),
        out_shape=(jax.ShapeDtypeStruct((L, D), low_type),) * 2,
        in_specs=[
            pl.BlockSpec((block, D), lambda i: (i, 0)),
            pl.BlockSpec((rows, D), lambda i: (0, 0)),
        ],
        out_specs=[pl.BlockSpec((block, D), lambda i: (i, 0))] * 2,
        cost_estimate=pl.CostEstimate(
            flops=8 * L * D * D, transcendentals=2 * L * D, bytes_accessed=16000000
        ),
        name="inner_forward",
    )(normed_low, weights)


def solution(mesh):
    dp_size = mesh.shape["dp"]
    tensor_size = mesh.shape["tensor"]
    masks = [1, 2, 6] + [1 << bit for bit in range(3, 16)]
    masks = masks[: dp_size.bit_length() - 1]

    def over_tensor(value, mask):
        return lax.ppermute(value, "tensor", [(i, i ^ mask) for i in range(tensor_size)])

    def over_dp(value, mask):
        return lax.ppermute(value, "dp", [(i, i ^ mask) for i in range(dp_size)])

    def gather_slots(own):
        first = over_tensor(own, 1)
        second = over_tensor(own, 2)
        return [own, first, second, over_tensor(second, 1)]

    def add_low(left, right):
        return (left.astype(wide) + right.astype(wide)).astype(low_type)

    def reduce_weight(kept, sent):
        total = add_low(kept, over_tensor(sent, 2))
        for mask in masks[:-1]:
            total = add_low(total, over_dp(total, mask))
        return total.astype(wide) + over_dp(total, masks[-1]).astype(wide)

    def body(
        tokens,
        grad_out,
        lengths,
        segment_ids,
        query_weight,
        query_bias,
        key_weight,
        value_weight,
        value_bias,
        mixer_weight,
        mixer_bias,
        first_gain,
        first_shift,
        inner_weight,
        inner_bias,
        outer_weight,
        outer_bias,
        second_gain,
        second_shift,
    ):
        width = query_weight.shape[1]
        place = lax.axis_index("tensor")
        bias_row = jnp.concatenate([query_bias, jnp.zeros_like(query_bias), value_bias])
        bias_row = jnp.pad(bias_row[None, :], ((0, 15), (0, D - 3 * width)))
        own_projection = jnp.concatenate(
            [query_weight.T, key_weight.T, value_weight.T, bias_row], axis=0
        )
        own_middle = jnp.concatenate(
            [mixer_weight, inner_weight, jnp.pad(inner_bias[None, :], ((0, 15), (0, 0)))], axis=0
        )
        projections = gather_slots(own_projection)
        middles = gather_slots(own_middle)
        outers = gather_slots(outer_weight)

        segment_row = lax.dynamic_index_in_dim(segment_ids, place, 0, keepdims=False)
        own_length = lax.dynamic_index_in_dim(lengths, place, 0, keepdims=False)
        position = jnp.arange(L, dtype=jnp.int32)
        live = position < own_length
        owner_column = segment_row[:, None]
        owner_row = jnp.where(live, segment_row, -1)[None, :]

        heads_out = [attend_forward(tokens, w, owner_column, owner_row) for w in projections]
        attn_branch = mixer_bias.astype(wide)
        for (_, attended, _), weights in zip(heads_out, middles):
            attn_branch = attn_branch + product(attended, weights[:width], NN)
        token_float = tokens.astype(wide)
        normed_one, first_hat, first_inverse = layer_norm(
            token_float + attn_branch, first_gain, first_shift
        )
        normed_low = normed_one.astype(low_type)
        hidden = [inner_forward(normed_low, weights, width) for weights in middles]
        ffn_branch = outer_bias.astype(wide)
        for (activated, _), weights in zip(hidden, outers):
            ffn_branch = ffn_branch + product(activated, weights, NN)
        layer_out, second_hat, second_inverse = layer_norm(
            normed_one + ffn_branch, second_gain, second_shift
        )
        valid = live.astype(wide)[:, None]
        stat_terms = jnp.stack(
            [
                jnp.sum(valid * token_float * token_float),
                jnp.sum(valid * attn_branch * attn_branch),
                jnp.sum(valid * ffn_branch * ffn_branch),
                jnp.sum(valid),
            ]
        )
        incoming = grad_out.astype(wide)
        second_gain_grad = jnp.sum(incoming * second_hat, axis=0)
        second_shift_grad = jnp.sum(incoming, axis=0)
        second_grad = norm_backward(incoming, second_hat, second_inverse, second_gain)
        outer_bias_grad = jnp.sum(second_grad, axis=0)
        ffn_low = second_grad.astype(low_type)

        def pair_product(left, right, left_other, right_other):
            return (
                product(left, right, TN) + product(left_other, right_other, TN)
            ).astype(low_type)

        ffn_other = over_tensor(ffn_low, 1)
        normed_other = over_tensor(normed_low, 1)
        activated_other = {j: over_tensor(hidden[j ^ 1][0], 1) for j in (0, 2)}
        outer_parts = {
            j: pair_product(hidden[j][0], ffn_low, activated_other[j], ffn_other) for j in (2, 0)
        }
        outer_weight_grad = reduce_weight(outer_parts[0], outer_parts[2])

        normed_grad = second_grad
        inner_lows, inner_bias_rows = [], []
        for (_, slope), outer, middle in zip(hidden, outers, middles):
            inner_grad = product(ffn_low, outer, NT) * slope.astype(wide)
            inner_bias_rows.append(jnp.sum(inner_grad, axis=0))
            inner_lows.append(inner_grad.astype(low_type))
        inner_other = {j: over_tensor(inner_lows[j ^ 1], 1) for j in (0, 2)}
        inner_parts = {
            j: pair_product(normed_low, inner_lows[j], normed_other, inner_other[j]) for j in (2, 0)
        }
        inner_weight_grad = reduce_weight(inner_parts[0], inner_parts[2])
        for inner_low, middle in zip(inner_lows, middles):
            normed_grad = normed_grad + product(inner_low, middle[width : width + D], NT)

        first_gain_grad = jnp.sum(normed_grad * first_hat, axis=0)
        first_shift_grad = jnp.sum(normed_grad, axis=0)
        first_grad = norm_backward(normed_grad, first_hat, first_inverse, first_gain)
        mixer_bias_grad = jnp.sum(first_grad, axis=0)
        branch_low = first_grad.astype(low_type)
        branch_other = over_tensor(branch_low, 1)
        attended_other = {j: over_tensor(heads_out[j ^ 1][1], 1) for j in (0, 2)}
        mixer_parts = {
            j: pair_product(heads_out[j][1], branch_low, attended_other[j], branch_other)
            for j in (2, 0)
        }
        mixer_weight_grad = reduce_weight(mixer_parts[0], mixer_parts[2])

        qkv_grads = [
            attend_backward(branch_low, middle, *kept)
            for kept, middle in zip(heads_out, middles)
        ]
        tokens_other = over_tensor(tokens, 1)
        qkv_other = {j: over_tensor(qkv_grads[j ^ 1], 1) for j in (0, 2)}
        qkv_parts = {
            j: pair_product(qkv_grads[j], tokens, qkv_other[j], tokens_other) for j in (2, 0)
        }
        qkv_weight_grad = reduce_weight(qkv_parts[0], qkv_parts[2])
        tokens_grad = first_grad
        for qkv_grad, projection in zip(qkv_grads, projections):
            tokens_grad = tokens_grad + product(qkv_grad, projection[: 3 * width], NN)

        def lane_pad(row):
            return jnp.pad(row, (0, D - row.shape[0]))

        bias_rows = [jnp.sum(qkv_grad.astype(wide), axis=0) for qkv_grad in qkv_grads]
        small = jnp.stack(
            [
                mixer_bias_grad,
                first_gain_grad,
                first_shift_grad,
                outer_bias_grad,
                second_gain_grad,
                second_shift_grad,
                lane_pad(stat_terms),
                jnp.zeros((D,), wide),
            ]
            + inner_bias_rows
            + [lane_pad(row) for row in bias_rows]
        )

        def reorder(rows, mask):
            slots = [8 + (j ^ mask) for j in range(4)] + [12 + (j ^ mask) for j in range(4)]
            return jnp.concatenate([rows[:8]] + [rows[i : i + 1] for i in slots])

        small = small + reorder(over_tensor(small, 1), 1)
        small = small + reorder(over_tensor(small, 2), 2)
        for mask in masks:
            small = small + over_dp(small, mask)
        statistics = jnp.sqrt(small[6, :3] / (small[6, 3] * D))
        return (
            layer_out.astype(low_type),
            tokens_grad,
            qkv_weight_grad[:width].T,
            small[12, :width],
            qkv_weight_grad[width : 2 * width].T,
            qkv_weight_grad[2 * width :].T,
            small[12, 2 * width : 3 * width],
            mixer_weight_grad,
            small[0],
            small[1],
            small[2],
            inner_weight_grad,
            small[8],
            outer_weight_grad,
            small[3],
            small[4],
            small[5],
            statistics,
        )

    in_specs = (
        P(("dp", "tensor"), None),
        P(("dp", "tensor"), None),
        P("dp"),
        P("dp", None),
        P(None, "tensor"),
        P("tensor"),
        P(None, "tensor"),
        P(None, "tensor"),
        P("tensor"),
        P("tensor", None),
        P(),
        P(),
        P(),
        P(None, "tensor"),
        P("tensor"),
        P("tensor", None),
        P(),
        P(),
        P(),
    )
    out_specs = (
        P(("dp", "tensor"), None),
        P(("dp", "tensor"), None),
        P(None, "tensor"),
        P("tensor"),
        P(None, "tensor"),
        P(None, "tensor"),
        P("tensor"),
        P("tensor", None),
        P(),
        P(),
        P(),
        P(None, "tensor"),
        P("tensor"),
        P("tensor", None),
        P(),
        P(),
        P(),
        P(),
    )
    return jax.shard_map(body, mesh=mesh, in_specs=in_specs, out_specs=out_specs, check_vma=False)
```

```python
import jax
import jax.numpy as jnp
from jax import lax
from jax.experimental import pallas as pl
from jax.experimental.pallas import tpu as pltpu
from jax.sharding import PartitionSpec as P

D = 768
HEAD_DIM = 64
L = 512
EXTRA = 32

eps_norm = 1e-06
root_half = 0.7071067811865476
inv_root_tau = 0.3989422804014327
low_type = jnp.bfloat16
wide = jnp.float32
NN = (((1,), (0,)), ((), ()))
NT = (((1,), (1,)), ((), ()))
TN = (((0,), (0,)), ((), ()))


def product(left, right, dims):
    return lax.dot_general(left, right, dims, preferred_element_type=wide)


def whole(shape):
    return pl.BlockSpec(shape, lambda *_: (0,) * len(shape), pipeline_mode=pl.Buffered(1))


def shaped(shape, dtype):
    return jax.ShapeDtypeStruct(shape, dtype)


def cost(micros):
    return pl.CostEstimate(
        flops=int(micros * 1e6 * 300), transcendentals=0, bytes_accessed=int(micros * 1e6)
    )


def attend_forward(scalars, segment_ids, tokens, projection):
    width = D // 4
    heads = width // HEAD_DIM
    block = 256

    def kernel(scalar_ref, segment_ref, tokens_ref, projection_ref, qkv_ref, attended_ref, probs_ref, mask):
        place, length = scalar_ref[0], scalar_ref[1]
        query_owner = segment_ref[pl.ds(place, 1), :].astype(wide)
        key_owner = jnp.broadcast_to(query_owner, (128, L)).T
        key_at = lax.broadcasted_iota(jnp.int32, (L, 128), 0)
        key_owner = jnp.where(key_at < length, key_owner, -1.0)
        query_at = lax.broadcasted_iota(jnp.int32, (L, 128), 1)
        for start in range(0, L, 128):
            allowed = (key_owner == query_owner[:, start : start + 128]) | (
                key_at == query_at + start
            )
            mask[:, start : start + 128] = jnp.where(allowed, 0.0, -1e30)
        bias = projection_ref[3 * width : 3 * width + 1, : 3 * width].astype(wide)
        qkv_ref[...] = (
            product(tokens_ref[...], projection_ref[: 3 * width, :], NT) + bias
        ).astype(low_type)

        @pl.loop(0, L // block)
        def _(step):
            rows = pl.ds(pl.multiple_of(step * block, block), block)
            for head in range(heads):
                at = head * HEAD_DIM
                queries = qkv_ref[rows, at : at + HEAD_DIM] * jnp.asarray(
                    HEAD_DIM**-0.5, low_type
                )
                key_rows = qkv_ref[:, width + at : width + at + HEAD_DIM]
                values = qkv_ref[:, 2 * width + at : 2 * width + at + HEAD_DIM]
                scores = product(key_rows, queries, NT) + mask[:, rows]
                highest = jnp.max(scores, axis=0, keepdims=True)
                expanded = jnp.exp(scores - highest)
                total = jnp.sum(expanded, axis=0, keepdims=True)
                probs = (expanded * (1.0 / total)).astype(low_type)
                probs_ref[head, :, rows] = probs
                attended_ref[rows, at : at + HEAD_DIM] = product(probs, values, TN).astype(
                    low_type
                )

    return pl.pallas_call(
        kernel,
        out_shape=(
            shaped((L, 3 * width), low_type),
            shaped((L, width), low_type),
            shaped((heads, L, L), low_type),
        ),
        in_specs=[pl.BlockSpec(memory_space=pltpu.SMEM)]
        + [pl.BlockSpec(memory_space=pltpu.VMEM)] * 3,
        scratch_shapes=[pltpu.VMEM((L, L), wide)],
        cost_estimate=cost(5),
        name="attend_forward",
    )(scalars, segment_ids, tokens, projection)


def attend_backward(branch_low, mixer, qkv, attended, probs):
    width = D // 4
    heads = width // HEAD_DIM
    block = 256

    def kernel(branch_ref, mixer_ref, qkv_ref, attended_ref, probs_ref, grad_ref, bias_ref, outgoing, sums):
        attended_grad = product(branch_ref[...], mixer_ref[...], NT).astype(low_type)
        outgoing[...] = attended_grad
        along = (attended_ref[...].astype(wide) * attended_grad.astype(wide)).T
        row_dots = [
            jnp.sum(along[head * HEAD_DIM : (head + 1) * HEAD_DIM], axis=0, keepdims=True)
            for head in range(heads)
        ]
        for head in range(heads):
            sums[head] = jnp.zeros((L, HEAD_DIM), wide)
        dots = jnp.concatenate(row_dots + [jnp.zeros((8 - heads, L), wide)], axis=0)
        bias_ref[...] = jnp.zeros((8, D), wide)
        bias_ref[:, :L] = dots

        @pl.loop(0, L // block)
        def _(step):
            rows = pl.ds(pl.multiple_of(step * block, block), block)
            for head in range(heads):
                at = head * HEAD_DIM
                queries = qkv_ref[:, at : at + HEAD_DIM] * jnp.asarray(HEAD_DIM**-0.5, low_type)
                key_rows = qkv_ref[rows, width + at : width + at + HEAD_DIM]
                values = qkv_ref[rows, 2 * width + at : 2 * width + at + HEAD_DIM]
                grad = outgoing[:, at : at + HEAD_DIM]
                probs = probs_ref[head, rows, :]
                probs_grad = product(values, grad, NT)
                scores_grad = (
                    probs.astype(wide) * (probs_grad - bias_ref[head : head + 1, :L])
                ).astype(low_type)
                grad_ref[rows, width + at : width + at + HEAD_DIM] = product(
                    scores_grad, queries, NN
                ).astype(low_type)
                grad_ref[rows, 2 * width + at : 2 * width + at + HEAD_DIM] = product(
                    probs, grad, NN
                ).astype(low_type)
                sums[head] += product(scores_grad, key_rows, TN)

        for head in range(heads):
            at = head * HEAD_DIM
            grad_ref[:, at : at + HEAD_DIM] = (sums[head] * (HEAD_DIM**-0.5)).astype(low_type)
        bias_ref[...] = jnp.zeros((8, D), wide)
        bias_ref[0:1, : 3 * width] = jnp.sum(grad_ref[...].astype(wide), axis=0, keepdims=True)

    return pl.pallas_call(
        kernel,
        out_shape=(shaped((L, 3 * width), low_type), shaped((8, D), wide)),
        scratch_shapes=[
            pltpu.VMEM((L, width), low_type),
            pltpu.VMEM((heads, L, HEAD_DIM), wide),
        ],
        cost_estimate=cost(6),
        name="attend_backward",
    )(branch_low, mixer, qkv, attended, probs)


def normalize(rows):
    center = rows - jnp.mean(rows, axis=-1, keepdims=True)
    inverse = lax.rsqrt(jnp.mean(center * center, axis=-1, keepdims=True) + eps_norm)
    return center * inverse, inverse


def normalize_backward(scaled, normed, inverse):
    middle = jnp.mean(scaled, axis=-1, keepdims=True)
    along = jnp.mean(scaled * normed, axis=-1, keepdims=True)
    return inverse * (scaled - middle - normed * along)


def column_sum(rows):
    return jnp.sum(rows, axis=0, keepdims=True)


def mix_norm(scalars, vectors, tokens, attended, mixers):
    block = 256
    width = D // 4

    def kernel(scalar_ref, vector_ref, tokens_ref, *refs):
        attended_refs, mixer_refs = refs[:4], refs[4:8]
        hat_ref, inverse_ref, low_ref, sums_ref = refs[8:]
        step = pl.program_id(0)
        total = product(attended_refs[0][...], mixer_refs[0][...], NN)
        for left, right in zip(attended_refs[1:], mixer_refs[1:]):
            total += product(left[...], right[...], NN)
        branch = total + vector_ref[0:1, :].astype(wide)
        rows = tokens_ref[...].astype(wide)
        hat, inverse = normalize(rows + branch)
        hat_ref[...] = hat
        inverse_ref[...] = inverse
        low_ref[...] = (
            hat * vector_ref[1:2, :].astype(wide) + vector_ref[2:3, :].astype(wide)
        ).astype(low_type)
        at = lax.broadcasted_iota(jnp.int32, (block, 1), 0) + step * block
        valid = (at < scalar_ref[1]).astype(wide)

        @pl.when(step == 0)
        def _():
            sums_ref[...] = jnp.zeros((8, D), wide)

        sums_ref[0:1, :] += column_sum(valid * rows * rows)
        sums_ref[1:2, :] += column_sum(valid * branch * branch)
        sums_ref[2:3, :] += column_sum(jnp.broadcast_to(valid, (block, D)))

    return pl.pallas_call(
        kernel,
        grid=(L // block,),
        out_shape=(
            shaped((L, D), wide),
            shaped((L, 1), wide),
            shaped((L, D), low_type),
            shaped((8, D), wide),
        ),
        in_specs=[
            pl.BlockSpec(memory_space=pltpu.SMEM),
            whole((8, D)),
            pl.BlockSpec((block, D), lambda i: (i, 0)),
        ]
        + [pl.BlockSpec((block, width), lambda i: (i, 0))] * 4
        + [whole((width, D))] * 4,
        out_specs=[
            pl.BlockSpec((block, D), lambda i: (i, 0)),
            pl.BlockSpec((block, 1), lambda i: (i, 0)),
            pl.BlockSpec((block, D), lambda i: (i, 0)),
            pl.BlockSpec((8, D), lambda i: (0, 0)),
        ],
        cost_estimate=cost(3),
        name="mix_norm",
    )(scalars, vectors, tokens, *attended, *mixers)


def pick(slot, refs, scratch):
    for index, ref in enumerate(refs):

        @pl.when(slot == index)
        def _(ref=ref):
            scratch[...] = ref[...]


KEEP = pl.BlockSpec((1, L, D), lambda g: (jnp.minimum(g, 1), 0, 0))
SEND = pl.BlockSpec((1, L, D), lambda g: (jnp.maximum(g - 2, 0), 0, 0))


def inner_forward(normed_low, weights, projections):
    chunk = 256
    width = D // 4

    def kernel(normed_ref, *refs):
        weight_refs, bias_refs = refs[:4], refs[4:8]
        keep_ref, send_ref, slope_ref, weight, bias = refs[8:]
        slot = pl.program_id(0)
        pick(slot, weight_refs, weight)
        pick(slot, bias_refs, bias)

        @pl.loop(0, D // chunk)
        def _(step):
            columns = pl.ds(pl.multiple_of(step * chunk, chunk), chunk)
            inner_pre = product(normed_ref[...], weight[:, columns], NN) + bias[
                0:16, columns
            ].astype(wide)[1:2, :]
            below = 0.5 * (1.0 + lax.erf(inner_pre * root_half))
            density = jnp.exp(-0.5 * inner_pre * inner_pre) * inv_root_tau
            activated = (inner_pre * below).astype(low_type)
            slope_ref[0, :, columns] = (below + inner_pre * density).astype(low_type)

            @pl.when(slot < 2)
            def _():
                keep_ref[0, :, columns] = activated

            @pl.when(slot >= 2)
            def _():
                send_ref[0, :, columns] = activated

    return pl.pallas_call(
        kernel,
        grid=(4,),
        out_shape=(
            shaped((2, L, D), low_type),
            shaped((2, L, D), low_type),
            shaped((4, L, D), low_type),
        ),
        in_specs=[whole((L, D))]
        + [whole((D, D))] * 4
        + [pl.BlockSpec((EXTRA, D), lambda g: (3 * width // EXTRA, 0))] * 4,
        out_specs=[KEEP, SEND, pl.BlockSpec((1, L, D), lambda g: (g, 0, 0))],
        scratch_shapes=[pltpu.VMEM((D, D), low_type), pltpu.VMEM((EXTRA, D), low_type)],
        cost_estimate=cost(13),
        name="inner_forward",
    )(normed_low, *weights, *projections)


def outer_norm(scalars, vectors, hat_one, grad_out, keep, send, weights):
    block = 256

    def kernel(scalar_ref, vector_ref, hat_ref, incoming_ref, keep_ref, send_ref, *refs):
        weight_refs = refs[:4]
        out_ref, grad_ref, low_ref, sums_ref = refs[4:]
        step = pl.program_id(0)
        total = product(keep_ref[0], weight_refs[0][...], NN)
        total += product(keep_ref[1], weight_refs[1][...], NN)
        total += product(send_ref[0], weight_refs[2][...], NN)
        total += product(send_ref[1], weight_refs[3][...], NN)
        vectors = vector_ref[...].astype(wide)
        branch = total + vectors[3:4]
        normed_one = hat_ref[...] * vectors[1:2] + vectors[2:3]
        hat, inverse = normalize(normed_one + branch)
        out_ref[...] = (hat * vectors[4:5] + vectors[5:6]).astype(low_type)
        incoming = incoming_ref[...].astype(wide)
        grad = normalize_backward(incoming * vectors[4:5], hat, inverse)
        grad_ref[...] = grad
        low_ref[...] = grad.astype(low_type)
        at = lax.broadcasted_iota(jnp.int32, (block, 1), 0) + step * block
        valid = (at < scalar_ref[1]).astype(wide)

        @pl.when(step == 0)
        def _():
            sums_ref[...] = jnp.zeros((8, D), wide)

        sums_ref[0:1, :] += column_sum(incoming * hat)
        sums_ref[1:2, :] += column_sum(incoming)
        sums_ref[2:3, :] += column_sum(grad)
        sums_ref[3:4, :] += column_sum(valid * branch * branch)

    rows = pl.BlockSpec((block, D), lambda i: (i, 0))
    pair = pl.BlockSpec((2, block, D), lambda i: (0, i, 0))
    return pl.pallas_call(
        kernel,
        grid=(L // block,),
        out_shape=(
            shaped((L, D), low_type),
            shaped((L, D), wide),
            shaped((L, D), low_type),
            shaped((8, D), wide),
        ),
        in_specs=[pl.BlockSpec(memory_space=pltpu.SMEM), whole((8, D)), rows, rows, pair, pair]
        + [whole((D, D))] * 4,
        out_specs=[rows, rows, rows, pl.BlockSpec((8, D), lambda i: (0, 0))],
        cost_estimate=cost(5),
        name="outer_norm",
    )(scalars, vectors, hat_one, grad_out, keep, send, *weights)


def inner_backward(ffn_low, slopes, weights):
    chunk = 256

    def kernel(ffn_ref, slope_ref, *refs):
        weight_refs = refs[:4]
        keep_ref, send_ref, bias_ref, weight = refs[4:]
        slot = pl.program_id(0)
        pick(slot, weight_refs, weight)

        @pl.when(slot == 0)
        def _():
            bias_ref[...] = jnp.zeros((8, D), wide)

        @pl.loop(0, D // chunk)
        def _(step):
            columns = pl.ds(pl.multiple_of(step * chunk, chunk), chunk)
            grad = product(ffn_ref[...], weight[columns, :], NT) * slope_ref[
                0, :, columns
            ].astype(wide)
            bias_ref[pl.ds(slot, 1), columns] = column_sum(grad)
            low = grad.astype(low_type)

            @pl.when(slot < 2)
            def _():
                keep_ref[0, :, columns] = low

            @pl.when(slot >= 2)
            def _():
                send_ref[0, :, columns] = low

    return pl.pallas_call(
        kernel,
        grid=(4,),
        out_shape=(
            shaped((2, L, D), low_type),
            shaped((2, L, D), low_type),
            shaped((8, D), wide),
        ),
        in_specs=[whole((L, D)), pl.BlockSpec((1, L, D), lambda g: (g, 0, 0))]
        + [whole((D, D))] * 4,
        out_specs=[KEEP, SEND, pl.BlockSpec((8, D), lambda g: (0, 0))],
        scratch_shapes=[pltpu.VMEM((D, D), low_type)],
        cost_estimate=cost(5),
        name="inner_backward",
    )(ffn_low, slopes, *weights)


def first_backward(vectors, hat_one, inverse_one, second_grad, keep, send, weights):
    block = 256

    def kernel(vector_ref, hat_ref, inverse_ref, second_ref, keep_ref, send_ref, *refs):
        weight_refs = refs[:4]
        grad_ref, low_ref, sums_ref = refs[4:]
        total = second_ref[...] + product(keep_ref[0], weight_refs[0][...], NT)
        total += product(keep_ref[1], weight_refs[1][...], NT)
        total += product(send_ref[0], weight_refs[2][...], NT)
        total += product(send_ref[1], weight_refs[3][...], NT)
        hat = hat_ref[...]
        gain = vector_ref[1:2, :].astype(wide)
        grad = normalize_backward(total * gain, hat, inverse_ref[...])
        grad_ref[...] = grad
        low_ref[...] = grad.astype(low_type)

        @pl.when(pl.program_id(0) == 0)
        def _():
            sums_ref[...] = jnp.zeros((8, D), wide)

        sums_ref[0:1, :] += column_sum(total * hat)
        sums_ref[1:2, :] += column_sum(total)
        sums_ref[2:3, :] += column_sum(grad)

    rows = pl.BlockSpec((block, D), lambda i: (i, 0))
    pair = pl.BlockSpec((2, block, D), lambda i: (0, i, 0))
    return pl.pallas_call(
        kernel,
        grid=(L // block,),
        out_shape=(shaped((L, D), wide), shaped((L, D), low_type), shaped((8, D), wide)),
        in_specs=[
            whole((8, D)),
            rows,
            pl.BlockSpec((block, 1), lambda i: (i, 0)),
            rows,
            pair,
            pair,
        ]
        + [whole((D, D))] * 4,
        out_specs=[rows, rows, pl.BlockSpec((8, D), lambda i: (0, 0))],
        cost_estimate=cost(5),
        name="first_backward",
    )(vectors, hat_one, inverse_one, second_grad, keep, send, *weights)


def input_backward(first_grad, qkv_grads, projections):
    block = 256
    width = D // 4

    def kernel(first_ref, *refs):
        grad_refs, weight_refs, out_ref = refs[:4], refs[4:8], refs[8]
        total = first_ref[...]
        for left, right in zip(grad_refs, weight_refs):
            total += product(left[...], right[: 3 * width, :], NN)
        out_ref[...] = total

    rows = pl.BlockSpec((block, D), lambda i: (i, 0))
    return pl.pallas_call(
        kernel,
        grid=(L // block,),
        out_shape=shaped((L, D), wide),
        in_specs=[rows]
        + [pl.BlockSpec((block, 3 * width), lambda i: (i, 0))] * 4
        + [whole((3 * width + EXTRA, D))] * 4,
        out_specs=rows,
        cost_estimate=cost(4),
        name="input_backward",
    )(first_grad, *qkv_grads, *projections)


def solution(mesh):
    dp_size = mesh.shape["dp"]
    tensor_size = mesh.shape["tensor"]
    masks = [1, 2, 6] + [1 << bit for bit in range(3, 16)]
    masks = masks[: dp_size.bit_length() - 1]

    def over_tensor(value, mask):
        return lax.ppermute(value, "tensor", [(i, i ^ mask) for i in range(tensor_size)])

    def over_dp(value, mask):
        return lax.ppermute(value, "dp", [(i, i ^ mask) for i in range(dp_size)])

    def body(
        tokens,
        grad_out,
        lengths,
        segment_ids,
        query_weight,
        query_bias,
        key_weight,
        value_weight,
        value_bias,
        mixer_weight,
        mixer_bias,
        first_gain,
        first_shift,
        inner_weight,
        inner_bias,
        outer_weight,
        outer_bias,
        second_gain,
        second_shift,
    ):
        width = query_weight.shape[1]
        place = lax.axis_index("tensor")
        odd = lax.axis_index("dp") % 2
        chain = [jnp.zeros((8, 128), wide)]

        def after(*values):
            held = lax.optimization_barrier((chain[0],) + values)
            return held[1:] if len(values) > 1 else held[1]

        def done(*values):
            chain[0] = lax.optimization_barrier((chain[0],) + values)[0]
            return values if len(values) > 1 else values[0]

        def half(value, which):
            rows = value.shape[0] // 2
            return lax.dynamic_slice_in_dim(value, which * rows, rows, 0)

        def join(mine, other):
            rows = mine.shape[0]
            out = jnp.zeros((2 * rows,) + mine.shape[1:], mine.dtype)
            out = lax.dynamic_update_slice_in_dim(out, mine, odd * rows, 0)
            return lax.dynamic_update_slice_in_dim(out, other, (1 - odd) * rows, 0)

        bias_row = jnp.concatenate([query_bias, jnp.zeros_like(query_bias), value_bias])
        own_projection = jnp.concatenate(
            [
                query_weight.T,
                key_weight.T,
                value_weight.T,
                jnp.pad(bias_row[None, :], ((0, 0), (0, D - 3 * width))),
                inner_bias[None, :],
                jnp.zeros((EXTRA - 2, D), low_type),
            ],
            axis=0,
        )
        own = [own_projection, mixer_weight, inner_weight, outer_weight]
        partner = [over_tensor(own[0], 1)]
        fetched = [over_tensor(half(own[0], odd), 2)]
        vectors = jnp.stack(
            [mixer_bias, first_gain, first_shift, outer_bias, second_gain, second_shift]
            + [jnp.zeros_like(mixer_bias)] * 2
        )
        scalars = jnp.stack(
            [place, lax.dynamic_index_in_dim(lengths, place, 0, keepdims=False)]
        ).astype(jnp.int32)
        for group in (1, 2, 3):
            fetched.append(over_tensor(half(own[group], odd), 2))
            partner.append(over_tensor(own[group], 1))

        def attend(slot, weights):
            weights = after(weights)
            return done(*attend_forward(scalars, segment_ids, tokens, weights))

        heads = {0: attend(0, own[0]), 1: attend(1, partner[0])}
        across, beyond = [], []
        for group in range(4):
            mask = 1
            across.append(join(fetched[group], over_dp(fetched[group], mask)))
            beyond.append(over_tensor(across[group], 1))
        slots = [[own[g], partner[g], across[g], beyond[g]] for g in range(4)]
        projections, mixers, inners, outers = slots
        heads[2] = attend(2, projections[2])
        heads[3] = attend(3, projections[3])
        attended = [heads[j][1] for j in range(4)]
        held = after(*mixers)
        hat_one, inverse_one, normed_low, sums_one = done(
            *mix_norm(scalars, vectors, tokens, attended, held)
        )
        order = (0, 2, 1, 3)
        held = after(*[inners[j] for j in order])
        keep, send, slopes = done(
            *inner_forward(normed_low, held, [projections[j] for j in order])
        )
        held = after(*[outers[j] for j in order])
        layer_out, second_grad, ffn_low, sums_two = done(
            *outer_norm(scalars, vectors, hat_one, grad_out, keep, send, held)
        )

        tokens_other = over_tensor(tokens, 1)
        attended_other = {0: over_tensor(attended[1], 1), 2: over_tensor(attended[3], 1)}
        normed_other = over_tensor(normed_low, 1)
        keep_other = over_tensor(send, 1)
        ffn_other = over_tensor(ffn_low, 1)

        def pair_product(left, right, left_other, right_other):
            left, right, left_other, right_other = after(left, right, left_other, right_other)
            return done(
                (product(left, right, TN) + product(left_other, right_other, TN)).astype(low_type)
            )

        def add_low(left, right):
            return (left.astype(wide) + right.astype(wide)).astype(low_type)

        class Reduction:
            def __init__(self, sent):
                self.incoming = over_tensor(sent, 2)
                self.kept = None
                self.stage = 0

            def hop(self):
                last = len(masks)
                if self.stage == 0:
                    kept, incoming = after(self.kept, self.incoming)
                    send = add_low(half(kept, 1 - odd), half(incoming, 1 - odd))
                    self.incoming = over_dp(done(send), masks[0])
                    self.kept = add_low(half(kept, odd), half(incoming, odd))
                elif self.stage <= last:
                    kept, incoming = after(self.kept, self.incoming)
                    self.kept = done(add_low(kept, incoming))
                    mask = masks[self.stage] if self.stage < last else masks[0]
                    self.incoming = over_dp(self.kept, mask)
                else:
                    kept, incoming = after(self.kept, self.incoming)
                    low = jnp.concatenate([kept, incoming], axis=0)
                    high = jnp.concatenate([incoming, kept], axis=0)
                    self.result = jnp.where(odd == 0, low, high).astype(wide)
                self.stage += 1

        cut = D // 2
        hops = len(masks) + 2

        def parts(left, right, left_other, right_other, rows):
            return [
                pair_product(left[:, a : a + rows], right, left_other[:, a : a + rows], right_other)
                for a in range(0, left.shape[1], rows)
            ]

        outer_chain = [Reduction(p) for p in parts(keep[1], ffn_low, keep_other[1], ffn_other, cut)]
        held = after(*[outers[j] for j in order])
        inner_keep, inner_send, inner_bias_rows = done(*inner_backward(ffn_low, slopes, held))
        inner_other = over_tensor(inner_send, 1)
        for reduction, kept in zip(outer_chain, parts(keep[0], ffn_low, keep_other[0], ffn_other, cut)):
            reduction.kept = kept
        held = after(*[inners[j] for j in order])
        first_grad, branch_low, sums_three = done(
            *first_backward(vectors, hat_one, inverse_one, second_grad, inner_keep, inner_send, held)
        )
        branch_other = over_tensor(branch_low, 1)
        inner_chain = [
            Reduction(p)
            for p in parts(normed_low, inner_keep[1], normed_other, inner_other[1], cut)
        ]
        outer_chain[0].hop()
        qkv_grads, qkv_bias = {}, {}

        def retreat(slot):
            low = after(branch_low)
            qkv_grads[slot], qkv_bias[slot] = done(
                *attend_backward(low, mixers[slot], *heads[slot])
            )

        retreat(3)
        qkv_other = {2: over_tensor(qkv_grads[3], 1)}
        outer_chain[1].hop()
        retreat(2)
        for reduction, kept in zip(
            inner_chain, parts(normed_low, inner_keep[0], normed_other, inner_other[0], cut)
        ):
            reduction.kept = kept
        outer_chain[0].hop()
        qkv_chain = [
            Reduction(p) for p in parts(qkv_grads[2], tokens, qkv_other[2], tokens_other, width)
        ]
        inner_chain[0].hop()
        outer_chain[1].hop()
        retreat(1)
        qkv_other[0] = over_tensor(qkv_grads[1], 1)
        outer_chain[0].hop()
        mixer_chain = Reduction(
            pair_product(attended[2], branch_low, attended_other[2], branch_other)
        )
        retreat(0)
        inner_chain[0].hop()
        inner_chain[1].hop()
        outer_chain[1].hop()
        outer_chain[0].hop()
        for reduction, kept in zip(
            qkv_chain, parts(qkv_grads[0], tokens, qkv_other[0], tokens_other, width)
        ):
            reduction.kept = kept
        mixer_chain.kept = pair_product(attended[0], branch_low, attended_other[0], branch_other)

        small = jnp.concatenate(
            [
                sums_one,
                sums_two,
                sums_three,
                inner_bias_rows[:4],
                qkv_bias[0][:1],
                qkv_bias[2][:1],
                qkv_bias[1][:1],
                qkv_bias[3][:1],
            ]
        )

        def swap(rows, which):
            return jnp.concatenate([rows[:24]] + [rows[i : i + 1] for i in which])

        small = small + swap(over_tensor(small, 1), (26, 27, 24, 25, 30, 31, 28, 29))
        held = after(first_grad, *[qkv_grads[j] for j in range(4)])
        tokens_grad = done(input_backward(held[0], held[1:], projections))
        small = small + swap(over_tensor(small, 2), (25, 24, 27, 26, 29, 28, 31, 30))
        pending = outer_chain + inner_chain + qkv_chain + [mixer_chain]
        dp_left = list(masks)
        while any(r.stage < hops for r in pending):
            for r in pending:
                if r.stage < hops:
                    r.hop()
            if dp_left:
                small = small + over_dp(small, dp_left.pop(0))
        while dp_left:
            small = small + over_dp(small, dp_left.pop(0))

        totals = jnp.sum(jnp.stack([small[0], small[1], small[11]]), axis=1)
        statistics = jnp.sqrt(totals / (small[2, 0] * D))
        stacked = lambda reductions: jnp.concatenate([r.result for r in reductions], axis=0)
        return (
            layer_out,
            tokens_grad,
            qkv_chain[0].result.T,
            small[28, :width],
            qkv_chain[1].result.T,
            qkv_chain[2].result.T,
            small[28, 2 * width : 3 * width],
            mixer_chain.result,
            small[18],
            small[16],
            small[17],
            stacked(inner_chain),
            small[24],
            stacked(outer_chain),
            small[10],
            small[8],
            small[9],
            statistics,
        )

    in_specs = (
        P(("dp", "tensor"), None),
        P(("dp", "tensor"), None),
        P("dp"),
        P("dp", None),
        P(None, "tensor"),
        P("tensor"),
        P(None, "tensor"),
        P(None, "tensor"),
        P("tensor"),
        P("tensor", None),
        P(),
        P(),
        P(),
        P(None, "tensor"),
        P("tensor"),
        P("tensor", None),
        P(),
        P(),
        P(),
    )
    out_specs = (
        P(("dp", "tensor"), None),
        P(("dp", "tensor"), None),
        P(None, "tensor"),
        P("tensor"),
        P(None, "tensor"),
        P(None, "tensor"),
        P("tensor"),
        P("tensor", None),
        P(),
        P(),
        P(),
        P(None, "tensor"),
        P("tensor"),
        P("tensor", None),
        P(),
        P(),
        P(),
        P(),
    )
    return jax.shard_map(body, mesh=mesh, in_specs=in_specs, out_specs=out_specs, check_vma=False)
```

```python
import jax
import jax.numpy as jnp
from jax import lax
from jax.experimental import pallas as pl
from jax.experimental.pallas import tpu as pltpu
from jax.sharding import PartitionSpec as P

D = 768
HEAD_DIM = 64
L = 512
EXTRA = 32

eps_norm = 1e-06
root_half = 0.7071067811865476
inv_root_tau = 0.3989422804014327
low_type = jnp.bfloat16
wide = jnp.float32
NN = (((1,), (0,)), ((), ()))
NT = (((1,), (1,)), ((), ()))
TN = (((0,), (0,)), ((), ()))


def product(left, right, dims):
    return lax.dot_general(left, right, dims, preferred_element_type=wide)


def shaped(shape, dtype):
    return jax.ShapeDtypeStruct(shape, dtype)


def cost(micros):
    return pl.CostEstimate(
        flops=int(micros * 1e6 * 300), transcendentals=0, bytes_accessed=int(micros * 1e6)
    )


def call(kernel, name, micros, out_shape, operands, scratch=(), limit=20):
    return pl.pallas_call(
        kernel,
        out_shape=out_shape,
        in_specs=[pl.BlockSpec(memory_space=pltpu.SMEM)]
        + [pl.BlockSpec(memory_space=pltpu.VMEM)] * (len(operands) - 1),
        out_specs=jax.tree.map(lambda _: pl.BlockSpec(memory_space=pltpu.VMEM), out_shape),
        scratch_shapes=list(scratch),
        compiler_params=pltpu.CompilerParams(vmem_limit_bytes=limit << 20),
        cost_estimate=cost(micros),
        name=name,
    )(*operands)


def assemble(parts, odd, scratch):
    if len(parts) == 1:
        scratch[...] = parts[0][...]
    else:
        rows = parts[0].shape[0]
        scratch[pl.ds(pl.multiple_of(odd * rows, rows), rows), :] = parts[0][...]
        scratch[pl.ds(pl.multiple_of((1 - odd) * rows, rows), rows), :] = parts[1][...]


def unflatten(refs, slots):
    out, at = [], 0
    for parts in slots:
        out.append(refs[at : at + len(parts)])
        at += len(parts)
    return out, refs[at:]


def flat(slots):
    return [part for parts in slots for part in parts]


def attend_forward(scalars, segment_ids, tokens, projection):
    width = D // 4
    heads = width // HEAD_DIM
    block = 256

    def kernel(scalar_ref, segment_ref, tokens_ref, *refs):
        (parts,), refs = unflatten(refs, [projection])
        qkv_ref, attended_ref, probs_ref, mask = refs[:4]
        place, length, odd = scalar_ref[0], scalar_ref[1], scalar_ref[2]
        if len(parts) == 1:
            weight = parts[0]
        else:
            weight = refs[4]
            assemble(parts, odd, weight)
        query_owner = segment_ref[pl.ds(place, 1), :].astype(wide)
        key_owner = jnp.broadcast_to(query_owner, (128, L)).T
        key_at = lax.broadcasted_iota(jnp.int32, (L, 128), 0)
        key_owner = jnp.where(key_at < length, key_owner, -1.0)
        query_at = lax.broadcasted_iota(jnp.int32, (L, 128), 1)
        for start in range(0, L, 128):
            allowed = (key_owner == query_owner[:, start : start + 128]) | (
                key_at == query_at + start
            )
            mask[:, start : start + 128] = jnp.where(allowed, 0.0, -1e30)
        bias = weight[3 * width : 3 * width + 1, : 3 * width].astype(wide)
        qkv_ref[...] = (product(tokens_ref[...], weight[: 3 * width, :], NT) + bias).astype(
            low_type
        )

        @pl.loop(0, L // block)
        def _(step):
            rows = pl.ds(pl.multiple_of(step * block, block), block)
            for head in range(heads):
                at = head * HEAD_DIM
                queries = qkv_ref[rows, at : at + HEAD_DIM] * jnp.asarray(
                    HEAD_DIM**-0.5, low_type
                )
                key_rows = qkv_ref[:, width + at : width + at + HEAD_DIM]
                values = qkv_ref[:, 2 * width + at : 2 * width + at + HEAD_DIM]
                scores = product(key_rows, queries, NT) + mask[:, rows]
                highest = jnp.max(scores, axis=0, keepdims=True)
                expanded = jnp.exp(scores - highest)
                total = jnp.sum(expanded, axis=0, keepdims=True)
                probs = (expanded * (1.0 / total)).astype(low_type)
                probs_ref[head, :, rows] = probs
                attended_ref[rows, at : at + HEAD_DIM] = product(probs, values, TN).astype(
                    low_type
                )

    scratch = [pltpu.VMEM((L, L), wide)]
    if len(projection) > 1:
        scratch.append(pltpu.VMEM((3 * width + EXTRA, D), low_type))
    return call(
        kernel,
        "attend_forward",
        5,
        (
            shaped((L, 3 * width), low_type),
            shaped((L, width), low_type),
            shaped((heads, L, L), low_type),
        ),
        [scalars, segment_ids, tokens, *projection],
        scratch,
    )


def attend_backward(scalars, slot, branch_low, mixer, qkv, attended, probs):
    width = D // 4
    heads = width // HEAD_DIM
    block = 256

    def kernel(scalar_ref, branch_ref, qkv_ref, attended_ref, probs_ref, *refs):
        (parts,), refs = unflatten(refs, [mixer])
        grad_ref, bias_ref, weight, outgoing, sums, dots = refs
        assemble(parts, scalar_ref[2], weight)
        attended_grad = product(branch_ref[...], weight[...], NT).astype(low_type)
        outgoing[...] = attended_grad
        along = (attended_ref[...].astype(wide) * attended_grad.astype(wide)).T
        for head in range(heads):
            dots[head : head + 1, :] = jnp.sum(
                along[head * HEAD_DIM : (head + 1) * HEAD_DIM], axis=0, keepdims=True
            )
            sums[head] = jnp.zeros((L, HEAD_DIM), wide)

        @pl.loop(0, L // block)
        def _(step):
            rows = pl.ds(pl.multiple_of(step * block, block), block)
            for head in range(heads):
                at = head * HEAD_DIM
                queries = qkv_ref[:, at : at + HEAD_DIM] * jnp.asarray(HEAD_DIM**-0.5, low_type)
                key_rows = qkv_ref[rows, width + at : width + at + HEAD_DIM]
                values = qkv_ref[rows, 2 * width + at : 2 * width + at + HEAD_DIM]
                grad = outgoing[:, at : at + HEAD_DIM]
                probs = probs_ref[head, rows, :]
                probs_grad = product(values, grad, NT)
                scores_grad = (
                    probs.astype(wide) * (probs_grad - dots[head : head + 1, :])
                ).astype(low_type)
                grad_ref[rows, width + at : width + at + HEAD_DIM] = product(
                    scores_grad, queries, NN
                ).astype(low_type)
                grad_ref[rows, 2 * width + at : 2 * width + at + HEAD_DIM] = product(
                    probs, grad, NN
                ).astype(low_type)
                sums[head] += product(scores_grad, key_rows, TN)

        for head in range(heads):
            at = head * HEAD_DIM
            grad_ref[:, at : at + HEAD_DIM] = (sums[head] * (HEAD_DIM**-0.5)).astype(low_type)
        bias_ref[...] = jnp.zeros((8, D), wide)
        quarter = scalar_ref[0] ^ slot
        bias_ref[pl.ds(quarter, 1), : 3 * width] = jnp.sum(
            grad_ref[...].astype(wide), axis=0, keepdims=True
        )

    return call(
        kernel,
        "attend_backward",
        5,
        (shaped((L, 3 * width), low_type), shaped((8, D), wide)),
        [scalars, branch_low, qkv, attended, probs, *mixer],
        [
            pltpu.VMEM((width, D), low_type),
            pltpu.VMEM((L, width), low_type),
            pltpu.VMEM((heads, L, HEAD_DIM), wide),
            pltpu.VMEM((8, L), wide),
        ],
    )


def normalize(rows):
    center = rows - jnp.mean(rows, axis=-1, keepdims=True)
    inverse = lax.rsqrt(jnp.mean(center * center, axis=-1, keepdims=True) + eps_norm)
    return center * inverse, inverse


def normalize_backward(scaled, normed, inverse):
    middle = jnp.mean(scaled, axis=-1, keepdims=True)
    along = jnp.mean(scaled * normed, axis=-1, keepdims=True)
    return inverse * (scaled - middle - normed * along)


def column_sum(rows):
    return jnp.sum(rows, axis=0, keepdims=True)


def in_place(parts, odd, scratch):
    if len(parts) == 1:
        return parts[0]
    assemble(parts, odd, scratch)
    return scratch


BLOCK = 256


def mix_norm(scalars, vectors, tokens, attended, mixers):
    width = D // 4

    def kernel(scalar_ref, vector_ref, tokens_ref, *refs):
        attended_refs = refs[:4]
        parts, refs = unflatten(refs[4:], mixers)
        hat_ref, inverse_ref, low_ref, sums_ref, scratch = refs
        length, odd = scalar_ref[1], scalar_ref[2]
        for index in range(4):
            assemble(parts[index], odd, scratch.at[pl.ds(index * width, width)])
        vectors = vector_ref[...].astype(wide)
        sums_ref[...] = jnp.zeros((8, D), wide)

        @pl.loop(0, L // BLOCK)
        def _(step):
            at = pl.ds(pl.multiple_of(step * BLOCK, BLOCK), BLOCK)
            branch = vectors[0:1]
            for index in range(4):
                branch = branch + product(
                    attended_refs[index][at, :], scratch[index * width : (index + 1) * width], NN
                )
            rows = tokens_ref[at, :].astype(wide)
            hat, inverse = normalize(rows + branch)
            hat_ref[at, :] = hat
            inverse_ref[at, :] = inverse
            low_ref[at, :] = (hat * vectors[1:2] + vectors[2:3]).astype(low_type)
            place = lax.broadcasted_iota(jnp.int32, (BLOCK, 1), 0) + step * BLOCK
            valid = (place < length).astype(wide)
            sums_ref[0:1, :] += column_sum(valid * rows * rows)
            sums_ref[1:2, :] += column_sum(valid * branch * branch)
            sums_ref[2:3, :] += column_sum(jnp.broadcast_to(valid, (BLOCK, D)))

    return call(
        kernel,
        "mix_norm",
        3,
        (shaped((L, D), wide), shaped((L, 1), wide), shaped((L, D), low_type), shaped((8, D), wide)),
        [scalars, vectors, tokens, *attended, *flat(mixers)],
        [pltpu.VMEM((D, D), low_type)],
    )


def inner_forward(scalars, normed_low, weights, biases):
    chunk = 256
    row = 3 * D // 4

    def kernel(scalar_ref, normed_ref, *refs):
        weight_refs, refs = unflatten(refs, weights)
        bias_refs, refs = unflatten(refs, biases)
        out_refs, slope_ref, weight, bias = refs[:4], refs[4], refs[5], refs[6]
        odd = scalar_ref[2]

        @pl.loop(0, 4)
        def _(slot):
            for index in range(4):

                @pl.when(slot == index)
                def _(index=index):
                    assemble(weight_refs[index], odd, weight)
                    parts = bias_refs[index]
                    if len(parts) == 1:
                        bias[...] = parts[0][row : row + 16, :]
                    else:
                        at = row - parts[0].shape[0]

                        @pl.when(odd == 1)
                        def _():
                            bias[...] = parts[0][at : at + 16, :]

                        @pl.when(odd == 0)
                        def _():
                            bias[...] = parts[1][at : at + 16, :]

            @pl.loop(0, D // chunk)
            def _(step):
                columns = pl.ds(pl.multiple_of(step * chunk, chunk), chunk)
                inner_pre = product(normed_ref[...], weight[:, columns], NN) + bias[
                    :, columns
                ].astype(wide)[1:2, :]
                below = 0.5 * (1.0 + lax.erf(inner_pre * root_half))
                density = jnp.exp(-0.5 * inner_pre * inner_pre) * inv_root_tau
                activated = (inner_pre * below).astype(low_type)
                slope_ref[slot, :, columns] = (below + inner_pre * density).astype(low_type)
                for index in range(4):

                    @pl.when(slot == index)
                    def _(index=index):
                        out_refs[index][:, columns] = activated

    return call(
        kernel,
        "inner_forward",
        10,
        (shaped((L, D), low_type),) * 4 + (shaped((4, L, D), low_type),),
        [scalars, normed_low, *flat(weights), *flat(biases)],
        [pltpu.VMEM((D, D), low_type), pltpu.VMEM((16, D), low_type)],
    )


def outer_norm(scalars, vectors, hat_one, grad_out, activated, weights):
    def kernel(scalar_ref, vector_ref, hat_ref, incoming_ref, *refs):
        left_refs = refs[:4]
        parts, refs = unflatten(refs[4:], weights)
        out_ref, grad_ref, low_ref, sums_ref, scratch = refs
        length, odd = scalar_ref[1], scalar_ref[2]
        weight_refs = [in_place(parts[i], odd, scratch.at[i % 2]) for i in range(4)]
        vectors = vector_ref[...].astype(wide)
        sums_ref[...] = jnp.zeros((8, D), wide)

        @pl.loop(0, L // BLOCK)
        def _(step):
            at = pl.ds(pl.multiple_of(step * BLOCK, BLOCK), BLOCK)
            branch = vectors[3:4]
            for left, right in zip(left_refs, weight_refs):
                branch = branch + product(left[at, :], right[...], NN)
            normed_one = hat_ref[at, :] * vectors[1:2] + vectors[2:3]
            hat, inverse = normalize(normed_one + branch)
            out_ref[at, :] = (hat * vectors[4:5] + vectors[5:6]).astype(low_type)
            incoming = incoming_ref[at, :].astype(wide)
            grad = normalize_backward(incoming * vectors[4:5], hat, inverse)
            grad_ref[at, :] = grad
            low_ref[at, :] = grad.astype(low_type)
            place = lax.broadcasted_iota(jnp.int32, (BLOCK, 1), 0) + step * BLOCK
            valid = (place < length).astype(wide)
            sums_ref[0:1, :] += column_sum(incoming * hat)
            sums_ref[1:2, :] += column_sum(incoming)
            sums_ref[2:3, :] += column_sum(grad)
            sums_ref[3:4, :] += column_sum(valid * branch * branch)

    return call(
        kernel,
        "outer_norm",
        4,
        (
            shaped((L, D), low_type),
            shaped((L, D), wide),
            shaped((L, D), low_type),
            shaped((8, D), wide),
        ),
        [scalars, vectors, hat_one, grad_out, *activated, *flat(weights)],
        [pltpu.VMEM((2, D, D), low_type)],
    )


def inner_backward(scalars, ffn_low, slopes, weights):
    chunk = 256

    def kernel(scalar_ref, ffn_ref, slope_ref, *refs):
        weight_refs, refs = unflatten(refs, weights)
        out_refs, bias_ref, weight = refs[:4], refs[4], refs[5]
        place, odd = scalar_ref[0], scalar_ref[2]
        bias_ref[...] = jnp.zeros((8, D), wide)

        @pl.loop(0, 4)
        def _(slot):
            for index in range(4):

                @pl.when(slot == index)
                def _(index=index):
                    assemble(weight_refs[index], odd, weight)

            @pl.loop(0, D // chunk)
            def _(step):
                columns = pl.ds(pl.multiple_of(step * chunk, chunk), chunk)
                grad = product(ffn_ref[...], weight[columns, :], NT) * slope_ref[
                    slot, :, columns
                ].astype(wide)
                bias_ref[pl.ds(place ^ slot, 1), columns] = column_sum(grad)
                low = grad.astype(low_type)
                for index in range(4):

                    @pl.when(slot == index)
                    def _(index=index):
                        out_refs[index][:, columns] = low

    return call(
        kernel,
        "inner_backward",
        4,
        (shaped((L, D), low_type),) * 4 + (shaped((8, D), wide),),
        [scalars, ffn_low, slopes, *flat(weights)],
        [pltpu.VMEM((D, D), low_type)],
    )


def first_backward(scalars, vectors, hat_one, inverse_one, second_grad, inner_lows, weights):
    def kernel(scalar_ref, vector_ref, hat_ref, inverse_ref, second_ref, *refs):
        left_refs = refs[:4]
        parts, refs = unflatten(refs[4:], weights)
        grad_ref, low_ref, sums_ref, scratch = refs
        odd = scalar_ref[2]
        weight_refs = [in_place(parts[i], odd, scratch.at[i % 2]) for i in range(4)]
        gain = vector_ref[1:2, :].astype(wide)
        sums_ref[...] = jnp.zeros((8, D), wide)

        @pl.loop(0, L // BLOCK)
        def _(step):
            at = pl.ds(pl.multiple_of(step * BLOCK, BLOCK), BLOCK)
            total = second_ref[at, :]
            for left, right in zip(left_refs, weight_refs):
                total = total + product(left[at, :], right[...], NT)
            hat = hat_ref[at, :]
            grad = normalize_backward(total * gain, hat, inverse_ref[at, :])
            grad_ref[at, :] = grad
            low_ref[at, :] = grad.astype(low_type)
            sums_ref[0:1, :] += column_sum(total * hat)
            sums_ref[1:2, :] += column_sum(total)
            sums_ref[2:3, :] += column_sum(grad)

    return call(
        kernel,
        "first_backward",
        4,
        (shaped((L, D), wide), shaped((L, D), low_type), shaped((8, D), wide)),
        [scalars, vectors, hat_one, inverse_one, second_grad, *inner_lows, *flat(weights)],
        [pltpu.VMEM((2, D, D), low_type)],
    )


def input_backward(scalars, first_grad, qkv_grads, projections):
    width = D // 4

    def kernel(scalar_ref, first_ref, *refs):
        left_refs = refs[:4]
        parts, refs = unflatten(refs[4:], projections)
        out_ref, scratch = refs
        odd = scalar_ref[2]
        weight_refs = [in_place(parts[i], odd, scratch.at[i % 2]) for i in range(4)]

        @pl.loop(0, L // BLOCK)
        def _(step):
            at = pl.ds(pl.multiple_of(step * BLOCK, BLOCK), BLOCK)
            total = first_ref[at, :]
            for left, right in zip(left_refs, weight_refs):
                total = total + product(left[at, :], right[: 3 * width, :], NN)
            out_ref[at, :] = total

    return call(
        kernel,
        "input_backward",
        3,
        shaped((L, D), wide),
        [scalars, first_grad, *qkv_grads, *flat(projections)],
        [pltpu.VMEM((2, 3 * width + EXTRA, D), low_type)],
    )


def solution(mesh):
    dp_size = mesh.shape["dp"]
    tensor_size = mesh.shape["tensor"]
    masks = [1, 2, 6] + [1 << bit for bit in range(3, 16)]
    masks = masks[: dp_size.bit_length() - 1]

    def over_tensor(value, mask):
        return lax.ppermute(value, "tensor", [(i, i ^ mask) for i in range(tensor_size)])

    def over_dp(value, mask):
        return lax.ppermute(value, "dp", [(i, i ^ mask) for i in range(dp_size)])

    def body(
        tokens,
        grad_out,
        lengths,
        segment_ids,
        query_weight,
        query_bias,
        key_weight,
        value_weight,
        value_bias,
        mixer_weight,
        mixer_bias,
        first_gain,
        first_shift,
        inner_weight,
        inner_bias,
        outer_weight,
        outer_bias,
        second_gain,
        second_shift,
    ):
        width = query_weight.shape[1]
        place = lax.axis_index("tensor")
        odd = lax.axis_index("dp") % 2
        chain = [jnp.zeros((8, 128), wide)]

        def after(*values):
            held = lax.optimization_barrier((chain[0],) + values)
            return held[1:] if len(values) > 1 else held[1]

        def done(*values):
            chain[0] = lax.optimization_barrier((chain[0],) + values)[0]
            return values if len(values) > 1 else values[0]

        def half(value, which):
            rows = value.shape[0] // 2
            return lax.dynamic_slice_in_dim(value, which * rows, rows, 0)

        bias_row = jnp.concatenate([query_bias, jnp.zeros_like(query_bias), value_bias])
        own_projection = jnp.concatenate(
            [
                query_weight.T,
                key_weight.T,
                value_weight.T,
                jnp.pad(bias_row[None, :], ((0, 0), (0, D - 3 * width))),
                inner_bias[None, :],
                jnp.zeros((EXTRA - 2, D), low_type),
            ],
            axis=0,
        )
        own_projection = done(own_projection)
        own = [own_projection, mixer_weight, inner_weight, outer_weight]
        mine, partner = [], []
        for group in range(4):
            piece = done(half(after(own[group]), odd))
            mine.append(over_tensor(piece, 2))
            partner.append(over_tensor(after(own[group]), 1))
        vectors = jnp.stack(
            [mixer_bias, first_gain, first_shift, outer_bias, second_gain, second_shift]
            + [jnp.zeros_like(mixer_bias)] * 2
        )
        scalars = jnp.stack(
            [place, lax.dynamic_index_in_dim(lengths, place, 0, keepdims=False), odd]
        ).astype(jnp.int32)
        vectors, scalars = done(vectors, scalars)
        slots = [[(own[group],), (partner[group],), None, None] for group in range(4)]

        def spread(group):
            near = done(after(mine[group]))
            far = over_dp(near, masks[0])
            slots[group][2] = (near, far)
            slots[group][3] = (over_tensor(near, 1), over_tensor(far, 1))

        heads = {}

        def attend(slot):
            weights = slots[0][slot]
            weights = (after(*weights),) if len(weights) == 1 else after(*weights)
            heads[slot] = done(*attend_forward(scalars, segment_ids, tokens, weights))

        attend(0)
        attend(1)
        spread(0)
        spread(1)
        spread(2)
        attend(2)
        attend(3)
        spread(3)
        projections, mixers, inners, outers = slots
        attended = [heads[j][1] for j in range(4)]
        hat_one, inverse_one, normed_low, sums_one = done(
            *mix_norm(scalars, vectors, tokens, attended, mixers)
        )
        *activated, slopes = done(*inner_forward(scalars, normed_low, inners, projections))
        layer_out, second_grad, ffn_low, sums_two = done(
            *outer_norm(scalars, vectors, hat_one, grad_out, activated, outers)
        )

        tokens_other = over_tensor(tokens, 1)
        attended_other = {j: over_tensor(attended[j ^ 1], 1) for j in (0, 2)}
        normed_other = over_tensor(normed_low, 1)
        activated_other = {j: over_tensor(activated[j ^ 1], 1) for j in (0, 2)}
        ffn_other = over_tensor(ffn_low, 1)

        def pair_product(left, right, left_other, right_other):
            left, right, left_other, right_other = after(left, right, left_other, right_other)
            return done(
                (product(left, right, TN) + product(left_other, right_other, TN)).astype(low_type)
            )

        def add_low(left, right):
            return (left.astype(wide) + right.astype(wide)).astype(low_type)

        last = len(masks)
        hops = last + 2

        class Reduction:
            def __init__(self, sent):
                self.incoming = over_tensor(sent, 2)
                self.kept = None
                self.stage = 0

            def hop(self):
                kept, incoming = after(self.kept, self.incoming)
                if self.stage == 0:
                    sent = done(add_low(half(kept, 1 - odd), half(incoming, 1 - odd)))
                    self.incoming = over_dp(sent, masks[0])
                    self.kept = add_low(half(kept, odd), half(incoming, odd))
                elif self.stage <= last:
                    self.kept = done(add_low(kept, incoming))
                    mask = masks[self.stage] if self.stage < last else masks[0]
                    self.incoming = over_dp(self.kept, mask)
                else:
                    self.halves = (
                        jnp.where(odd == 0, kept, incoming).astype(wide),
                        jnp.where(odd == 0, incoming, kept).astype(wide),
                    )
                self.stage += 1

        def cut(value):
            rows = value.shape[0] // 2
            return [value[:rows], value[rows:]]

        *inner_lows, inner_bias_rows = done(*inner_backward(scalars, ffn_low, slopes, outers))
        inner_other = {j: over_tensor(inner_lows[j ^ 1], 1) for j in (0, 2)}

        def outer_part(j):
            return [pair_product(activated[j], ffn_low, activated_other[j], ffn_other)]

        def inner_part(j):
            return cut(pair_product(normed_low, inner_lows[j], normed_other, inner_other[j]))

        outer_chain = [Reduction(part) for part in outer_part(2)]
        first_grad, branch_low, sums_three = done(
            *first_backward(
                scalars, vectors, hat_one, inverse_one, second_grad, inner_lows, inners
            )
        )
        branch_other = over_tensor(branch_low, 1)
        inner_chain = [Reduction(part) for part in inner_part(2)]

        qkv_grads, qkv_bias, qkv_other = {}, {}, {}

        def retreat(slot):
            low = after(branch_low)
            qkv_grads[slot], qkv_bias[slot] = done(
                *attend_backward(scalars, slot, low, mixers[slot], *heads[slot])
            )

        def heads_part(j):
            qkv = pair_product(qkv_grads[j], tokens, qkv_other[j], tokens_other)
            mixer = pair_product(attended[j], branch_low, attended_other[j], branch_other)
            return [qkv[: 2 * width], done(jnp.concatenate([qkv[2 * width :], mixer]))]

        def keep(reductions, parts):
            for reduction, part in zip(reductions, parts):
                reduction.kept = part

        retreat(3)
        qkv_other[2] = over_tensor(qkv_grads[3], 1)
        retreat(2)
        keep(outer_chain, outer_part(0))
        heads_chain = [Reduction(part) for part in heads_part(2)]
        retreat(1)
        qkv_other[0] = over_tensor(qkv_grads[1], 1)
        outer_chain[0].hop()
        retreat(0)
        keep(inner_chain, inner_part(0))
        keep(heads_chain, heads_part(0))
        inner_chain[0].hop()
        small = jnp.concatenate(
            [
                sums_one,
                sums_two,
                sums_three,
                inner_bias_rows,
                qkv_bias[0] + qkv_bias[1] + qkv_bias[2] + qkv_bias[3],
            ]
        )
        small = done(small)
        small_hops = [(over_tensor, 1), (over_tensor, 2)] + [(over_dp, mask) for mask in masks]

        def small_hop(small):
            over, mask = small_hops.pop(0)
            return done(small + after(over(small, mask)))

        tokens_grad = done(
            input_backward(scalars, first_grad, [qkv_grads[j] for j in range(4)], projections)
        )
        chains = outer_chain + inner_chain + heads_chain
        order = [0, 1, 2, 0, 1, 3, 2, 0, 1, 4, 2, 0, 3, 4, 1, 2, 3, 4, 1, 2, 3, 4, 3, 4]
        for which in order:
            if chains[which].stage < hops:
                chains[which].hop()
            if small_hops:
                small = small_hop(small)
        while small_hops:
            small = small_hop(small)
        for chunk in chains:
            while chunk.stage < hops:
                chunk.hop()

        totals = jnp.sum(jnp.stack([small[0], small[1], small[11]]), axis=1)
        statistics = jnp.sqrt(totals / (small[2, 0] * D))
        own_inner_bias = lax.dynamic_index_in_dim(small[24:28], place, 0, keepdims=False)
        own_qkv_bias = lax.dynamic_index_in_dim(small[32:36], place, 0, keepdims=False)
        query_grad, key_grad = heads_chain[0].halves
        value_grad, mixer_grad = heads_chain[1].halves
        return (
            layer_out,
            tokens_grad,
            query_grad.T,
            own_qkv_bias[:width],
            key_grad.T,
            value_grad.T,
            own_qkv_bias[2 * width : 3 * width],
            mixer_grad,
            small[18],
            small[16],
            small[17],
            jnp.concatenate([part for chunk in inner_chain for part in chunk.halves]),
            own_inner_bias,
            jnp.concatenate([part for chunk in outer_chain for part in chunk.halves]),
            small[10],
            small[8],
            small[9],
            statistics,
        )

    in_specs = (
        P(("dp", "tensor"), None),
        P(("dp", "tensor"), None),
        P("dp"),
        P("dp", None),
        P(None, "tensor"),
        P("tensor"),
        P(None, "tensor"),
        P(None, "tensor"),
        P("tensor"),
        P("tensor", None),
        P(),
        P(),
        P(),
        P(None, "tensor"),
        P("tensor"),
        P("tensor", None),
        P(),
        P(),
        P(),
    )
    out_specs = (
        P(("dp", "tensor"), None),
        P(("dp", "tensor"), None),
        P(None, "tensor"),
        P("tensor"),
        P(None, "tensor"),
        P(None, "tensor"),
        P("tensor"),
        P("tensor", None),
        P(),
        P(),
        P(),
        P(None, "tensor"),
        P("tensor"),
        P("tensor", None),
        P(),
        P(),
        P(),
        P(),
    )
    return jax.shard_map(body, mesh=mesh, in_specs=in_specs, out_specs=out_specs, check_vma=False)
```

```python
import jax
import jax.numpy as jnp
from jax import lax
from jax.experimental import pallas as pl
from jax.experimental.pallas import tpu as pltpu
from jax.sharding import PartitionSpec as P

D = 768
HEAD_DIM = 64
L = 512
EXTRA = 32

eps_norm = 1e-06
root_half = 0.7071067811865476
inv_root_tau = 0.3989422804014327
low_type = jnp.bfloat16
wide = jnp.float32
NN = (((1,), (0,)), ((), ()))
NT = (((1,), (1,)), ((), ()))
TN = (((0,), (0,)), ((), ()))


def product(left, right, dims):
    return lax.dot_general(left, right, dims, preferred_element_type=wide)


def shaped(shape, dtype):
    return jax.ShapeDtypeStruct(shape, dtype)


COST = 100000000000
ORDER = (1, 0, 1, 2, 0, 3, 1, 2, 0, 2, 3, 1, 3, 2, 3, 1, 3, 2)


def call(kernel, name, out_shape, operands, spaces, out_spaces, scratch=(), limit=14):
    place = {"v": pltpu.VMEM, "h": pltpu.HBM}
    out_shape = tuple(
        pltpu.HBM(one.shape, one.dtype) if letter == "h" else one
        for one, letter in zip(out_shape, out_spaces)
    )
    operands = operands[:1] + [
        pltpu.with_memory_space_constraint(one, pltpu.HBM) if letter == "h" else one
        for one, letter in zip(operands[1:], spaces)
    ]
    return pl.pallas_call(
        kernel,
        out_shape=out_shape,
        in_specs=[pl.BlockSpec(memory_space=pltpu.SMEM)]
        + [pl.BlockSpec(memory_space=place[letter]) for letter in spaces],
        out_specs=tuple(pl.BlockSpec(memory_space=place[letter]) for letter in out_spaces),
        scratch_shapes=list(scratch),
        compiler_params=pltpu.CompilerParams(vmem_limit_bytes=limit << 20),
        cost_estimate=pl.CostEstimate(flops=COST, transcendentals=0, bytes_accessed=COST // 300),
        name=name,
    )(*operands)


def read_scalars(scalar_ref):
    place = scalar_ref[0]
    return place, scalar_ref[1], scalar_ref[2 + place]


def begin(source, target, semaphore):
    copy = pltpu.make_async_copy(source, target, semaphore)
    copy.start()
    return copy


def begin_weight(parts, odd, target, semaphores, at, first=0):
    rows = target.shape[0] // len(parts)
    first = first // len(parts)
    parts = [part.at[pl.ds(first, rows)] for part in parts]
    if len(parts) == 1:
        return [begin(parts[0], target, semaphores.at[at])]
    return [
        begin(
            part,
            target.at[pl.ds(pl.multiple_of(which * rows, rows), rows)],
            semaphores.at[at + index],
        )
        for index, (part, which) in enumerate(zip(parts, (odd, 1 - odd)))
    ]


def wait(copies):
    for copy in copies:
        copy.wait()


def unflatten(refs, slots):
    out, at = [], 0
    for parts in slots:
        out.append(refs[at : at + len(parts)])
        at += len(parts)
    return out, refs[at:]


def flat(slots):
    return [part for parts in slots for part in parts]


WIDTH = D // 4
PROJECTION_ROWS = 3 * WIDTH + EXTRA


def prepare(scalars, vectors, weights, mixer, inner, outer):
    rows = PROJECTION_ROWS + WIDTH

    def kernel(scalar_ref, vector_ref, query, key, value, mixer_in, inner_in, outer_in, *refs):
        piece_ref, inner_out, outer_out, own_out, own_ref, semaphores = refs
        odd = scalar_ref[1]
        fetches = [
            begin(source, own_ref.at[pl.ds(start, WIDTH)], semaphores.at[index])
            for index, (source, start) in enumerate(
                zip((query, key, value, mixer_in), (0, WIDTH, 2 * WIDTH, PROJECTION_ROWS))
            )
        ]
        half = D // 2
        chosen = pl.ds(pl.multiple_of(odd * half, half), half)
        passes = [
            begin(inner_in.at[chosen], inner_out, semaphores.at[4]),
            begin(outer_in.at[chosen], outer_out, semaphores.at[5]),
        ]
        own_ref[3 * WIDTH : PROJECTION_ROWS, :] = jnp.zeros((EXTRA, D), low_type)
        own_ref[3 * WIDTH : 3 * WIDTH + 8, :] = vector_ref[8:16, :]
        wait(fetches)
        copies = [begin(own_ref, own_out, semaphores.at[6])]
        half = PROJECTION_ROWS // 2
        piece_ref[:half, :] = own_ref[pl.ds(pl.multiple_of(odd * half, 16), half), :]
        half_mixer = WIDTH // 2
        piece_ref[half:, :] = own_ref[
            pl.ds(pl.multiple_of(PROJECTION_ROWS + odd * half_mixer, 16), half_mixer), :
        ]
        wait(copies + passes)

    return call(
        kernel,
        "prepare",
        (
            shaped((rows // 2, D), low_type),
            shaped((D // 2, D), low_type),
            shaped((D // 2, D), low_type),
            shaped((rows, D), low_type),
        ),
        [scalars, vectors, *weights, mixer, inner, outer],
        "vhhhhhh",
        "vvvh",
        [pltpu.VMEM((rows, D), low_type), pltpu.SemaphoreType.DMA((7,))],
    )


def tick(scalars, token):
    def kernel(scalar_ref, token_ref, out_ref):
        out_ref[...] = token_ref[...]

    return call(kernel, "tick", (shaped(token.shape, token.dtype),), [scalars, token], "v", "v")[0]


def add_rows(left, right):
    return (left.astype(wide) + right.astype(wide)).astype(low_type)


def split_add(scalars, kept, incoming):
    half = kept.shape[0] // 2

    def kernel(scalar_ref, kept_ref, incoming_ref, send_ref, keep_ref):
        odd = scalar_ref[1]
        theirs = pl.ds(pl.multiple_of((1 - odd) * half, 16), half)
        ours = pl.ds(pl.multiple_of(odd * half, 16), half)
        send_ref[...] = add_rows(kept_ref[theirs, :], incoming_ref[theirs, :])
        keep_ref[...] = add_rows(kept_ref[ours, :], incoming_ref[ours, :])

    return call(
        kernel,
        "split_add",
        (shaped((half, D), low_type),) * 2,
        [scalars, kept, incoming],
        "vv",
        "vv",
    )


def message(rows, extra):
    high = extra.astype(low_type)
    return jnp.concatenate([rows, high, (extra - high.astype(wide)).astype(low_type)], axis=0)


def mixed_hop(scalars, kept, extra, incoming, split):
    rows = kept.shape[0] // 2 if split else kept.shape[0]
    count = extra.shape[0]

    def kernel(scalar_ref, kept_ref, extra_ref, incoming_ref, message_ref, keep_ref, out_ref):
        at = kept.shape[0]
        total = extra_ref[...] + (
            incoming_ref[at : at + count, :].astype(wide)
            + incoming_ref[at + count : at + 2 * count, :].astype(wide)
        )
        out_ref[...] = total
        high = total.astype(low_type)
        message_ref[rows : rows + count, :] = high
        message_ref[rows + count :, :] = (total - high.astype(wide)).astype(low_type)
        if split:
            odd = scalar_ref[1]
            theirs = pl.ds(pl.multiple_of((1 - odd) * rows, 16), rows)
            ours = pl.ds(pl.multiple_of(odd * rows, 16), rows)
            message_ref[:rows, :] = add_rows(kept_ref[theirs, :], incoming_ref[theirs, :])
            keep_ref[...] = add_rows(kept_ref[ours, :], incoming_ref[ours, :])
        else:
            joined = add_rows(kept_ref[...], incoming_ref[:rows, :])
            message_ref[:rows, :] = joined
            keep_ref[...] = joined

    return call(
        kernel,
        "mixed_hop",
        (
            shaped((rows + 2 * count, D), low_type),
            shaped((rows, D), low_type),
            shaped((count, D), wide),
        ),
        [scalars, kept, extra, incoming],
        "vvv",
        "vvv",
    )


def finish(scalars, kept, incoming, outputs):
    half = kept.shape[0]
    rows = 2 * half // outputs

    def kernel(scalar_ref, kept_ref, incoming_ref, *refs):
        outs, joined, semaphores = refs[:outputs], refs[outputs], refs[outputs + 1]
        odd = scalar_ref[1]
        joined[pl.ds(pl.multiple_of(odd * half, 16), half), :] = kept_ref[...].astype(wide)
        joined[pl.ds(pl.multiple_of((1 - odd) * half, 16), half), :] = incoming_ref[
            :half, :
        ].astype(wide)
        wait(
            [
                begin(joined.at[pl.ds(index * rows, rows)], out, semaphores.at[index])
                for index, out in enumerate(outs)
            ]
        )

    return call(
        kernel,
        "finish",
        (shaped((rows, D), wide),) * outputs,
        [scalars, kept, incoming],
        "vv",
        "h" * outputs,
        [pltpu.VMEM((2 * half, D), wide), pltpu.SemaphoreType.DMA((outputs,))],
    )


def attend_forward(scalars, segment_ids, tokens, projection):
    width = D // 4
    heads = width // HEAD_DIM
    block = 256

    def kernel(scalar_ref, segment_ref, tokens_ref, *refs):
        (parts,), refs = unflatten(refs, [projection])
        attended_ref, bias_ref, qkv_out, probs_out, mask, weight, qkv_ref, probs_ref, semaphores = refs
        place, odd, length = read_scalars(scalar_ref)
        fetch = begin_weight(parts, odd, weight, semaphores, 0)
        query_owner = segment_ref[pl.ds(place, 1), :].astype(wide)
        key_owner = jnp.broadcast_to(query_owner, (128, L)).T
        key_at = lax.broadcasted_iota(jnp.int32, (L, 128), 0)
        key_owner = jnp.where(key_at < length, key_owner, -1.0)
        query_at = lax.broadcasted_iota(jnp.int32, (L, 128), 1)
        for start in range(0, L, 128):
            allowed = (key_owner == query_owner[:, start : start + 128]) | (
                key_at == query_at + start
            )
            mask[:, start : start + 128] = jnp.where(allowed, 0.0, -1e30)
        wait(fetch)
        bias_ref[...] = weight[3 * width : 3 * width + 16, :]
        bias = weight[3 * width : 3 * width + 1, : 3 * width].astype(wide)
        qkv_ref[...] = (product(tokens_ref[...], weight[: 3 * width, :], NT) + bias).astype(
            low_type
        )
        qkv_copy = begin(qkv_ref, qkv_out, semaphores.at[2])

        @pl.loop(0, L // block)
        def _(step):
            rows = pl.ds(pl.multiple_of(step * block, block), block)
            for head in range(heads):
                at = head * HEAD_DIM
                queries = qkv_ref[rows, at : at + HEAD_DIM] * jnp.asarray(
                    HEAD_DIM**-0.5, low_type
                )
                key_rows = qkv_ref[:, width + at : width + at + HEAD_DIM]
                values = qkv_ref[:, 2 * width + at : 2 * width + at + HEAD_DIM]
                scores = product(key_rows, queries, NT) + mask[:, rows]
                highest = jnp.max(scores, axis=0, keepdims=True)
                expanded = jnp.exp(scores - highest)
                total = jnp.sum(expanded, axis=0, keepdims=True)
                probs = (expanded * (1.0 / total)).astype(low_type)
                probs_ref[step, head] = probs
                attended_ref[rows, at : at + HEAD_DIM] = product(probs, values, TN).astype(
                    low_type
                )
            begin(probs_ref.at[step], probs_out.at[step], semaphores.at[3 + step])

        qkv_copy.wait()
        for step in range(L // block):
            pltpu.make_async_copy(
                probs_ref.at[step], probs_out.at[step], semaphores.at[3 + step]
            ).wait()

    kept = (L // block, heads, L, block)
    return call(
        kernel,
        "attend_forward",
        (
            shaped((L, width), low_type),
            shaped((16, D), low_type),
            shaped((L, 3 * width), low_type),
            shaped(kept, low_type),
        ),
        [scalars, segment_ids, tokens, *projection],
        "vv" + "h" * len(projection),
        "vvhh",
        [
            pltpu.VMEM((L, L), wide),
            pltpu.VMEM((3 * width + EXTRA, D), low_type),
            pltpu.VMEM((L, 3 * width), low_type),
            pltpu.VMEM(kept, low_type),
            pltpu.SemaphoreType.DMA((3 + L // block,)),
        ],
    )


def attend_backward(scalars, slot, branch_low, mixer, attended, qkv, probs):
    width = D // 4
    heads = width // HEAD_DIM
    block = 256

    def kernel(scalar_ref, branch_ref, attended_ref, qkv_in, probs_in, *refs):
        (parts,), refs = unflatten(refs, [mixer])
        grad_ref, bias_ref, weight, qkv_ref, probs_ref, outgoing, sums, dots, semaphores = refs
        fetch = begin_weight(parts, scalar_ref[1], weight, semaphores, 0, PROJECTION_ROWS)
        fetch_rest = [
            begin(qkv_in, qkv_ref, semaphores.at[2]),
            begin(probs_in, probs_ref, semaphores.at[3]),
        ]
        wait(fetch)
        attended_grad = product(branch_ref[...], weight[...], NT).astype(low_type)
        outgoing[...] = attended_grad
        along = (attended_ref[...].astype(wide) * attended_grad.astype(wide)).T
        for head in range(heads):
            dots[head : head + 1, :] = jnp.sum(
                along[head * HEAD_DIM : (head + 1) * HEAD_DIM], axis=0, keepdims=True
            )
            sums[head] = jnp.zeros((L, HEAD_DIM), wide)
        wait(fetch_rest)

        @pl.loop(0, L // block)
        def _(step):
            rows = pl.ds(pl.multiple_of(step * block, block), block)
            for head in range(heads):
                at = head * HEAD_DIM
                queries = qkv_ref[:, at : at + HEAD_DIM] * jnp.asarray(HEAD_DIM**-0.5, low_type)
                key_rows = qkv_ref[rows, width + at : width + at + HEAD_DIM]
                values = qkv_ref[rows, 2 * width + at : 2 * width + at + HEAD_DIM]
                grad = outgoing[:, at : at + HEAD_DIM]
                probs = jnp.concatenate(
                    [probs_ref[part, head, rows, :] for part in range(L // block)], axis=1
                )
                probs_grad = product(values, grad, NT)
                scores_grad = (
                    probs.astype(wide) * (probs_grad - dots[head : head + 1, :])
                ).astype(low_type)
                grad_ref[rows, width + at : width + at + HEAD_DIM] = product(
                    scores_grad, queries, NN
                ).astype(low_type)
                grad_ref[rows, 2 * width + at : 2 * width + at + HEAD_DIM] = product(
                    probs, grad, NN
                ).astype(low_type)
                sums[head] += product(scores_grad, key_rows, TN)

        for head in range(heads):
            at = head * HEAD_DIM
            grad_ref[:, at : at + HEAD_DIM] = (sums[head] * (HEAD_DIM**-0.5)).astype(low_type)
        bias_ref[...] = jnp.zeros((8, D), wide)
        quarter = scalar_ref[0] ^ slot
        bias_ref[pl.ds(quarter, 1), : 3 * width] = jnp.sum(
            grad_ref[...].astype(wide), axis=0, keepdims=True
        )

    return call(
        kernel,
        "attend_backward",
        (shaped((L, 3 * width), low_type), shaped((8, D), wide)),
        [scalars, branch_low, attended, qkv, probs, *mixer],
        "vvhh" + "h" * len(mixer),
        "vv",
        [
            pltpu.VMEM((width, D), low_type),
            pltpu.VMEM((L, 3 * width), low_type),
            pltpu.VMEM(probs.shape, low_type),
            pltpu.VMEM((L, width), low_type),
            pltpu.VMEM((heads, L, HEAD_DIM), wide),
            pltpu.VMEM((8, L), wide),
            pltpu.SemaphoreType.DMA((4,)),
        ],
    )


def normalize(rows):
    center = rows - jnp.mean(rows, axis=-1, keepdims=True)
    inverse = lax.rsqrt(jnp.mean(center * center, axis=-1, keepdims=True) + eps_norm)
    return center * inverse, inverse


def normalize_backward(scaled, normed, inverse):
    middle = jnp.mean(scaled, axis=-1, keepdims=True)
    along = jnp.mean(scaled * normed, axis=-1, keepdims=True)
    return inverse * (scaled - middle - normed * along)


def column_sum(rows):
    return jnp.sum(rows, axis=0, keepdims=True)


BLOCK = 256
STEPS = L // BLOCK


def block_rows(step):
    return pl.ds(pl.multiple_of(step * BLOCK, BLOCK), BLOCK)


def mix_norm(scalars, vectors, tokens, attended, mixers):
    width = D // 4

    def kernel(scalar_ref, vector_ref, tokens_ref, *refs):
        attended_refs = refs[:4]
        parts, refs = unflatten(refs[4:], mixers)
        inverse_ref, low_ref, sums_ref, hat_out, weight, hat_ref, semaphores = refs
        _, odd, length = read_scalars(scalar_ref)
        fetches = [
            begin_weight(
                parts[i], odd, weight.at[pl.ds(i * width, width)], semaphores, 2 * i, PROJECTION_ROWS
            )
            for i in range(4)
        ]
        vectors = vector_ref[...].astype(wide)
        sums_ref[...] = jnp.zeros((8, D), wide)
        for fetch in fetches:
            wait(fetch)

        @pl.loop(0, STEPS)
        def _(step):
            at = block_rows(step)
            branch = vectors[0:1]
            for index in range(4):
                branch = branch + product(
                    attended_refs[index][at, :], weight[index * width : (index + 1) * width], NN
                )
            rows = tokens_ref[at, :].astype(wide)
            hat, inverse = normalize(rows + branch)
            hat_ref[at, :] = hat
            begin(hat_ref.at[at], hat_out.at[at], semaphores.at[8 + step])
            inverse_ref[at, :] = inverse
            low_ref[at, :] = (hat * vectors[1:2] + vectors[2:3]).astype(low_type)
            place = lax.broadcasted_iota(jnp.int32, (BLOCK, 1), 0) + step * BLOCK
            valid = (place < length).astype(wide)
            sums_ref[0:1, :] += column_sum(valid * rows * rows)
            sums_ref[1:2, :] += column_sum(valid * branch * branch)
            sums_ref[2:3, :] += column_sum(jnp.broadcast_to(valid, (BLOCK, D)))

        for step in range(STEPS):
            at = block_rows(step)
            pltpu.make_async_copy(hat_ref.at[at], hat_out.at[at], semaphores.at[8 + step]).wait()

    return call(
        kernel,
        "mix_norm",
        (shaped((L, 1), wide), shaped((L, D), low_type), shaped((8, D), wide), shaped((L, D), wide)),
        [scalars, vectors, tokens, *attended, *flat(mixers)],
        "vv" + "v" * 4 + "h" * len(flat(mixers)),
        "vvvh",
        [
            pltpu.VMEM((D, D), low_type),
            pltpu.VMEM((L, D), wide),
            pltpu.SemaphoreType.DMA((8 + STEPS,)),
        ],
    )


def inner_forward(scalars, normed_low, weights, biases):
    chunk = 256

    def kernel(scalar_ref, normed_ref, *refs):
        bias_refs = refs[:2]
        parts, refs = unflatten(refs[2:], weights)
        out_refs, slope_out, weight, bias, slope_ref, semaphores = refs[:2], *refs[2:]
        odd = scalar_ref[1]
        fetches = [begin_weight(parts[i], odd, weight.at[i], semaphores, 2 * i) for i in range(2)]
        for index in range(2):
            bias[index] = bias_refs[index][...].astype(wide)

        @pl.loop(0, 2)
        def _(slot):
            for index in range(2):

                @pl.when(slot == index)
                def _(index=index):
                    wait(fetches[index])

            @pl.loop(0, D // chunk)
            def _(step):
                columns = pl.ds(pl.multiple_of(step * chunk, chunk), chunk)
                inner_pre = (
                    product(normed_ref[...], weight[slot, :, columns], NN)
                    + bias[slot, 1:2, columns]
                )
                below = 0.5 * (1.0 + lax.erf(inner_pre * root_half))
                density = jnp.exp(-0.5 * inner_pre * inner_pre) * inv_root_tau
                activated = (inner_pre * below).astype(low_type)
                slope_ref[slot, :, columns] = (below + inner_pre * density).astype(low_type)
                for index in range(2):

                    @pl.when(slot == index)
                    def _(index=index):
                        out_refs[index][:, columns] = activated

            begin(slope_ref.at[slot], slope_out.at[slot], semaphores.at[4 + slot])

        for slot in range(2):
            pltpu.make_async_copy(
                slope_ref.at[slot], slope_out.at[slot], semaphores.at[4 + slot]
            ).wait()

    return call(
        kernel,
        "inner_forward",
        (shaped((L, D), low_type),) * 2 + (shaped((2, L, D), low_type),),
        [scalars, normed_low, *biases, *flat(weights)],
        "vvv" + "h" * len(flat(weights)),
        "vvh",
        [
            pltpu.VMEM((2, D, D), low_type),
            pltpu.VMEM((2, 16, D), wide),
            pltpu.VMEM((2, L, D), low_type),
            pltpu.SemaphoreType.DMA((6,)),
        ],
    )


def outer_norm(scalars, vectors, hat_one, grad_out, activated, weights):
    def kernel(scalar_ref, vector_ref, hat_in, incoming_in, *refs):
        left_refs = refs[:4]
        parts, refs = unflatten(refs[4:], weights)
        low_ref, sums_ref, grad_out_ref, result_out = refs[:4]
        weight, hat_ref, incoming_ref, grad_ref, result_ref, semaphores = refs[4:]
        _, odd, length = read_scalars(scalar_ref)
        fetches = [begin_weight(parts[i], odd, weight.at[i], semaphores, 2 * i) for i in range(4)]
        fetch_rest = [
            begin(hat_in, hat_ref, semaphores.at[8]),
            begin(incoming_in, incoming_ref, semaphores.at[9]),
        ]
        vectors = vector_ref[...].astype(wide)
        sums_ref[...] = jnp.zeros((8, D), wide)

        def outgoing(step):
            at = block_rows(step)
            return (
                pltpu.make_async_copy(
                    grad_ref.at[at], grad_out_ref.at[at], semaphores.at[10 + 2 * step]
                ),
                pltpu.make_async_copy(
                    result_ref.at[at], result_out.at[at], semaphores.at[11 + 2 * step]
                ),
            )

        @pl.loop(0, STEPS)
        def _(step):
            at = block_rows(step)
            branch = vectors[3:4]
            for index in range(4):

                @pl.when(step == 0)
                def _(index=index):
                    wait(fetches[index])

                branch = branch + product(left_refs[index][at, :], weight[index], NN)

            @pl.when(step == 0)
            def _():
                wait(fetch_rest)

            normed_one = hat_ref[at, :] * vectors[1:2] + vectors[2:3]
            hat, inverse = normalize(normed_one + branch)
            result_ref[at, :] = (hat * vectors[4:5] + vectors[5:6]).astype(low_type)
            incoming = incoming_ref[at, :].astype(wide)
            grad = normalize_backward(incoming * vectors[4:5], hat, inverse)
            grad_ref[at, :] = grad
            for copy in outgoing(step):
                copy.start()
            low_ref[at, :] = grad.astype(low_type)
            place = lax.broadcasted_iota(jnp.int32, (BLOCK, 1), 0) + step * BLOCK
            valid = (place < length).astype(wide)
            sums_ref[0:1, :] += column_sum(incoming * hat)
            sums_ref[1:2, :] += column_sum(incoming)
            sums_ref[2:3, :] += column_sum(grad)
            sums_ref[3:4, :] += column_sum(valid * branch * branch)

        for step in range(STEPS):
            wait(outgoing(step))

    return call(
        kernel,
        "outer_norm",
        (
            shaped((L, D), low_type),
            shaped((8, D), wide),
            shaped((L, D), wide),
            shaped((L, D), low_type),
        ),
        [scalars, vectors, hat_one, grad_out, *activated, *flat(weights)],
        "vhh" + "v" * 4 + "h" * len(flat(weights)),
        "vvhh",
        [
            pltpu.VMEM((4, D, D), low_type),
            pltpu.VMEM((L, D), wide),
            pltpu.VMEM((L, D), low_type),
            pltpu.VMEM((L, D), wide),
            pltpu.VMEM((L, D), low_type),
            pltpu.SemaphoreType.DMA((10 + 2 * STEPS,)),
        ],
        limit=18,
    )


def inner_backward(scalars, ffn_low, slopes, weights):
    chunk = 256

    def kernel(scalar_ref, ffn_ref, slope_one, slope_two, *refs):
        parts, refs = unflatten(refs, weights)
        out_refs, bias_ref, weight, slope_ref, semaphores = refs[:4], *refs[4:]
        place, odd = scalar_ref[0], scalar_ref[1]
        fetches = []
        for index in range(4):
            slope = (slope_one, slope_two)[index // 2]
            fetches.append(
                begin_weight(parts[index], odd, weight.at[index], semaphores, 2 * index)
                + [begin(slope.at[index % 2], slope_ref.at[index], semaphores.at[8 + index])]
            )
        bias_ref[...] = jnp.zeros((8, D), wide)

        @pl.loop(0, 4)
        def _(slot):
            for index in range(4):

                @pl.when(slot == index)
                def _(index=index):
                    wait(fetches[index])

            @pl.loop(0, D // chunk)
            def _(step):
                columns = pl.ds(pl.multiple_of(step * chunk, chunk), chunk)
                grad = product(ffn_ref[...], weight[slot, columns, :], NT) * slope_ref[
                    slot, :, columns
                ].astype(wide)
                bias_ref[pl.ds(place ^ slot, 1), columns] = column_sum(grad)
                low = grad.astype(low_type)
                for index in range(4):

                    @pl.when(slot == index)
                    def _(index=index):
                        out_refs[index][:, columns] = low

    return call(
        kernel,
        "inner_backward",
        (shaped((L, D), low_type),) * 4 + (shaped((8, D), wide),),
        [scalars, ffn_low, *slopes, *flat(weights)],
        "vhh" + "h" * len(flat(weights)),
        "vvvvv",
        [
            pltpu.VMEM((4, D, D), low_type),
            pltpu.VMEM((4, L, D), low_type),
            pltpu.SemaphoreType.DMA((12,)),
        ],
        limit=16,
    )


def first_backward(scalars, vectors, hat_one, inverse_one, second_grad, inner_lows, weights):
    def kernel(scalar_ref, vector_ref, hat_in, inverse_ref, second_in, *refs):
        left_refs = refs[:4]
        parts, refs = unflatten(refs[4:], weights)
        low_ref, sums_ref, grad_out, weight, hat_ref, second_ref, grad_ref, semaphores = refs
        odd = scalar_ref[1]
        fetches = [begin_weight(parts[i], odd, weight.at[i], semaphores, 2 * i) for i in range(4)]
        fetch_rest = [
            begin(second_in, second_ref, semaphores.at[8]),
            begin(hat_in, hat_ref, semaphores.at[9]),
        ]
        gain = vector_ref[1:2, :].astype(wide)
        sums_ref[...] = jnp.zeros((8, D), wide)

        @pl.loop(0, STEPS)
        def _(step):
            at = block_rows(step)
            total = 0.0
            for index in range(4):

                @pl.when(step == 0)
                def _(index=index):
                    wait(fetches[index])

                total = total + product(left_refs[index][at, :], weight[index], NT)

            @pl.when(step == 0)
            def _():
                wait(fetch_rest)

            total = total + second_ref[at, :]
            hat = hat_ref[at, :]
            grad = normalize_backward(total * gain, hat, inverse_ref[at, :])
            grad_ref[at, :] = grad
            begin(grad_ref.at[at], grad_out.at[at], semaphores.at[10 + step])
            low_ref[at, :] = grad.astype(low_type)
            sums_ref[0:1, :] += column_sum(total * hat)
            sums_ref[1:2, :] += column_sum(total)
            sums_ref[2:3, :] += column_sum(grad)

        for step in range(STEPS):
            at = block_rows(step)
            pltpu.make_async_copy(grad_ref.at[at], grad_out.at[at], semaphores.at[10 + step]).wait()

    return call(
        kernel,
        "first_backward",
        (shaped((L, D), low_type), shaped((8, D), wide), shaped((L, D), wide)),
        [scalars, vectors, hat_one, inverse_one, second_grad, *inner_lows, *flat(weights)],
        "vhvh" + "v" * 4 + "h" * len(flat(weights)),
        "vvh",
        [
            pltpu.VMEM((4, D, D), low_type),
            pltpu.VMEM((L, D), wide),
            pltpu.VMEM((L, D), wide),
            pltpu.VMEM((L, D), wide),
            pltpu.SemaphoreType.DMA((10 + STEPS,)),
        ],
        limit=18,
    )


def input_backward(scalars, first_grad, qkv_grads, projections):
    width = D // 4

    def kernel(scalar_ref, first_in, *refs):
        left_refs = refs[:4]
        parts, refs = unflatten(refs[4:], projections)
        out, weight, first_ref, semaphores = refs
        odd = scalar_ref[1]
        fetches = [begin_weight(parts[i], odd, weight.at[i], semaphores, 2 * i) for i in range(4)]
        fetch_first = begin(first_in, first_ref, semaphores.at[8])

        @pl.loop(0, STEPS)
        def _(step):
            at = block_rows(step)
            total = 0.0
            for index in range(4):

                @pl.when(step == 0)
                def _(index=index):
                    wait(fetches[index])

                total = total + product(left_refs[index][at, :], weight[index, : 3 * width], NN)

            @pl.when(step == 0)
            def _():
                fetch_first.wait()

            first_ref[at, :] = total + first_ref[at, :]
            begin(first_ref.at[at], out.at[at], semaphores.at[9 + step])

        for step in range(STEPS):
            at = block_rows(step)
            pltpu.make_async_copy(first_ref.at[at], out.at[at], semaphores.at[9 + step]).wait()

    return call(
        kernel,
        "input_backward",
        (shaped((L, D), wide),),
        [scalars, first_grad, *qkv_grads, *flat(projections)],
        "h" + "v" * 4 + "h" * len(flat(projections)),
        "h",
        [
            pltpu.VMEM((4, 3 * width + EXTRA, D), low_type),
            pltpu.VMEM((L, D), wide),
            pltpu.SemaphoreType.DMA((9 + STEPS,)),
        ],
        limit=16,
    )[0]


def solution(mesh):
    dp_size = mesh.shape["dp"]
    tensor_size = mesh.shape["tensor"]
    masks = [1, 2, 6] + [1 << bit for bit in range(3, 16)]
    masks = masks[: dp_size.bit_length() - 1]

    def over_tensor(value, mask):
        return lax.ppermute(value, "tensor", [(i, i ^ mask) for i in range(tensor_size)])

    def over_dp(value, mask):
        return lax.ppermute(value, "dp", [(i, i ^ mask) for i in range(dp_size)])

    def body(
        tokens,
        grad_out,
        lengths,
        segment_ids,
        query_weight,
        query_bias,
        key_weight,
        value_weight,
        value_bias,
        mixer_weight,
        mixer_bias,
        first_gain,
        first_shift,
        inner_weight,
        inner_bias,
        outer_weight,
        outer_bias,
        second_gain,
        second_shift,
    ):
        width = query_weight.shape[1]
        place = lax.axis_index("tensor")
        odd = lax.axis_index("dp") % 2
        chain = [jnp.zeros((8, 128), wide)]

        def after(*values):
            held = lax.optimization_barrier((chain[0],) + values)
            return held[1:] if len(values) > 1 else held[1]

        def done(*values):
            chain[0] = lax.optimization_barrier((chain[0],) + values)[0]
            return values if len(values) > 1 else values[0]

        lines = [mixer_bias, first_gain, first_shift, outer_bias, second_gain, second_shift]
        lines = dict(enumerate(lines))
        lines[8] = jnp.pad(query_bias, (0, D - width)) + jnp.pad(
            value_bias, (2 * width, D - 3 * width)
        )
        lines[9] = inner_bias
        line_at = lax.broadcasted_iota(jnp.int32, (16, D), 0)
        vectors = jnp.zeros((16, D), low_type)
        for index, line in lines.items():
            vectors = jnp.where(line_at == index, line[None, :], vectors)
        scalars = jnp.concatenate([jnp.stack([place, odd]).astype(jnp.int32), lengths])

        def hold():
            chain[0] = tick(scalars, chain[0])

        def send(value, mask):
            return over_tensor(after(value), mask)

        def pass_y(value):
            return over_dp(after(value), masks[0])

        def land(value):
            return done(after(value))

        def stage(function, *operands):
            return done(*function(after(scalars), *operands))

        piece, inner_piece, outer_piece, own_heads = done(
            *prepare(
                scalars,
                vectors,
                [query_weight.T, key_weight.T, value_weight.T],
                mixer_weight,
                inner_weight,
                outer_weight,
            )
        )
        heads = {}

        def attend(slot, parts):
            heads[slot] = stage(attend_forward, segment_ids, tokens, parts)

        heads_x = send(piece, 2)
        heads_core = send(own_heads, 1)
        hold()
        attend(0, (own_heads,))
        heads_core = land(heads_core)
        inner_core = send(inner_weight, 1)
        attend(1, (heads_core,))
        inner_core = land(inner_core)
        heads_x = land(heads_x)
        heads_y = pass_y(heads_x)
        inner_x = send(inner_piece, 2)
        heads_near = send(heads_x, 1)
        hold()
        heads_near = land(heads_near)
        outer_core = send(outer_weight, 1)
        hold()
        outer_core = land(outer_core)
        tokens_other = send(tokens, 1)
        hold()
        tokens_other = land(tokens_other)
        heads_y = land(heads_y)
        heads_far = send(heads_y, 1)
        inner_x = land(inner_x)
        inner_y = pass_y(inner_x)
        outer_x = send(outer_piece, 2)
        inner_near = send(inner_x, 1)
        hold()
        attend(2, (heads_x, heads_y))
        heads_far = land(heads_far)
        inner_near = land(inner_near)
        attend(3, (heads_near, heads_far))
        attended = [heads[j][0] for j in range(4)]
        inner_biases = [heads[j][1] for j in range(4)]
        projections = mixers = [
            (own_heads,),
            (heads_core,),
            (heads_x, heads_y),
            (heads_near, heads_far),
        ]
        inverse_one, normed_low, sums_one, hat_one = stage(
            mix_norm, vectors, tokens, attended, mixers
        )
        attended_other = {j: send(attended[j ^ 1], 1) for j in (0, 2)}
        *activated, slope_one = stage(
            inner_forward, normed_low, [(inner_weight,), (inner_core,)], inner_biases[:2]
        )
        attended_other = {j: land(attended_other[j]) for j in (0, 2)}
        outer_x = land(outer_x)
        outer_y = pass_y(outer_x)
        outer_near = send(outer_x, 1)
        inner_y = land(inner_y)
        inner_far = send(inner_y, 1)
        hold()
        normed_other = send(normed_low, 1)
        outer_near = land(outer_near)
        inner_far = land(inner_far)
        *more, slope_two = stage(
            inner_forward,
            normed_low,
            [(inner_x, inner_y), (inner_near, inner_far)],
            inner_biases[2:],
        )
        activated = activated + more
        inners = [(inner_weight,), (inner_core,), (inner_x, inner_y), (inner_near, inner_far)]
        normed_other = land(normed_other)
        activated_other = {j: send(activated[j ^ 1], 1) for j in (0, 2)}
        hold()
        activated_other = {j: land(activated_other[j]) for j in (0, 2)}
        outer_y = land(outer_y)
        outer_far = send(outer_y, 1)
        hold()
        outer_far = land(outer_far)
        outers = [(outer_weight,), (outer_core,), (outer_x, outer_y), (outer_near, outer_far)]
        ffn_low, sums_two, second_grad, layer_out = stage(
            outer_norm, vectors, hat_one, grad_out, activated, outers
        )

        def pair_product(left, right, left_other, right_other):
            left, right, left_other, right_other = after(left, right, left_other, right_other)
            return done(
                (product(left, right, TN) + product(left_other, right_other, TN)).astype(low_type)
            )

        last = len(masks)
        hops = last + 2

        class Reduction:
            def __init__(self, sent, outputs=1):
                self.incoming = send(sent, 2)
                hold()
                self.kept = None
                self.stage = 0
                self.outputs = outputs

            def hop(self):
                kept, incoming = after(self.kept, self.incoming)
                if self.stage == 0:
                    sent, self.kept = stage(split_add, kept, incoming)
                    self.incoming = over_dp(after(sent), masks[0])
                    hold()
                elif self.stage <= last:
                    self.kept = done(add_rows(kept, incoming))
                    mask = masks[self.stage] if self.stage < last else masks[0]
                    self.incoming = over_dp(after(self.kept), mask)
                    hold()
                else:
                    self.result = finish(after(scalars), kept, incoming, self.outputs)
                    done(*self.result)
                self.stage += 1

        class MixedReduction(Reduction):
            def __init__(self, sent, kept, extra):
                super().__init__(done(message(sent, extra)))
                self.kept, self.extra = kept, extra

            def hop(self):
                if self.stage > last:
                    super().hop()
                    return
                kept, extra, incoming = after(self.kept, self.extra, self.incoming)
                text, self.kept, self.extra = stage(
                    mixed_hop, kept, extra, incoming, self.stage == 0
                )
                mask = masks[self.stage] if self.stage < last else masks[0]
                self.incoming = over_dp(after(text), mask)
                hold()
                self.stage += 1

        def outer_part(j):
            return pair_product(activated[j], ffn_low, activated_other[j], ffn_other)

        def inner_part(j):
            return pair_product(normed_low, inner_lows[j], normed_other, inner_other[j])

        def heads_part(j):
            return pair_product(qkv_grads[j], tokens, qkv_other[j], tokens_other)

        def mixer_part(j):
            return pair_product(attended[j], branch_low, attended_other[j], branch_other)

        ffn_other = send(ffn_low, 1)
        *inner_lows, inner_bias_rows = stage(
            inner_backward, ffn_low, [slope_one, slope_two], outers
        )
        ffn_other = land(ffn_other)
        inner_other = {2: send(inner_lows[3], 1), 0: send(inner_lows[1], 1)}
        outer_chain = Reduction(outer_part(2))
        branch_low, sums_three, first_grad = stage(
            first_backward, vectors, hat_one, inverse_one, second_grad, inner_lows, inners
        )
        inner_other = {j: land(inner_other[j]) for j in (2, 0)}
        branch_other = send(branch_low, 1)
        inner_chain = Reduction(inner_part(2))
        qkv_grads, qkv_bias, qkv_other = {}, {}, {}

        def retreat(slot):
            attended_low, _, qkv, probs = heads[slot]
            qkv_grads[slot], qkv_bias[slot] = stage(
                attend_backward, slot, branch_low, mixers[slot], attended_low, qkv, probs
            )

        retreat(3)
        branch_other = land(branch_other)
        qkv_other[2] = send(qkv_grads[3], 1)
        retreat(2)
        qkv_other[2] = land(qkv_other[2])
        heads_chain = Reduction(heads_part(2), 3)
        outer_chain.kept = outer_part(0)
        retreat(1)
        outer_chain.hop()
        qkv_other[0] = send(qkv_grads[1], 1)
        retreat(0)
        qkv_other[0] = land(qkv_other[0])
        small = done(
            jnp.concatenate(
                [
                    sums_one,
                    sums_two,
                    sums_three,
                    inner_bias_rows,
                    qkv_bias[0] + qkv_bias[1] + qkv_bias[2] + qkv_bias[3],
                ]
            )
        )
        small_other = send(small, 1)
        mixer_sent, mixer_kept = mixer_part(2), mixer_part(0)
        small = done(small + after(small_other))
        mixer_chain = MixedReduction(mixer_sent, mixer_kept, small)
        inner_chain.kept = inner_part(0)
        heads_chain.kept = heads_part(0)
        outer_chain.hop()
        tokens_grad = done(
            input_backward(
                after(scalars), first_grad, [qkv_grads[j] for j in range(4)], projections
            )
        )
        chains = [outer_chain, inner_chain, heads_chain, mixer_chain]
        for which in ORDER:
            if chains[which].stage < hops:
                chains[which].hop()
        for chain_left in chains:
            while chain_left.stage < hops:
                chain_left.hop()
        small = mixer_chain.extra

        totals = jnp.sum(jnp.stack([small[0], small[1], small[11]]), axis=1)
        statistics = jnp.sqrt(totals / (small[2, 0] * D))
        own_inner_bias = lax.dynamic_index_in_dim(small[24:28], place, 0, keepdims=False)
        own_qkv_bias = lax.dynamic_index_in_dim(small[32:36], place, 0, keepdims=False)
        query_grad, key_grad, value_grad = heads_chain.result
        return (
            layer_out,
            tokens_grad,
            query_grad.T,
            own_qkv_bias[:width],
            key_grad.T,
            value_grad.T,
            own_qkv_bias[2 * width : 3 * width],
            mixer_chain.result[0],
            small[18],
            small[16],
            small[17],
            inner_chain.result[0],
            own_inner_bias,
            outer_chain.result[0],
            small[10],
            small[8],
            small[9],
            statistics,
        )

    in_specs = (
        P(("dp", "tensor"), None),
        P(("dp", "tensor"), None),
        P("dp"),
        P("dp", None),
        P(None, "tensor"),
        P("tensor"),
        P(None, "tensor"),
        P(None, "tensor"),
        P("tensor"),
        P("tensor", None),
        P(),
        P(),
        P(),
        P(None, "tensor"),
        P("tensor"),
        P("tensor", None),
        P(),
        P(),
        P(),
    )
    out_specs = (
        P(("dp", "tensor"), None),
        P(("dp", "tensor"), None),
        P(None, "tensor"),
        P("tensor"),
        P(None, "tensor"),
        P(None, "tensor"),
        P("tensor"),
        P("tensor", None),
        P(),
        P(),
        P(),
        P(None, "tensor"),
        P("tensor"),
        P("tensor", None),
        P(),
        P(),
        P(),
        P(),
    )
    return jax.shard_map(body, mesh=mesh, in_specs=in_specs, out_specs=out_specs, check_vma=False)
```

```python
import jax
import jax.numpy as jnp
from jax import lax
from jax.experimental import pallas as pl
from jax.experimental.pallas import tpu as pltpu
from jax.sharding import PartitionSpec as P

D = 768
HEAD_DIM = 64
L = 512
EXTRA = 32

eps_norm = 1e-06
root_half = 0.7071067811865476
inv_root_tau = 0.3989422804014327
low_type = jnp.bfloat16
wide = jnp.float32
NN = (((1,), (0,)), ((), ()))
NT = (((1,), (1,)), ((), ()))
TN = (((0,), (0,)), ((), ()))


def product(left, right, dims):
    return lax.dot_general(left, right, dims, preferred_element_type=wide)


def shaped(shape, dtype):
    return jax.ShapeDtypeStruct(shape, dtype)


COST = 100000000000
PRICES = {
    "prepare": 100000000000,
    "attend_forward": 100000000000,
    "mix_norm": 100000000000,
    "inner_forward": 5000000000,
    "middle": 100000000000,
    "attend_backward": 100000000000,
    "input_backward": 1000000000,
    "split_add": 1000000000,
    "mixed_hop": 1000000000,
    "finish": 1000000000,
    "take_halves": 1000000000,
    "add_halves": 1000000000,
    "tick": 100000000000,
}
HOLD_HOPS = False
HOLD_A = False
HOLD_B = False
HOLD_C = False
HOLD_D = False
HOLD_X = False
HOLD_Y = False
HOLD_Z = False
BRANCH_LATE = False
PLAN = (
    "o3", "o2", "i3", "X0", "i1", "i2", "i0", "Y1", "b3", "h3", "b2", "h2",
    "X2", "o1", "o0", "b1", "H0", "h1", "b0", "H1", "m3", "m1", "m2", "m0",
    "S0", "h0", "M3", "H0", "H2", "H1", "H0", "H3", "B0", "H2", "H0", "H1",
    "H3", "H2", "H0", "H1", "H3", "H2", "H0", "H1", "H3", "H2", "H3", "H1",
)


def call(
    kernel, name, out_shape, operands, spaces, out_spaces, scratch=(), limit=14
):
    place = {"v": pltpu.VMEM, "h": pltpu.HBM}
    price = PRICES.get(name, COST)
    out_shape = tuple(
        pltpu.HBM(one.shape, one.dtype) if letter == "h" else one
        for one, letter in zip(out_shape, out_spaces)
    )
    operands = operands[:1] + [
        pltpu.with_memory_space_constraint(one, pltpu.HBM) if letter == "h" else one
        for one, letter in zip(operands[1:], spaces)
    ]
    return pl.pallas_call(
        kernel,
        out_shape=out_shape,
        in_specs=[pl.BlockSpec(memory_space=pltpu.SMEM)]
        + [pl.BlockSpec(memory_space=place[letter]) for letter in spaces],
        out_specs=tuple(pl.BlockSpec(memory_space=place[letter]) for letter in out_spaces),
        scratch_shapes=list(scratch),
        compiler_params=pltpu.CompilerParams(vmem_limit_bytes=limit << 20),
        cost_estimate=pl.CostEstimate(flops=price, transcendentals=0, bytes_accessed=price // 300),
        name=name,
    )(*operands)


def read_scalars(scalar_ref):
    place = scalar_ref[0]
    return place, scalar_ref[1], scalar_ref[2 + place]


def begin(source, target, semaphore):
    copy = pltpu.make_async_copy(source, target, semaphore)
    copy.start()
    return copy


def begin_weight(parts, odd, target, semaphores, at, first=0):
    rows = target.shape[0] // len(parts)
    first = first // len(parts)
    parts = [part.at[pl.ds(first, rows)] for part in parts]
    if len(parts) == 1:
        return [begin(parts[0], target, semaphores.at[at])]
    return [
        begin(
            part,
            target.at[pl.ds(pl.multiple_of(which * rows, rows), rows)],
            semaphores.at[at + index],
        )
        for index, (part, which) in enumerate(zip(parts, (odd, 1 - odd)))
    ]


def wait(copies):
    for copy in copies:
        copy.wait()


def unflatten(refs, slots):
    out, at = [], 0
    for parts in slots:
        out.append(refs[at : at + len(parts)])
        at += len(parts)
    return out, refs[at:]


def flat(slots):
    return [part for parts in slots for part in parts]


WIDTH = D // 4
PROJECTION_ROWS = 3 * WIDTH + EXTRA


def prepare(scalars, vectors, weights, mixer, inner, outer):
    rows = PROJECTION_ROWS + WIDTH

    def kernel(scalar_ref, vector_ref, query, key, value, mixer_in, inner_in, outer_in, *refs):
        inner_out, outer_out, own_out, own_ref, semaphores = refs
        odd = scalar_ref[1]
        fetches = [
            begin(source, own_ref.at[pl.ds(start, WIDTH)], semaphores.at[index])
            for index, (source, start) in enumerate(
                zip((query, key, value, mixer_in), (0, WIDTH, 2 * WIDTH, PROJECTION_ROWS))
            )
        ]
        half = D // 2
        chosen = pl.ds(pl.multiple_of(odd * half, half), half)
        passes = [
            begin(inner_in.at[chosen], inner_out, semaphores.at[4]),
            begin(outer_in.at[chosen], outer_out, semaphores.at[5]),
        ]
        own_ref[3 * WIDTH : PROJECTION_ROWS, :] = jnp.zeros((EXTRA, D), low_type)
        own_ref[3 * WIDTH : 3 * WIDTH + 8, :] = vector_ref[8:16, :]
        wait(fetches)
        copies = [begin(own_ref, own_out, semaphores.at[6])]
        wait(copies + passes)

    return call(
        kernel,
        "prepare",
        (
            shaped((D // 2, D), low_type),
            shaped((D // 2, D), low_type),
            shaped((rows, D), low_type),
        ),
        [scalars, vectors, *weights, mixer, inner, outer],
        "vhhhhhh",
        "vvh",
        [pltpu.VMEM((rows, D), low_type), pltpu.SemaphoreType.DMA((7,))],
    )


def tick(scalars, token):
    def kernel(scalar_ref, token_ref, out_ref):
        out_ref[...] = token_ref[...]

    return call(kernel, "tick", (shaped(token.shape, token.dtype),), [scalars, token], "v", "v")[0]


def add_rows(left, right):
    return (left.astype(wide) + right.astype(wide)).astype(low_type)


def split_add(scalars, own, partner, incoming):
    half = own.shape[0] // 2

    def kernel(scalar_ref, own_ref, partner_ref, incoming_ref, send_ref, keep_ref):
        odd = scalar_ref[1]
        for which, out_ref in ((1 - odd, send_ref), (odd, keep_ref)):
            rows = pl.ds(pl.multiple_of(which * half, 16), half)
            total = own_ref[rows, :].astype(wide) + partner_ref[rows, :].astype(wide)
            out_ref[...] = (total + incoming_ref[rows, :].astype(wide)).astype(low_type)

    return call(
        kernel,
        "split_add",
        (shaped((half, D), low_type),) * 2,
        [scalars, own, partner, incoming],
        "vvv",
        "vv",
    )


def message(rows, extra):
    high = extra.astype(low_type)
    return jnp.concatenate([rows, high, (extra - high.astype(wide)).astype(low_type)], axis=0)


def mixed_hop(scalars, kept, extra, incoming, split):
    rows = kept.shape[0] // 2 if split else kept.shape[0]
    count = extra.shape[0]

    def kernel(scalar_ref, kept_ref, extra_ref, incoming_ref, message_ref, keep_ref, out_ref):
        at = kept.shape[0]
        total = extra_ref[...] + (
            incoming_ref[at : at + count, :].astype(wide)
            + incoming_ref[at + count : at + 2 * count, :].astype(wide)
        )
        out_ref[...] = total
        high = total.astype(low_type)
        message_ref[rows : rows + count, :] = high
        message_ref[rows + count :, :] = (total - high.astype(wide)).astype(low_type)
        if split:
            odd = scalar_ref[1]
            theirs = pl.ds(pl.multiple_of((1 - odd) * rows, 16), rows)
            ours = pl.ds(pl.multiple_of(odd * rows, 16), rows)
            message_ref[:rows, :] = add_rows(kept_ref[theirs, :], incoming_ref[theirs, :])
            keep_ref[...] = add_rows(kept_ref[ours, :], incoming_ref[ours, :])
        else:
            joined = add_rows(kept_ref[...], incoming_ref[:rows, :])
            message_ref[:rows, :] = joined
            keep_ref[...] = joined

    return call(
        kernel,
        "mixed_hop",
        (
            shaped((rows + 2 * count, D), low_type),
            shaped((rows, D), low_type),
            shaped((count, D), wide),
        ),
        [scalars, kept, extra, incoming],
        "vvv",
        "vvv",
    )


def finish(scalars, kept, incoming, outputs):
    half = kept.shape[0]
    rows = 2 * half // outputs

    def kernel(scalar_ref, kept_ref, incoming_ref, *refs):
        outs, joined, semaphores = refs[:outputs], refs[outputs], refs[outputs + 1]
        odd = scalar_ref[1]
        joined[pl.ds(pl.multiple_of(odd * half, 16), half), :] = kept_ref[...].astype(wide)
        joined[pl.ds(pl.multiple_of((1 - odd) * half, 16), half), :] = incoming_ref[
            :half, :
        ].astype(wide)
        wait(
            [
                begin(joined.at[pl.ds(index * rows, rows)], out, semaphores.at[index])
                for index, out in enumerate(outs)
            ]
        )

    return call(
        kernel,
        "finish",
        (shaped((rows, D), wide),) * outputs,
        [scalars, kept, incoming],
        "vv",
        "h" * outputs,
        [pltpu.VMEM((2 * half, D), wide), pltpu.SemaphoreType.DMA((outputs,))],
    )


def attend_forward(scalars, segment_ids, tokens, projection):
    width = D // 4
    heads = width // HEAD_DIM
    block = 256

    def kernel(scalar_ref, segment_ref, tokens_ref, *refs):
        (parts,), refs = unflatten(refs, [projection])
        attended_ref, bias_ref, qkv_out, probs_out, mask, weight, qkv_ref, probs_ref, semaphores = refs
        place, odd, length = read_scalars(scalar_ref)
        fetch = begin_weight(parts, odd, weight, semaphores, 0)
        query_owner = segment_ref[pl.ds(place, 1), :].astype(wide)
        key_owner = jnp.broadcast_to(query_owner, (128, L)).T
        key_at = lax.broadcasted_iota(jnp.int32, (L, 128), 0)
        key_owner = jnp.where(key_at < length, key_owner, -1.0)
        query_at = lax.broadcasted_iota(jnp.int32, (L, 128), 1)
        for start in range(0, L, 128):
            allowed = (key_owner == query_owner[:, start : start + 128]) | (
                key_at == query_at + start
            )
            mask[:, start : start + 128] = jnp.where(allowed, 0.0, -1e30)
        wait(fetch)
        bias_ref[...] = weight[3 * width : 3 * width + 16, :]
        bias = weight[3 * width : 3 * width + 1, : 3 * width].astype(wide)
        qkv_ref[...] = (product(tokens_ref[...], weight[: 3 * width, :], NT) + bias).astype(
            low_type
        )
        qkv_copy = begin(qkv_ref, qkv_out, semaphores.at[2])

        @pl.loop(0, L // block)
        def _(step):
            rows = pl.ds(pl.multiple_of(step * block, block), block)
            for head in range(heads):
                at = head * HEAD_DIM
                queries = qkv_ref[rows, at : at + HEAD_DIM] * jnp.asarray(
                    HEAD_DIM**-0.5, low_type
                )
                key_rows = qkv_ref[:, width + at : width + at + HEAD_DIM]
                values = qkv_ref[:, 2 * width + at : 2 * width + at + HEAD_DIM]
                scores = product(key_rows, queries, NT) + mask[:, rows]
                highest = jnp.max(scores, axis=0, keepdims=True)
                expanded = jnp.exp(scores - highest)
                total = jnp.sum(expanded, axis=0, keepdims=True)
                probs = (expanded * (1.0 / total)).astype(low_type)
                probs_ref[step, head] = probs
                attended_ref[rows, at : at + HEAD_DIM] = product(probs, values, TN).astype(
                    low_type
                )
            begin(probs_ref.at[step], probs_out.at[step], semaphores.at[3 + step])

        qkv_copy.wait()
        for step in range(L // block):
            pltpu.make_async_copy(
                probs_ref.at[step], probs_out.at[step], semaphores.at[3 + step]
            ).wait()

    kept = (L // block, heads, L, block)
    return call(
        kernel,
        "attend_forward",
        (
            shaped((L, width), low_type),
            shaped((16, D), low_type),
            shaped((L, 3 * width), low_type),
            shaped(kept, low_type),
        ),
        [scalars, segment_ids, tokens, *projection],
        "vv" + "h" * len(projection),
        "vvhh",
        [
            pltpu.VMEM((L, L), wide),
            pltpu.VMEM((3 * width + EXTRA, D), low_type),
            pltpu.VMEM((L, 3 * width), low_type),
            pltpu.VMEM(kept, low_type),
            pltpu.SemaphoreType.DMA((3 + L // block,)),
        ],
    )


def attend_backward(scalars, slot, branch_low, mixer, attended, qkv, probs):
    width = D // 4
    heads = width // HEAD_DIM
    block = 256

    def kernel(scalar_ref, branch_ref, attended_ref, qkv_in, probs_in, *refs):
        (parts,), refs = unflatten(refs, [mixer])
        grad_ref, bias_ref, weight, qkv_ref, probs_ref, outgoing, sums, dots, semaphores = refs
        fetch = begin_weight(parts, scalar_ref[1], weight, semaphores, 0, PROJECTION_ROWS)
        fetch_rest = [
            begin(qkv_in, qkv_ref, semaphores.at[2]),
            begin(probs_in, probs_ref, semaphores.at[3]),
        ]
        wait(fetch)
        attended_grad = product(branch_ref[...], weight[...], NT).astype(low_type)
        outgoing[...] = attended_grad
        along = (attended_ref[...].astype(wide) * attended_grad.astype(wide)).T
        for head in range(heads):
            dots[head : head + 1, :] = jnp.sum(
                along[head * HEAD_DIM : (head + 1) * HEAD_DIM], axis=0, keepdims=True
            )
            sums[head] = jnp.zeros((L, HEAD_DIM), wide)
        wait(fetch_rest)

        @pl.loop(0, L // block)
        def _(step):
            rows = pl.ds(pl.multiple_of(step * block, block), block)
            for head in range(heads):
                at = head * HEAD_DIM
                queries = qkv_ref[:, at : at + HEAD_DIM] * jnp.asarray(HEAD_DIM**-0.5, low_type)
                key_rows = qkv_ref[rows, width + at : width + at + HEAD_DIM]
                values = qkv_ref[rows, 2 * width + at : 2 * width + at + HEAD_DIM]
                grad = outgoing[:, at : at + HEAD_DIM]
                probs = jnp.concatenate(
                    [probs_ref[part, head, rows, :] for part in range(L // block)], axis=1
                )
                probs_grad = product(values, grad, NT)
                scores_grad = (
                    probs.astype(wide) * (probs_grad - dots[head : head + 1, :])
                ).astype(low_type)
                grad_ref[rows, width + at : width + at + HEAD_DIM] = product(
                    scores_grad, queries, NN
                ).astype(low_type)
                grad_ref[rows, 2 * width + at : 2 * width + at + HEAD_DIM] = product(
                    probs, grad, NN
                ).astype(low_type)
                sums[head] += product(scores_grad, key_rows, TN)

        for head in range(heads):
            at = head * HEAD_DIM
            grad_ref[:, at : at + HEAD_DIM] = (sums[head] * (HEAD_DIM**-0.5)).astype(low_type)
        bias_ref[...] = jnp.zeros((8, D), wide)
        quarter = scalar_ref[0] ^ slot
        bias_ref[pl.ds(quarter, 1), : 3 * width] = jnp.sum(
            grad_ref[...].astype(wide), axis=0, keepdims=True
        )

    return call(
        kernel,
        "attend_backward",
        (shaped((L, 3 * width), low_type), shaped((8, D), wide)),
        [scalars, branch_low, attended, qkv, probs, *mixer],
        "vvhh" + "h" * len(mixer),
        "vv",
        [
            pltpu.VMEM((width, D), low_type),
            pltpu.VMEM((L, 3 * width), low_type),
            pltpu.VMEM(probs.shape, low_type),
            pltpu.VMEM((L, width), low_type),
            pltpu.VMEM((heads, L, HEAD_DIM), wide),
            pltpu.VMEM((8, L), wide),
            pltpu.SemaphoreType.DMA((4,)),
        ],
    )


def normalize(rows):
    center = rows - jnp.mean(rows, axis=-1, keepdims=True)
    inverse = lax.rsqrt(jnp.mean(center * center, axis=-1, keepdims=True) + eps_norm)
    return center * inverse, inverse


def normalize_backward(scaled, normed, inverse):
    middle = jnp.mean(scaled, axis=-1, keepdims=True)
    along = jnp.mean(scaled * normed, axis=-1, keepdims=True)
    return inverse * (scaled - middle - normed * along)


def column_sum(rows):
    return jnp.sum(rows, axis=0, keepdims=True)


BLOCK = 256
STEPS = L // BLOCK


def block_rows(step):
    return pl.ds(pl.multiple_of(step * BLOCK, BLOCK), BLOCK)


def mix_norm(scalars, vectors, tokens, attended, mixers):
    width = D // 4

    def kernel(scalar_ref, vector_ref, tokens_ref, *refs):
        attended_refs = refs[:4]
        parts, refs = unflatten(refs[4:], mixers)
        inverse_ref, low_ref, sums_ref, hat_out, weight, hat_ref, semaphores = refs
        _, odd, length = read_scalars(scalar_ref)
        fetches = [
            begin_weight(
                parts[i], odd, weight.at[pl.ds(i * width, width)], semaphores, 2 * i, PROJECTION_ROWS
            )
            for i in range(4)
        ]
        vectors = vector_ref[...].astype(wide)
        sums_ref[...] = jnp.zeros((8, D), wide)
        for fetch in fetches:
            wait(fetch)

        @pl.loop(0, STEPS)
        def _(step):
            at = block_rows(step)
            branch = vectors[0:1]
            for index in range(4):
                branch = branch + product(
                    attended_refs[index][at, :], weight[index * width : (index + 1) * width], NN
                )
            rows = tokens_ref[at, :].astype(wide)
            hat, inverse = normalize(rows + branch)
            hat_ref[at, :] = hat
            begin(hat_ref.at[at], hat_out.at[at], semaphores.at[8 + step])
            inverse_ref[at, :] = inverse
            low_ref[at, :] = (hat * vectors[1:2] + vectors[2:3]).astype(low_type)
            place = lax.broadcasted_iota(jnp.int32, (BLOCK, 1), 0) + step * BLOCK
            valid = (place < length).astype(wide)
            sums_ref[0:1, :] += column_sum(valid * rows * rows)
            sums_ref[1:2, :] += column_sum(valid * branch * branch)
            sums_ref[2:3, :] += column_sum(jnp.broadcast_to(valid, (BLOCK, D)))

        for step in range(STEPS):
            at = block_rows(step)
            pltpu.make_async_copy(hat_ref.at[at], hat_out.at[at], semaphores.at[8 + step]).wait()

    return call(
        kernel,
        "mix_norm",
        (shaped((L, 1), wide), shaped((L, D), low_type), shaped((8, D), wide), shaped((L, D), wide)),
        [scalars, vectors, tokens, *attended, *flat(mixers)],
        "vv" + "v" * 4 + "h" * len(flat(mixers)),
        "vvvh",
        [
            pltpu.VMEM((D, D), low_type),
            pltpu.VMEM((L, D), wide),
            pltpu.SemaphoreType.DMA((8 + STEPS,)),
        ],
    )


def inner_forward(scalars, normed_low, weights, biases):
    chunk = 256

    def kernel(scalar_ref, normed_ref, *refs):
        bias_refs = refs[:2]
        parts, refs = unflatten(refs[2:], weights)
        out_refs, slope_out, weight, bias, slope_ref, semaphores = refs[:2], *refs[2:]
        odd = scalar_ref[1]
        fetches = [begin_weight(parts[i], odd, weight.at[i], semaphores, 2 * i) for i in range(2)]
        for index in range(2):
            bias[index] = bias_refs[index][...].astype(wide)

        @pl.loop(0, 2)
        def _(slot):
            for index in range(2):

                @pl.when(slot == index)
                def _(index=index):
                    wait(fetches[index])

            @pl.loop(0, D // chunk)
            def _(step):
                columns = pl.ds(pl.multiple_of(step * chunk, chunk), chunk)
                inner_pre = (
                    product(normed_ref[...], weight[slot, :, columns], NN)
                    + bias[slot, 1:2, columns]
                )
                below = 0.5 * (1.0 + lax.erf(inner_pre * root_half))
                density = jnp.exp(-0.5 * inner_pre * inner_pre) * inv_root_tau
                activated = (inner_pre * below).astype(low_type)
                slope_ref[slot, :, columns] = (below + inner_pre * density).astype(low_type)
                for index in range(2):

                    @pl.when(slot == index)
                    def _(index=index):
                        out_refs[index][:, columns] = activated

            begin(slope_ref.at[slot], slope_out.at[slot], semaphores.at[4 + slot])

        for slot in range(2):
            pltpu.make_async_copy(
                slope_ref.at[slot], slope_out.at[slot], semaphores.at[4 + slot]
            ).wait()

    return call(
        kernel,
        "inner_forward",
        (shaped((L, D), low_type),) * 2 + (shaped((2, L, D), low_type),),
        [scalars, normed_low, *biases, *flat(weights)],
        "vvv" + "h" * len(flat(weights)),
        "vvh",
        [
            pltpu.VMEM((2, D, D), low_type),
            pltpu.VMEM((2, 16, D), wide),
            pltpu.VMEM((2, L, D), low_type),
            pltpu.SemaphoreType.DMA((6,)),
        ],
    )


def middle(
    scalars, vectors, hat_one, inverse_one, grad_out, activated, slopes, outers, inners
):
    chunk = 256

    def kernel(scalar_ref, vector_ref, hat_in, inverse_ref, incoming_in, *refs):
        left_refs, slope_in = refs[:4], refs[4:6]
        outer_parts, refs = unflatten(refs[6:], outers)
        inner_parts, refs = unflatten(refs, inners)
        low_ref, branch_ref, bias_ref, sums_ref = refs[:4]
        inner_refs, grad_out_ref, result_out = refs[4:8], refs[8], refs[9]
        outer, inner, slope_ref, hat_ref, incoming_ref, second_ref, grad_ref, result_ref = refs[10:18]
        semaphores = refs[18]
        place, odd, length = read_scalars(scalar_ref)
        fetch_outer = [
            begin_weight(outer_parts[i], odd, outer.at[i], semaphores, 2 * i) for i in range(4)
        ]
        fetch_rest = [
            begin(hat_in, hat_ref, semaphores.at[8]),
            begin(incoming_in, incoming_ref, semaphores.at[9]),
        ]
        fetch_slope = [
            begin(slope_in[i // 2].at[i % 2], slope_ref.at[i], semaphores.at[10 + i])
            for i in range(4)
        ]
        fetch_inner = [
            begin_weight(inner_parts[i], odd, inner.at[i], semaphores, 14 + 2 * i)
            for i in range(4)
        ]
        vectors = vector_ref[...].astype(wide)
        sums_ref[...] = jnp.zeros((16, D), wide)
        bias_ref[...] = jnp.zeros((8, D), wide)

        def result_copy(step):
            at = block_rows(step)
            return pltpu.make_async_copy(
                result_ref.at[at], result_out.at[at], semaphores.at[22 + step]
            )

        def grad_copy(step):
            at = block_rows(step)
            return pltpu.make_async_copy(
                grad_ref.at[at], grad_out_ref.at[at], semaphores.at[22 + STEPS + step]
            )

        @pl.loop(0, STEPS)
        def _(step):
            at = block_rows(step)
            branch = vectors[3:4]
            for index in range(4):

                @pl.when(step == 0)
                def _(index=index):
                    wait(fetch_outer[index])

                branch = branch + product(left_refs[index][at, :], outer[index], NN)

            @pl.when(step == 0)
            def _():
                wait(fetch_rest)

            normed_one = hat_ref[at, :] * vectors[1:2] + vectors[2:3]
            hat, inverse = normalize(normed_one + branch)
            result_ref[at, :] = (hat * vectors[4:5] + vectors[5:6]).astype(low_type)
            result_copy(step).start()
            incoming = incoming_ref[at, :].astype(wide)
            grad = normalize_backward(incoming * vectors[4:5], hat, inverse)
            second_ref[at, :] = grad
            low_ref[at, :] = grad.astype(low_type)
            row = lax.broadcasted_iota(jnp.int32, (BLOCK, 1), 0) + step * BLOCK
            valid = (row < length).astype(wide)
            sums_ref[0:1, :] += column_sum(incoming * hat)
            sums_ref[1:2, :] += column_sum(incoming)
            sums_ref[2:3, :] += column_sum(grad)
            sums_ref[3:4, :] += column_sum(valid * branch * branch)

        @pl.loop(0, 4)
        def _(slot):
            for index in range(4):

                @pl.when(slot == index)
                def _(index=index):
                    fetch_slope[index].wait()

            @pl.loop(0, D // chunk)
            def _(step):
                columns = pl.ds(pl.multiple_of(step * chunk, chunk), chunk)
                grad = product(low_ref[...], outer[slot, columns, :], NT) * slope_ref[
                    slot, :, columns
                ].astype(wide)
                bias_ref[pl.ds(place ^ slot, 1), columns] = column_sum(grad)
                low = grad.astype(low_type)
                for index in range(4):

                    @pl.when(slot == index)
                    def _(index=index):
                        inner_refs[index][:, columns] = low

        for fetch in fetch_inner:
            wait(fetch)

        @pl.loop(0, STEPS)
        def _(step):
            at = block_rows(step)
            total = second_ref[at, :]
            for index in range(4):
                total = total + product(inner_refs[index][at, :], inner[index], NT)
            hat = hat_ref[at, :]
            grad = normalize_backward(total * vectors[1:2], hat, inverse_ref[at, :])
            grad_ref[at, :] = grad
            grad_copy(step).start()
            branch_ref[at, :] = grad.astype(low_type)
            sums_ref[8:9, :] += column_sum(total * hat)
            sums_ref[9:10, :] += column_sum(total)
            sums_ref[10:11, :] += column_sum(grad)

        for step in range(STEPS):
            result_copy(step).wait()
            grad_copy(step).wait()

    return call(
        kernel,
        "middle",
        (
            shaped((L, D), low_type),
            shaped((L, D), low_type),
            shaped((8, D), wide),
            shaped((16, D), wide),
        )
        + (shaped((L, D), low_type),) * 4
        + (shaped((L, D), wide), shaped((L, D), low_type)),
        [
            scalars,
            vectors,
            hat_one,
            inverse_one,
            grad_out,
            *activated,
            *slopes,
            *flat(outers),
            *flat(inners),
        ],
        "vhvh" + "vvvv" + "hh" + "h" * len(flat(outers) + flat(inners)),
        "vvvv" + "vvvv" + "hh",
        [
            pltpu.VMEM((4, D, D), low_type),
            pltpu.VMEM((4, D, D), low_type),
            pltpu.VMEM((4, L, D), low_type),
            pltpu.VMEM((L, D), wide),
            pltpu.VMEM((L, D), low_type),
            pltpu.VMEM((L, D), wide),
            pltpu.VMEM((L, D), wide),
            pltpu.VMEM((L, D), low_type),
            pltpu.SemaphoreType.DMA((22 + 2 * STEPS,)),
        ],
        limit=32,
    )


def take_halves(scalars, near, near_partner, far, far_partner):
    half = near.shape[0] // 2

    def kernel(scalar_ref, near_ref, near_other, far_ref, far_other, send_ref, near_out, far_out):
        odd = scalar_ref[1]
        theirs = pl.ds(pl.multiple_of((1 - odd) * half, 16), half)
        ours = pl.ds(pl.multiple_of(odd * half, 16), half)
        send_ref[:half, :] = add_rows(near_ref[theirs, :], near_other[theirs, :])
        send_ref[half:, :] = add_rows(far_ref[theirs, :], far_other[theirs, :])
        near_out[...] = add_rows(near_ref[ours, :], near_other[ours, :])
        far_out[...] = add_rows(far_ref[ours, :], far_other[ours, :])

    return call(
        kernel,
        "take_halves",
        (shaped((2 * half, D), low_type),) + (shaped((half, D), low_type),) * 2,
        [scalars, near, near_partner, far, far_partner],
        "vvvv",
        "vvv",
    )


def add_halves(scalars, near, far, incoming):
    half = near.shape[0]

    def kernel(scalar_ref, near_ref, far_ref, incoming_ref, near_out, far_out):
        near_out[...] = add_rows(near_ref[...], incoming_ref[:half, :])
        far_out[...] = add_rows(far_ref[...], incoming_ref[half:, :])

    return call(
        kernel,
        "add_halves",
        (shaped((half, D), low_type),) * 2,
        [scalars, near, far, incoming],
        "vvv",
        "vv",
    )


def input_backward(scalars, first_grad, qkv_grads, projections):
    width = D // 4

    def kernel(scalar_ref, first_in, *refs):
        left_refs = refs[:4]
        parts, refs = unflatten(refs[4:], projections)
        out, weight, first_ref, semaphores = refs
        odd = scalar_ref[1]
        fetches = [begin_weight(parts[i], odd, weight.at[i], semaphores, 2 * i) for i in range(4)]
        fetch_first = begin(first_in, first_ref, semaphores.at[8])

        @pl.loop(0, STEPS)
        def _(step):
            at = block_rows(step)
            total = 0.0
            for index in range(4):

                @pl.when(step == 0)
                def _(index=index):
                    wait(fetches[index])

                total = total + product(left_refs[index][at, :], weight[index, : 3 * width], NN)

            @pl.when(step == 0)
            def _():
                fetch_first.wait()

            first_ref[at, :] = total + first_ref[at, :]
            begin(first_ref.at[at], out.at[at], semaphores.at[9 + step])

        for step in range(STEPS):
            at = block_rows(step)
            pltpu.make_async_copy(first_ref.at[at], out.at[at], semaphores.at[9 + step]).wait()

    return call(
        kernel,
        "input_backward",
        (shaped((L, D), wide),),
        [scalars, first_grad, *qkv_grads, *flat(projections)],
        "h" + "v" * 4 + "h" * len(flat(projections)),
        "h",
        [
            pltpu.VMEM((4, 3 * width + EXTRA, D), low_type),
            pltpu.VMEM((L, D), wide),
            pltpu.SemaphoreType.DMA((9 + STEPS,)),
        ],
        limit=16,
    )[0]


def solution(mesh):
    dp_size = mesh.shape["dp"]
    tensor_size = mesh.shape["tensor"]
    masks = [1, 2, 6] + [1 << bit for bit in range(3, 16)]
    masks = masks[: dp_size.bit_length() - 1]

    def over_tensor(value, mask):
        return lax.ppermute(value, "tensor", [(i, i ^ mask) for i in range(tensor_size)])

    def over_dp(value, mask):
        return lax.ppermute(value, "dp", [(i, i ^ mask) for i in range(dp_size)])

    def body(
        tokens,
        grad_out,
        lengths,
        segment_ids,
        query_weight,
        query_bias,
        key_weight,
        value_weight,
        value_bias,
        mixer_weight,
        mixer_bias,
        first_gain,
        first_shift,
        inner_weight,
        inner_bias,
        outer_weight,
        outer_bias,
        second_gain,
        second_shift,
    ):
        width = query_weight.shape[1]
        place = lax.axis_index("tensor")
        odd = lax.axis_index("dp") % 2
        chain = [jnp.zeros((8, 128), wide)]

        def after(*values):
            held = lax.optimization_barrier((chain[0],) + values)
            return held[1:] if len(values) > 1 else held[1]

        def done(*values):
            chain[0] = lax.optimization_barrier((chain[0],) + values)[0]
            return values if len(values) > 1 else values[0]

        lines = [mixer_bias, first_gain, first_shift, outer_bias, second_gain, second_shift]
        lines = dict(enumerate(lines))
        lines[8] = jnp.pad(query_bias, (0, D - width)) + jnp.pad(
            value_bias, (2 * width, D - 3 * width)
        )
        lines[9] = inner_bias
        line_at = lax.broadcasted_iota(jnp.int32, (16, D), 0)
        vectors = jnp.zeros((16, D), low_type)
        for index, line in lines.items():
            vectors = jnp.where(line_at == index, line[None, :], vectors)
        scalars = jnp.concatenate([jnp.stack([place, odd]).astype(jnp.int32), lengths])

        def hold():
            chain[0] = tick(scalars, chain[0])

        def send(value, mask):
            return over_tensor(after(value), mask)

        def pass_y(value):
            return over_dp(after(value), masks[0])

        def land(value):
            return done(after(value))

        def stage(function, *operands):
            return done(*function(after(scalars), *operands))

        inner_piece, outer_piece, own_heads = done(
            *prepare(
                scalars,
                vectors,
                [query_weight.T, key_weight.T, value_weight.T],
                mixer_weight,
                inner_weight,
                outer_weight,
            )
        )
        heads = {}

        def attend(slot, parts):
            heads[slot] = stage(attend_forward, segment_ids, tokens, parts)

        heads_x = send(own_heads, 2)
        heads_core = send(own_heads, 1)
        hold()
        attend(0, (own_heads,))
        heads_core = land(heads_core)
        inner_core = send(inner_weight, 1)
        attend(1, (heads_core,))
        inner_core = land(inner_core)
        outer_core = send(outer_weight, 1)
        hold()
        heads_x = land(heads_x)
        inner_x = send(inner_piece, 2)
        heads_near = send(heads_x, 1)
        outer_core = land(outer_core)
        if HOLD_A:
            hold()
        attend(2, (heads_x,))
        heads_near = land(heads_near)
        attend(3, (heads_near,))
        inner_x = land(inner_x)
        inner_y = pass_y(inner_x)
        outer_x = send(outer_piece, 2)
        inner_near = send(inner_x, 1)
        if HOLD_B:
            hold()
        attended = [heads[j][0] for j in range(4)]
        inner_biases = [heads[j][1] for j in range(4)]
        projections = mixers = [(own_heads,), (heads_core,), (heads_x,), (heads_near,)]
        inverse_one, normed_low, sums_one, hat_one = stage(
            mix_norm, vectors, tokens, attended, mixers
        )
        inner_near = land(inner_near)
        *activated, slope_one = stage(
            inner_forward, normed_low, [(inner_weight,), (inner_core,)], inner_biases[:2]
        )
        outer_x = land(outer_x)
        outer_y = pass_y(outer_x)
        outer_near = send(outer_x, 1)
        if HOLD_C:
            hold()
        inner_y = land(inner_y)
        inner_far = send(inner_y, 1)
        if HOLD_D:
            hold()
        outer_near = land(outer_near)
        inner_far = land(inner_far)
        *more, slope_two = stage(
            inner_forward,
            normed_low,
            [(inner_x, inner_y), (inner_near, inner_far)],
            inner_biases[2:],
        )
        activated = activated + more
        inners = [(inner_weight,), (inner_core,), (inner_x, inner_y), (inner_near, inner_far)]
        outer_y = land(outer_y)
        outer_far = send(outer_y, 1)
        hold()
        outer_far = land(outer_far)
        outers = [(outer_weight,), (outer_core,), (outer_x, outer_y), (outer_near, outer_far)]
        ffn_low, branch_low, inner_bias_rows, sums_two, *rest = stage(
            middle,
            vectors,
            hat_one,
            inverse_one,
            grad_out,
            activated,
            [slope_one, slope_two],
            outers,
            inners,
        )
        *inner_lows, first_grad, layer_out = rest

        def part(left, right):
            left, right = after(left, right)
            return done(product(left, right, TN).astype(low_type))

        def add_low(left, right):
            return done(add_rows(*after(left, right)))

        last = len(masks)
        hops = last + 2

        class Reduction:
            def __init__(self, sent, outputs=1):
                self.incoming = send(sent, 2)
                if HOLD_X:
                    hold()
                self.stage = 0
                self.outputs = outputs

            def hop(self):
                if self.stage == 0:
                    own, partner, incoming = after(self.own, self.partner, self.incoming)
                    sent, self.kept = stage(split_add, own, partner, incoming)
                    self.incoming = over_dp(after(sent), masks[0])
                    if HOLD_HOPS:
                        hold()
                elif self.stage <= last:
                    kept, incoming = after(self.kept, self.incoming)
                    self.kept = done(add_rows(kept, incoming))
                    mask = masks[self.stage] if self.stage < last else masks[0]
                    self.incoming = over_dp(after(self.kept), mask)
                    if HOLD_HOPS:
                        hold()
                else:
                    kept, incoming = after(self.kept, self.incoming)
                    self.result = finish(after(scalars), kept, incoming, self.outputs)
                    done(*self.result)
                self.stage += 1

        class MixedReduction(Reduction):
            def __init__(self, sent, kept, extra):
                super().__init__(done(message(sent, extra)))
                self.kept, self.extra = kept, extra

            def hop(self):
                if self.stage > last:
                    super().hop()
                    return
                kept, extra, incoming = after(self.kept, self.extra, self.incoming)
                text, self.kept, self.extra = stage(
                    mixed_hop, kept, extra, incoming, self.stage == 0
                )
                mask = masks[self.stage] if self.stage < last else masks[0]
                self.incoming = over_dp(after(text), mask)
                if HOLD_HOPS:
                    hold()
                self.stage += 1

        class CrossReduction(Reduction):
            def __init__(self, near, near_partner, far, far_partner, outputs=1):
                sent, self.near, self.far = stage(
                    take_halves, *after(near, near_partner, far, far_partner)
                )
                self.incoming = over_dp(after(sent), masks[0])
                if HOLD_Y:
                    hold()
                self.stage = 0
                self.outputs = outputs

            def hop(self):
                if self.stage == 0:
                    near, far, incoming = after(self.near, self.far, self.incoming)
                    self.kept, far = stage(add_halves, near, far, incoming)
                    self.incoming = send(far, 2)
                    if HOLD_Z:
                        hold()
                    self.stage = 1
                else:
                    super().hop()

        partner = {}
        outer_parts, inner_parts, heads_parts = {}, {}, {}
        qkv_grads, qkv_bias = {}, {}

        def retreat(slot):
            attended_low, _, qkv, probs = heads[slot]
            qkv_grads[slot], qkv_bias[slot] = stage(
                attend_backward, slot, branch_low, mixers[slot], attended_low, qkv, probs
            )

        def split_step(name, slot):
            left, right = {
                "o": (activated[slot], ffn_low),
                "i": (normed_low, inner_lows[slot]),
                "m": (attended[slot], branch_low),
                "h": (qkv_grads.get(slot), tokens),
            }[name]
            share = part(left, right)
            if slot % 2:
                partner[name, slot - 1] = send(share, 1)
            else:
                own_share[name, slot] = share

        def own_sum(name, slot):
            return add_low(own_share[name, slot], partner[name, slot])

        own_share, chains = {}, {}
        for step in PLAN:
            name, slot = step[0], int(step[1])
            if name == "b":
                retreat(slot)
            elif name in "oimh":
                split_step(name, slot)
            elif name == "X":
                which = ("o", None, "h")[slot]
                chains[slot] = Reduction(own_sum(which, 2), 3 if slot == 2 else 1)
            elif name == "Y":
                chains[1] = CrossReduction(
                    own_share["i", 0], partner["i", 0], own_share["i", 2], partner["i", 2]
                )
            elif name == "S":
                small = done(
                    jnp.concatenate(
                        [
                            sums_one,
                            sums_two,
                            inner_bias_rows,
                            qkv_bias[0] + qkv_bias[1] + qkv_bias[2] + qkv_bias[3],
                        ]
                    )
                )
                small_other = send(small, 1)
            elif name == "M":
                small = done(small + after(small_other))
                chains[3] = MixedReduction(own_sum("m", 2), own_sum("m", 0), small)
            elif name == "B":
                tokens_grad = done(
                    input_backward(
                        after(scalars), first_grad, [qkv_grads[j] for j in range(4)], projections
                    )
                )
            else:
                chain_now = chains[slot]
                if chain_now.stage == 0 and slot in (0, 2):
                    which = "o" if slot == 0 else "h"
                    chain_now.own, chain_now.partner = own_share[which, 0], partner[which, 0]
                if chain_now.stage < hops:
                    chain_now.hop()
        for chain_left in chains.values():
            while chain_left.stage < hops:
                chain_left.hop()
        small = chains[3].extra
        outer_chain, inner_chain, heads_chain, mixer_chain = (chains[j] for j in range(4))

        totals = jnp.sum(jnp.stack([small[0], small[1], small[11]]), axis=1)
        statistics = jnp.sqrt(totals / (small[2, 0] * D))
        own_inner_bias = lax.dynamic_index_in_dim(small[24:28], place, 0, keepdims=False)
        own_qkv_bias = lax.dynamic_index_in_dim(small[32:36], place, 0, keepdims=False)
        query_grad, key_grad, value_grad = heads_chain.result
        return (
            layer_out,
            tokens_grad,
            query_grad.T,
            own_qkv_bias[:width],
            key_grad.T,
            value_grad.T,
            own_qkv_bias[2 * width : 3 * width],
            mixer_chain.result[0],
            small[18],
            small[16],
            small[17],
            inner_chain.result[0],
            own_inner_bias,
            outer_chain.result[0],
            small[10],
            small[8],
            small[9],
            statistics,
        )

    in_specs = (
        P(("dp", "tensor"), None),
        P(("dp", "tensor"), None),
        P("dp"),
        P("dp", None),
        P(None, "tensor"),
        P("tensor"),
        P(None, "tensor"),
        P(None, "tensor"),
        P("tensor"),
        P("tensor", None),
        P(),
        P(),
        P(),
        P(None, "tensor"),
        P("tensor"),
        P("tensor", None),
        P(),
        P(),
        P(),
    )
    out_specs = (
        P(("dp", "tensor"), None),
        P(("dp", "tensor"), None),
        P(None, "tensor"),
        P("tensor"),
        P(None, "tensor"),
        P(None, "tensor"),
        P("tensor"),
        P("tensor", None),
        P(),
        P(),
        P(),
        P(None, "tensor"),
        P("tensor"),
        P("tensor", None),
        P(),
        P(),
        P(),
        P(),
    )
    return jax.shard_map(body, mesh=mesh, in_specs=in_specs, out_specs=out_specs, check_vma=False)
```

```python
import jax
import jax.numpy as jnp
from jax import lax
from jax.experimental import pallas as pl
from jax.experimental.pallas import tpu as pltpu
from jax.sharding import PartitionSpec as P

D = 768
HEAD_DIM = 64
L = 512
EXTRA = 32

eps_norm = 1e-06
root_half = 0.7071067811865476
inv_root_tau = 0.3989422804014327
low_type = jnp.bfloat16
wide = jnp.float32
NN = (((1,), (0,)), ((), ()))
NT = (((1,), (1,)), ((), ()))
TN = (((0,), (0,)), ((), ()))


def product(left, right, dims):
    return lax.dot_general(left, right, dims, preferred_element_type=wide)


def shaped(shape, dtype):
    return jax.ShapeDtypeStruct(shape, dtype)


COST = 100000000000
PRICES = {
    "prepare": 100000000000,
    "attend_forward": 100000000000,
    "mix_norm": 100000000000,
    "inner_forward": 5000000000,
    "middle": 100000000000,
    "attend_backward": 100000000000,
    "input_backward": 0,
    "split_add": 0,
    "mixed_hop": 0,
    "finish": 0,
    "take_halves": 0,
    "add_halves": 0,
    "join": 0,
    "tick": 100000000000,
}
HOLD_HOPS = False
HOLD_A = False
HOLD_B = False
HOLD_C = False
HOLD_D = False
HOLD_X = False
HOLD_Y = False
HOLD_Z = False
BRANCH_LATE = False
PLAN = (
    "o3", "o2", "i3", "X0", "i1", "i2", "i0", "Y1", "b3", "h3", "b2", "h2",
    "X2", "o1", "o0", "b1", "H0", "h1", "b0", "H1", "m3", "m1", "m2", "m0",
    "S0", "h0", "M3", "H0", "H2", "H1", "H0", "H3", "H2", "H0", "H1", "B0",
    "H3", "H2", "H0", "H1", "H3", "H2", "H0", "H1", "H3", "H2", "H1", "H3",
    "H2", "H0", "H1",
)


def call(
    kernel, name, out_shape, operands, spaces, out_spaces, scratch=(), limit=14
):
    place = {"v": pltpu.VMEM, "h": pltpu.HBM}
    price = PRICES.get(name, COST)
    out_shape = tuple(
        pltpu.HBM(one.shape, one.dtype) if letter == "h" else one
        for one, letter in zip(out_shape, out_spaces)
    )
    operands = operands[:1] + [
        pltpu.with_memory_space_constraint(one, pltpu.HBM) if letter == "h" else one
        for one, letter in zip(operands[1:], spaces)
    ]
    return pl.pallas_call(
        kernel,
        out_shape=out_shape,
        in_specs=[pl.BlockSpec(memory_space=pltpu.SMEM)]
        + [pl.BlockSpec(memory_space=place[letter]) for letter in spaces],
        out_specs=tuple(pl.BlockSpec(memory_space=place[letter]) for letter in out_spaces),
        scratch_shapes=list(scratch),
        compiler_params=pltpu.CompilerParams(vmem_limit_bytes=limit << 20),
        cost_estimate=pl.CostEstimate(flops=price, transcendentals=0, bytes_accessed=price // 300),
        name=name,
    )(*operands)


def read_scalars(scalar_ref):
    place = scalar_ref[0]
    return place, scalar_ref[1], scalar_ref[3 + place]


def begin(source, target, semaphore):
    copy = pltpu.make_async_copy(source, target, semaphore)
    copy.start()
    return copy


def begin_weight(parts, odd, target, semaphores, at, first=0):
    rows = target.shape[0] // len(parts)
    first = first // len(parts)
    parts = [part.at[pl.ds(first, rows)] for part in parts]
    if len(parts) == 1:
        return [begin(parts[0], target, semaphores.at[at])]
    return [
        begin(
            part,
            target.at[pl.ds(pl.multiple_of(which * rows, rows), rows)],
            semaphores.at[at + index],
        )
        for index, (part, which) in enumerate(zip(parts, (odd, 1 - odd)))
    ]


def wait(copies):
    for copy in copies:
        copy.wait()


def unflatten(refs, slots):
    out, at = [], 0
    for parts in slots:
        out.append(refs[at : at + len(parts)])
        at += len(parts)
    return out, refs[at:]


def flat(slots):
    return [part for parts in slots for part in parts]


WIDTH = D // 4
PROJECTION_ROWS = 3 * WIDTH + EXTRA


def prepare(scalars, vectors, weights, mixer, inner, outer):
    rows = PROJECTION_ROWS + WIDTH

    def kernel(scalar_ref, vector_ref, query, key, value, mixer_in, inner_in, outer_in, *refs):
        inner_out, outer_out, own_out, own_ref, semaphores = refs
        odd = scalar_ref[1]
        fetches = [
            begin(source, own_ref.at[pl.ds(start, WIDTH)], semaphores.at[index])
            for index, (source, start) in enumerate(
                zip((query, key, value, mixer_in), (0, WIDTH, 2 * WIDTH, PROJECTION_ROWS))
            )
        ]
        half = D // 2
        chosen = pl.ds(pl.multiple_of(odd * half, half), half)
        passes = [
            begin(inner_in.at[chosen], inner_out, semaphores.at[4]),
            begin(outer_in.at[chosen], outer_out, semaphores.at[5]),
        ]
        own_ref[3 * WIDTH : PROJECTION_ROWS, :] = jnp.zeros((EXTRA, D), low_type)
        own_ref[3 * WIDTH : 3 * WIDTH + 8, :] = vector_ref[8:16, :]
        wait(fetches)
        copies = [begin(own_ref, own_out, semaphores.at[6])]
        wait(copies + passes)

    return call(
        kernel,
        "prepare",
        (
            shaped((D // 2, D), low_type),
            shaped((D // 2, D), low_type),
            shaped((rows, D), low_type),
        ),
        [scalars, vectors, *weights, mixer, inner, outer],
        "vhhhhhh",
        "vvh",
        [pltpu.VMEM((rows, D), low_type), pltpu.SemaphoreType.DMA((7,))],
    )


def tick(scalars, token):
    def kernel(scalar_ref, token_ref, out_ref):
        out_ref[...] = token_ref[...]

    return call(kernel, "tick", (shaped(token.shape, token.dtype),), [scalars, token], "v", "v")[0]


def add_rows(left, right):
    return (left.astype(wide) + right.astype(wide)).astype(low_type)


Y_BIT, Z_BIT = 1, 2


def split_add(scalars, bit, *terms):
    half = terms[0].shape[0] // 2

    def kernel(scalar_ref, *refs):
        mine = scalar_ref[bit]
        for which, out_ref in ((1 - mine, refs[-2]), (mine, refs[-1])):
            rows = pl.ds(pl.multiple_of(which * half, 16), half)
            total = refs[0][rows, :].astype(wide)
            for ref in refs[1:-2]:
                total = total + ref[rows, :].astype(wide)
            out_ref[...] = total.astype(low_type)

    return call(
        kernel,
        "split_add",
        (shaped((half, D), low_type),) * 2,
        [scalars, *terms],
        "v" * len(terms),
        "vv",
    )


def join(scalars, bit, mine, other):
    half = mine.shape[0]

    def kernel(scalar_ref, mine_ref, other_ref, out_ref):
        at = scalar_ref[bit]
        out_ref[pl.ds(pl.multiple_of(at * half, 16), half), :] = mine_ref[...]
        out_ref[pl.ds(pl.multiple_of((1 - at) * half, 16), half), :] = other_ref[...]

    return call(
        kernel, "join", (shaped((2 * half, D), low_type),), [scalars, mine, other], "vv", "v"
    )[0]


def take_halves(scalars, bit, near, near_partner, far, far_partner):
    half = near.shape[0] // 2

    def kernel(scalar_ref, near_ref, near_other, far_ref, far_other, send_ref, near_out, far_out):
        mine = scalar_ref[bit]
        theirs = pl.ds(pl.multiple_of((1 - mine) * half, 16), half)
        ours = pl.ds(pl.multiple_of(mine * half, 16), half)
        send_ref[:half, :] = add_rows(near_ref[theirs, :], near_other[theirs, :])
        send_ref[half:, :] = add_rows(far_ref[theirs, :], far_other[theirs, :])
        near_out[...] = add_rows(near_ref[ours, :], near_other[ours, :])
        far_out[...] = add_rows(far_ref[ours, :], far_other[ours, :])

    return call(
        kernel,
        "take_halves",
        (shaped((2 * half, D), low_type),) + (shaped((half, D), low_type),) * 2,
        [scalars, near, near_partner, far, far_partner],
        "vvvv",
        "vvv",
    )


def message(rows, extra):
    high = extra.astype(low_type)
    return jnp.concatenate([rows, high, (extra - high.astype(wide)).astype(low_type)], axis=0)


def mixed_hop(scalars, kept, extra, incoming, split):
    rows = kept.shape[0] // 2 if split else kept.shape[0]
    count = extra.shape[0]

    def kernel(scalar_ref, kept_ref, extra_ref, incoming_ref, message_ref, keep_ref, out_ref):
        at = kept.shape[0]
        total = extra_ref[...] + (
            incoming_ref[at : at + count, :].astype(wide)
            + incoming_ref[at + count : at + 2 * count, :].astype(wide)
        )
        out_ref[...] = total
        high = total.astype(low_type)
        message_ref[rows : rows + count, :] = high
        message_ref[rows + count :, :] = (total - high.astype(wide)).astype(low_type)
        if split:
            odd = scalar_ref[1]
            theirs = pl.ds(pl.multiple_of((1 - odd) * rows, 16), rows)
            ours = pl.ds(pl.multiple_of(odd * rows, 16), rows)
            message_ref[:rows, :] = add_rows(kept_ref[theirs, :], incoming_ref[theirs, :])
            keep_ref[...] = add_rows(kept_ref[ours, :], incoming_ref[ours, :])
        else:
            joined = add_rows(kept_ref[...], incoming_ref[:rows, :])
            message_ref[:rows, :] = joined
            keep_ref[...] = joined

    return call(
        kernel,
        "mixed_hop",
        (
            shaped((rows + 2 * count, D), low_type),
            shaped((rows, D), low_type),
            shaped((count, D), wide),
        ),
        [scalars, kept, extra, incoming],
        "vvv",
        "vvv",
    )


def finish(scalars, bit, kept, incoming, outputs):
    half = kept.shape[0]
    rows = 2 * half // outputs

    def kernel(scalar_ref, kept_ref, incoming_ref, *refs):
        outs, joined, semaphores = refs[:outputs], refs[outputs], refs[outputs + 1]
        odd = scalar_ref[bit]
        joined[pl.ds(pl.multiple_of(odd * half, 16), half), :] = kept_ref[...].astype(wide)
        joined[pl.ds(pl.multiple_of((1 - odd) * half, 16), half), :] = incoming_ref[
            :half, :
        ].astype(wide)
        wait(
            [
                begin(joined.at[pl.ds(index * rows, rows)], out, semaphores.at[index])
                for index, out in enumerate(outs)
            ]
        )

    return call(
        kernel,
        "finish",
        (shaped((rows, D), wide),) * outputs,
        [scalars, kept, incoming],
        "vv",
        "h" * outputs,
        [pltpu.VMEM((2 * half, D), wide), pltpu.SemaphoreType.DMA((outputs,))],
    )


def attend_forward(scalars, segment_ids, tokens, projection):
    width = D // 4
    heads = width // HEAD_DIM
    block = 256

    def kernel(scalar_ref, segment_ref, tokens_ref, *refs):
        (parts,), refs = unflatten(refs, [projection])
        attended_ref, bias_ref, qkv_out, probs_out, mask, weight, qkv_ref, probs_ref, semaphores = refs
        place, odd, length = read_scalars(scalar_ref)
        fetch = begin_weight(parts, odd, weight, semaphores, 0)
        query_owner = segment_ref[pl.ds(place, 1), :].astype(wide)
        key_owner = jnp.broadcast_to(query_owner, (128, L)).T
        key_at = lax.broadcasted_iota(jnp.int32, (L, 128), 0)
        key_owner = jnp.where(key_at < length, key_owner, -1.0)
        query_at = lax.broadcasted_iota(jnp.int32, (L, 128), 1)
        for start in range(0, L, 128):
            allowed = (key_owner == query_owner[:, start : start + 128]) | (
                key_at == query_at + start
            )
            mask[:, start : start + 128] = jnp.where(allowed, 0.0, -1e30)
        wait(fetch)
        bias_ref[...] = weight[3 * width : 3 * width + 16, :]
        bias = weight[3 * width : 3 * width + 1, : 3 * width].astype(wide)
        qkv_ref[...] = (product(tokens_ref[...], weight[: 3 * width, :], NT) + bias).astype(
            low_type
        )
        qkv_copy = begin(qkv_ref, qkv_out, semaphores.at[2])

        @pl.loop(0, L // block)
        def _(step):
            rows = pl.ds(pl.multiple_of(step * block, block), block)
            for head in range(heads):
                at = head * HEAD_DIM
                queries = qkv_ref[rows, at : at + HEAD_DIM] * jnp.asarray(
                    HEAD_DIM**-0.5, low_type
                )
                key_rows = qkv_ref[:, width + at : width + at + HEAD_DIM]
                values = qkv_ref[:, 2 * width + at : 2 * width + at + HEAD_DIM]
                scores = product(key_rows, queries, NT) + mask[:, rows]
                highest = jnp.max(scores, axis=0, keepdims=True)
                expanded = jnp.exp(scores - highest)
                total = jnp.sum(expanded, axis=0, keepdims=True)
                probs = (expanded * (1.0 / total)).astype(low_type)
                probs_ref[step, head] = probs
                attended_ref[rows, at : at + HEAD_DIM] = product(probs, values, TN).astype(
                    low_type
                )
            begin(probs_ref.at[step], probs_out.at[step], semaphores.at[3 + step])

        qkv_copy.wait()
        for step in range(L // block):
            pltpu.make_async_copy(
                probs_ref.at[step], probs_out.at[step], semaphores.at[3 + step]
            ).wait()

    kept = (L // block, heads, L, block)
    return call(
        kernel,
        "attend_forward",
        (
            shaped((L, width), low_type),
            shaped((16, D), low_type),
            shaped((L, 3 * width), low_type),
            shaped(kept, low_type),
        ),
        [scalars, segment_ids, tokens, *projection],
        "vv" + "h" * len(projection),
        "vvhh",
        [
            pltpu.VMEM((L, L), wide),
            pltpu.VMEM((3 * width + EXTRA, D), low_type),
            pltpu.VMEM((L, 3 * width), low_type),
            pltpu.VMEM(kept, low_type),
            pltpu.SemaphoreType.DMA((3 + L // block,)),
        ],
    )


def attend_backward(scalars, slot, branch_low, mixer, attended, qkv, probs):
    width = D // 4
    heads = width // HEAD_DIM
    block = 256

    def kernel(scalar_ref, branch_ref, attended_ref, qkv_in, probs_in, *refs):
        (parts,), refs = unflatten(refs, [mixer])
        grad_ref, bias_ref, weight, qkv_ref, probs_ref, outgoing, sums, dots, semaphores = refs
        fetch = begin_weight(parts, scalar_ref[1], weight, semaphores, 0, PROJECTION_ROWS)
        fetch_rest = [
            begin(qkv_in, qkv_ref, semaphores.at[2]),
            begin(probs_in, probs_ref, semaphores.at[3]),
        ]
        wait(fetch)
        attended_grad = product(branch_ref[...], weight[...], NT).astype(low_type)
        outgoing[...] = attended_grad
        along = (attended_ref[...].astype(wide) * attended_grad.astype(wide)).T
        for head in range(heads):
            dots[head : head + 1, :] = jnp.sum(
                along[head * HEAD_DIM : (head + 1) * HEAD_DIM], axis=0, keepdims=True
            )
            sums[head] = jnp.zeros((L, HEAD_DIM), wide)
        wait(fetch_rest)

        @pl.loop(0, L // block)
        def _(step):
            rows = pl.ds(pl.multiple_of(step * block, block), block)
            for head in range(heads):
                at = head * HEAD_DIM
                queries = qkv_ref[:, at : at + HEAD_DIM] * jnp.asarray(HEAD_DIM**-0.5, low_type)
                key_rows = qkv_ref[rows, width + at : width + at + HEAD_DIM]
                values = qkv_ref[rows, 2 * width + at : 2 * width + at + HEAD_DIM]
                grad = outgoing[:, at : at + HEAD_DIM]
                probs = jnp.concatenate(
                    [probs_ref[part, head, rows, :] for part in range(L // block)], axis=1
                )
                probs_grad = product(values, grad, NT)
                scores_grad = (
                    probs.astype(wide) * (probs_grad - dots[head : head + 1, :])
                ).astype(low_type)
                grad_ref[rows, width + at : width + at + HEAD_DIM] = product(
                    scores_grad, queries, NN
                ).astype(low_type)
                grad_ref[rows, 2 * width + at : 2 * width + at + HEAD_DIM] = product(
                    probs, grad, NN
                ).astype(low_type)
                sums[head] += product(scores_grad, key_rows, TN)

        for head in range(heads):
            at = head * HEAD_DIM
            grad_ref[:, at : at + HEAD_DIM] = (sums[head] * (HEAD_DIM**-0.5)).astype(low_type)
        bias_ref[...] = jnp.zeros((8, D), wide)
        quarter = scalar_ref[0] ^ slot
        bias_ref[pl.ds(quarter, 1), : 3 * width] = jnp.sum(
            grad_ref[...].astype(wide), axis=0, keepdims=True
        )

    return call(
        kernel,
        "attend_backward",
        (shaped((L, 3 * width), low_type), shaped((8, D), wide)),
        [scalars, branch_low, attended, qkv, probs, *mixer],
        "vvhh" + "h" * len(mixer),
        "vv",
        [
            pltpu.VMEM((width, D), low_type),
            pltpu.VMEM((L, 3 * width), low_type),
            pltpu.VMEM(probs.shape, low_type),
            pltpu.VMEM((L, width), low_type),
            pltpu.VMEM((heads, L, HEAD_DIM), wide),
            pltpu.VMEM((8, L), wide),
            pltpu.SemaphoreType.DMA((4,)),
        ],
    )


def normalize(rows):
    center = rows - jnp.mean(rows, axis=-1, keepdims=True)
    inverse = lax.rsqrt(jnp.mean(center * center, axis=-1, keepdims=True) + eps_norm)
    return center * inverse, inverse


def normalize_backward(scaled, normed, inverse):
    middle = jnp.mean(scaled, axis=-1, keepdims=True)
    along = jnp.mean(scaled * normed, axis=-1, keepdims=True)
    return inverse * (scaled - middle - normed * along)


def column_sum(rows):
    return jnp.sum(rows, axis=0, keepdims=True)


BLOCK = 256
STEPS = L // BLOCK


def block_rows(step):
    return pl.ds(pl.multiple_of(step * BLOCK, BLOCK), BLOCK)


def mix_norm(scalars, vectors, tokens, attended, mixers):
    width = D // 4

    def kernel(scalar_ref, vector_ref, tokens_ref, *refs):
        attended_refs = refs[:4]
        parts, refs = unflatten(refs[4:], mixers)
        inverse_ref, low_ref, sums_ref, hat_out, weight, hat_ref, semaphores = refs
        _, odd, length = read_scalars(scalar_ref)
        fetches = [
            begin_weight(
                parts[i], odd, weight.at[pl.ds(i * width, width)], semaphores, 2 * i, PROJECTION_ROWS
            )
            for i in range(4)
        ]
        vectors = vector_ref[...].astype(wide)
        sums_ref[...] = jnp.zeros((8, D), wide)
        for fetch in fetches:
            wait(fetch)

        @pl.loop(0, STEPS)
        def _(step):
            at = block_rows(step)
            branch = vectors[0:1]
            for index in range(4):
                branch = branch + product(
                    attended_refs[index][at, :], weight[index * width : (index + 1) * width], NN
                )
            rows = tokens_ref[at, :].astype(wide)
            hat, inverse = normalize(rows + branch)
            hat_ref[at, :] = hat
            begin(hat_ref.at[at], hat_out.at[at], semaphores.at[8 + step])
            inverse_ref[at, :] = inverse
            low_ref[at, :] = (hat * vectors[1:2] + vectors[2:3]).astype(low_type)
            place = lax.broadcasted_iota(jnp.int32, (BLOCK, 1), 0) + step * BLOCK
            valid = (place < length).astype(wide)
            sums_ref[0:1, :] += column_sum(valid * rows * rows)
            sums_ref[1:2, :] += column_sum(valid * branch * branch)
            sums_ref[2:3, :] += column_sum(jnp.broadcast_to(valid, (BLOCK, D)))

        for step in range(STEPS):
            at = block_rows(step)
            pltpu.make_async_copy(hat_ref.at[at], hat_out.at[at], semaphores.at[8 + step]).wait()

    return call(
        kernel,
        "mix_norm",
        (shaped((L, 1), wide), shaped((L, D), low_type), shaped((8, D), wide), shaped((L, D), wide)),
        [scalars, vectors, tokens, *attended, *flat(mixers)],
        "vv" + "v" * 4 + "h" * len(flat(mixers)),
        "vvvh",
        [
            pltpu.VMEM((D, D), low_type),
            pltpu.VMEM((L, D), wide),
            pltpu.SemaphoreType.DMA((8 + STEPS,)),
        ],
    )


def inner_forward(scalars, normed_low, weights, biases):
    chunk = 256

    def kernel(scalar_ref, normed_ref, *refs):
        bias_refs = refs[:2]
        parts, refs = unflatten(refs[2:], weights)
        out_refs, slope_out, weight, bias, slope_ref, semaphores = refs[:2], *refs[2:]
        odd = scalar_ref[1]
        fetches = [begin_weight(parts[i], odd, weight.at[i], semaphores, 2 * i) for i in range(2)]
        for index in range(2):
            bias[index] = bias_refs[index][...].astype(wide)

        @pl.loop(0, 2)
        def _(slot):
            for index in range(2):

                @pl.when(slot == index)
                def _(index=index):
                    wait(fetches[index])

            @pl.loop(0, D // chunk)
            def _(step):
                columns = pl.ds(pl.multiple_of(step * chunk, chunk), chunk)
                inner_pre = (
                    product(normed_ref[...], weight[slot, :, columns], NN)
                    + bias[slot, 1:2, columns]
                )
                below = 0.5 * (1.0 + lax.erf(inner_pre * root_half))
                density = jnp.exp(-0.5 * inner_pre * inner_pre) * inv_root_tau
                activated = (inner_pre * below).astype(low_type)
                slope_ref[slot, :, columns] = (below + inner_pre * density).astype(low_type)
                for index in range(2):

                    @pl.when(slot == index)
                    def _(index=index):
                        out_refs[index][:, columns] = activated

            begin(slope_ref.at[slot], slope_out.at[slot], semaphores.at[4 + slot])

        for slot in range(2):
            pltpu.make_async_copy(
                slope_ref.at[slot], slope_out.at[slot], semaphores.at[4 + slot]
            ).wait()

    return call(
        kernel,
        "inner_forward",
        (shaped((L, D), low_type),) * 2 + (shaped((2, L, D), low_type),),
        [scalars, normed_low, *biases, *flat(weights)],
        "vvv" + "h" * len(flat(weights)),
        "vvh",
        [
            pltpu.VMEM((2, D, D), low_type),
            pltpu.VMEM((2, 16, D), wide),
            pltpu.VMEM((2, L, D), low_type),
            pltpu.SemaphoreType.DMA((6,)),
        ],
    )


def middle(
    scalars, vectors, hat_one, inverse_one, grad_out, activated, slopes, outers, inners
):
    chunk = 256

    def kernel(scalar_ref, vector_ref, hat_in, inverse_ref, incoming_in, *refs):
        left_refs, slope_in = refs[:4], refs[4:6]
        outer_parts, refs = unflatten(refs[6:], outers)
        inner_parts, refs = unflatten(refs, inners)
        low_ref, branch_ref, bias_ref, sums_ref = refs[:4]
        inner_refs, grad_out_ref, result_out = refs[4:8], refs[8], refs[9]
        outer, inner, slope_ref, hat_ref, incoming_ref, second_ref, grad_ref, result_ref = refs[10:18]
        semaphores = refs[18]
        place, odd, length = read_scalars(scalar_ref)
        fetch_outer = [
            begin_weight(outer_parts[i], odd, outer.at[i], semaphores, 2 * i) for i in range(4)
        ]
        fetch_rest = [
            begin(hat_in, hat_ref, semaphores.at[8]),
            begin(incoming_in, incoming_ref, semaphores.at[9]),
        ]
        fetch_slope = [
            begin(slope_in[i // 2].at[i % 2], slope_ref.at[i], semaphores.at[10 + i])
            for i in range(4)
        ]
        fetch_inner = [
            begin_weight(inner_parts[i], odd, inner.at[i], semaphores, 14 + 2 * i)
            for i in range(4)
        ]
        vectors = vector_ref[...].astype(wide)
        sums_ref[...] = jnp.zeros((16, D), wide)
        bias_ref[...] = jnp.zeros((8, D), wide)

        def result_copy(step):
            at = block_rows(step)
            return pltpu.make_async_copy(
                result_ref.at[at], result_out.at[at], semaphores.at[22 + step]
            )

        def grad_copy(step):
            at = block_rows(step)
            return pltpu.make_async_copy(
                grad_ref.at[at], grad_out_ref.at[at], semaphores.at[22 + STEPS + step]
            )

        @pl.loop(0, STEPS)
        def _(step):
            at = block_rows(step)
            branch = vectors[3:4]
            for index in range(4):

                @pl.when(step == 0)
                def _(index=index):
                    wait(fetch_outer[index])

                branch = branch + product(left_refs[index][at, :], outer[index], NN)

            @pl.when(step == 0)
            def _():
                wait(fetch_rest)

            normed_one = hat_ref[at, :] * vectors[1:2] + vectors[2:3]
            hat, inverse = normalize(normed_one + branch)
            result_ref[at, :] = (hat * vectors[4:5] + vectors[5:6]).astype(low_type)
            result_copy(step).start()
            incoming = incoming_ref[at, :].astype(wide)
            grad = normalize_backward(incoming * vectors[4:5], hat, inverse)
            second_ref[at, :] = grad
            low_ref[at, :] = grad.astype(low_type)
            row = lax.broadcasted_iota(jnp.int32, (BLOCK, 1), 0) + step * BLOCK
            valid = (row < length).astype(wide)
            sums_ref[0:1, :] += column_sum(incoming * hat)
            sums_ref[1:2, :] += column_sum(incoming)
            sums_ref[2:3, :] += column_sum(grad)
            sums_ref[3:4, :] += column_sum(valid * branch * branch)

        @pl.loop(0, 4)
        def _(slot):
            for index in range(4):

                @pl.when(slot == index)
                def _(index=index):
                    fetch_slope[index].wait()

            @pl.loop(0, D // chunk)
            def _(step):
                columns = pl.ds(pl.multiple_of(step * chunk, chunk), chunk)
                grad = product(low_ref[...], outer[slot, columns, :], NT) * slope_ref[
                    slot, :, columns
                ].astype(wide)
                bias_ref[pl.ds(place ^ slot, 1), columns] = column_sum(grad)
                low = grad.astype(low_type)
                for index in range(4):

                    @pl.when(slot == index)
                    def _(index=index):
                        inner_refs[index][:, columns] = low

        for fetch in fetch_inner:
            wait(fetch)

        @pl.loop(0, STEPS)
        def _(step):
            at = block_rows(step)
            total = second_ref[at, :]
            for index in range(4):
                total = total + product(inner_refs[index][at, :], inner[index], NT)
            hat = hat_ref[at, :]
            grad = normalize_backward(total * vectors[1:2], hat, inverse_ref[at, :])
            grad_ref[at, :] = grad
            grad_copy(step).start()
            branch_ref[at, :] = grad.astype(low_type)
            sums_ref[8:9, :] += column_sum(total * hat)
            sums_ref[9:10, :] += column_sum(total)
            sums_ref[10:11, :] += column_sum(grad)

        for step in range(STEPS):
            result_copy(step).wait()
            grad_copy(step).wait()

    return call(
        kernel,
        "middle",
        (
            shaped((L, D), low_type),
            shaped((L, D), low_type),
            shaped((8, D), wide),
            shaped((16, D), wide),
        )
        + (shaped((L, D), low_type),) * 4
        + (shaped((L, D), wide), shaped((L, D), low_type)),
        [
            scalars,
            vectors,
            hat_one,
            inverse_one,
            grad_out,
            *activated,
            *slopes,
            *flat(outers),
            *flat(inners),
        ],
        "vhvh" + "vvvv" + "hh" + "h" * len(flat(outers) + flat(inners)),
        "vvvv" + "vvvv" + "hh",
        [
            pltpu.VMEM((4, D, D), low_type),
            pltpu.VMEM((4, D, D), low_type),
            pltpu.VMEM((4, L, D), low_type),
            pltpu.VMEM((L, D), wide),
            pltpu.VMEM((L, D), low_type),
            pltpu.VMEM((L, D), wide),
            pltpu.VMEM((L, D), wide),
            pltpu.VMEM((L, D), low_type),
            pltpu.SemaphoreType.DMA((22 + 2 * STEPS,)),
        ],
        limit=32,
    )


def add_halves(scalars, near, far, incoming):
    half = near.shape[0]

    def kernel(scalar_ref, near_ref, far_ref, incoming_ref, near_out, far_out):
        near_out[...] = add_rows(near_ref[...], incoming_ref[:half, :])
        far_out[...] = add_rows(far_ref[...], incoming_ref[half:, :])

    return call(
        kernel,
        "add_halves",
        (shaped((half, D), low_type),) * 2,
        [scalars, near, far, incoming],
        "vvv",
        "vv",
    )


def input_backward(scalars, first_grad, qkv_grads, projections):
    width = D // 4

    def kernel(scalar_ref, first_in, *refs):
        left_refs = refs[:4]
        parts, refs = unflatten(refs[4:], projections)
        out, weight, first_ref, semaphores = refs
        odd = scalar_ref[1]
        fetches = [begin_weight(parts[i], odd, weight.at[i], semaphores, 2 * i) for i in range(4)]
        fetch_first = begin(first_in, first_ref, semaphores.at[8])

        @pl.loop(0, STEPS)
        def _(step):
            at = block_rows(step)
            total = 0.0
            for index in range(4):

                @pl.when(step == 0)
                def _(index=index):
                    wait(fetches[index])

                total = total + product(left_refs[index][at, :], weight[index, : 3 * width], NN)

            @pl.when(step == 0)
            def _():
                fetch_first.wait()

            first_ref[at, :] = total + first_ref[at, :]
            begin(first_ref.at[at], out.at[at], semaphores.at[9 + step])

        for step in range(STEPS):
            at = block_rows(step)
            pltpu.make_async_copy(first_ref.at[at], out.at[at], semaphores.at[9 + step]).wait()

    return call(
        kernel,
        "input_backward",
        (shaped((L, D), wide),),
        [scalars, first_grad, *qkv_grads, *flat(projections)],
        "h" + "v" * 4 + "h" * len(flat(projections)),
        "h",
        [
            pltpu.VMEM((4, 3 * width + EXTRA, D), low_type),
            pltpu.VMEM((L, D), wide),
            pltpu.SemaphoreType.DMA((9 + STEPS,)),
        ],
        limit=16,
    )[0]


def solution(mesh):
    dp_size = mesh.shape["dp"]
    tensor_size = mesh.shape["tensor"]
    masks = [1 << bit for bit in range(dp_size.bit_length() - 1)]

    def over_tensor(value, mask):
        return lax.ppermute(value, "tensor", [(i, i ^ mask) for i in range(tensor_size)])

    def over_dp(value, mask):
        return lax.ppermute(value, "dp", [(i, i ^ mask) for i in range(dp_size)])

    def body(
        tokens,
        grad_out,
        lengths,
        segment_ids,
        query_weight,
        query_bias,
        key_weight,
        value_weight,
        value_bias,
        mixer_weight,
        mixer_bias,
        first_gain,
        first_shift,
        inner_weight,
        inner_bias,
        outer_weight,
        outer_bias,
        second_gain,
        second_shift,
    ):
        width = query_weight.shape[1]
        place = lax.axis_index("tensor")
        odd = lax.axis_index("dp") % 2
        chain = [jnp.zeros((8, 128), wide)]

        def after(*values):
            held = lax.optimization_barrier((chain[0],) + values)
            return held[1:] if len(values) > 1 else held[1]

        def done(*values):
            chain[0] = lax.optimization_barrier((chain[0],) + values)[0]
            return values if len(values) > 1 else values[0]

        lines = [mixer_bias, first_gain, first_shift, outer_bias, second_gain, second_shift]
        lines = dict(enumerate(lines))
        lines[8] = jnp.pad(query_bias, (0, D - width)) + jnp.pad(
            value_bias, (2 * width, D - 3 * width)
        )
        lines[9] = inner_bias
        line_at = lax.broadcasted_iota(jnp.int32, (16, D), 0)
        vectors = jnp.zeros((16, D), low_type)
        for index, line in lines.items():
            vectors = jnp.where(line_at == index, line[None, :], vectors)
        high = lax.axis_index("dp") // 2 % 2
        scalars = jnp.concatenate([jnp.stack([place, odd, high]).astype(jnp.int32), lengths])

        def hold():
            chain[0] = tick(scalars, chain[0])

        def send(value, mask):
            return over_tensor(after(value), mask)

        def pass_y(value):
            return over_dp(after(value), masks[0])

        def land(value):
            return done(after(value))

        def stage(function, *operands):
            return done(*function(after(scalars), *operands))

        inner_piece, outer_piece, own_heads = done(
            *prepare(
                scalars,
                vectors,
                [query_weight.T, key_weight.T, value_weight.T],
                mixer_weight,
                inner_weight,
                outer_weight,
            )
        )
        heads = {}

        def attend(slot, parts):
            heads[slot] = stage(attend_forward, segment_ids, tokens, parts)

        heads_x = send(own_heads, 2)
        heads_core = send(own_heads, 1)
        hold()
        attend(0, (own_heads,))
        heads_core = land(heads_core)
        inner_core = send(inner_weight, 1)
        attend(1, (heads_core,))
        inner_core = land(inner_core)
        outer_core = send(outer_weight, 1)
        hold()
        heads_x = land(heads_x)
        inner_x = send(inner_piece, 2)
        heads_near = send(heads_x, 1)
        outer_core = land(outer_core)
        if HOLD_A:
            hold()
        attend(2, (heads_x,))
        heads_near = land(heads_near)
        attend(3, (heads_near,))
        inner_x = land(inner_x)
        inner_y = pass_y(inner_x)
        outer_x = send(outer_piece, 2)
        inner_near = send(inner_x, 1)
        if HOLD_B:
            hold()
        attended = [heads[j][0] for j in range(4)]
        inner_biases = [heads[j][1] for j in range(4)]
        projections = mixers = [(own_heads,), (heads_core,), (heads_x,), (heads_near,)]
        inverse_one, normed_low, sums_one, hat_one = stage(
            mix_norm, vectors, tokens, attended, mixers
        )
        inner_near = land(inner_near)
        *activated, slope_one = stage(
            inner_forward, normed_low, [(inner_weight,), (inner_core,)], inner_biases[:2]
        )
        outer_x = land(outer_x)
        outer_y = pass_y(outer_x)
        outer_near = send(outer_x, 1)
        if HOLD_C:
            hold()
        inner_y = land(inner_y)
        inner_far = send(inner_y, 1)
        if HOLD_D:
            hold()
        outer_near = land(outer_near)
        inner_far = land(inner_far)
        *more, slope_two = stage(
            inner_forward,
            normed_low,
            [(inner_x, inner_y), (inner_near, inner_far)],
            inner_biases[2:],
        )
        activated = activated + more
        inners = [(inner_weight,), (inner_core,), (inner_x, inner_y), (inner_near, inner_far)]
        outer_y = land(outer_y)
        outer_far = send(outer_y, 1)
        hold()
        outer_far = land(outer_far)
        outers = [(outer_weight,), (outer_core,), (outer_x, outer_y), (outer_near, outer_far)]
        ffn_low, branch_low, inner_bias_rows, sums_two, *rest = stage(
            middle,
            vectors,
            hat_one,
            inverse_one,
            grad_out,
            activated,
            [slope_one, slope_two],
            outers,
            inners,
        )
        *inner_lows, first_grad, layer_out = rest

        def part(left, right):
            left, right = after(left, right)
            return done(product(left, right, TN).astype(low_type))

        def add_low(left, right):
            return done(add_rows(*after(left, right)))

        class Reduction:
            def __init__(self, outputs=1, bits=(Y_BIT, Z_BIT)):
                self.outputs, self.bits = outputs, bits
                self.todo = ["split", "split"] + ["add"] * (len(masks) - 2)
                self.todo += ["back", "join", "end"]
                self.level = 0

            def begin(self, sent):
                self.incoming = send(sent, 2)
                if HOLD_X:
                    hold()
                return self

            def across(self, value, mask):
                self.incoming = over_dp(after(value), mask)
                if HOLD_HOPS:
                    hold()

            def terms(self):
                return (self.kept,)

            def hop(self):
                if not self.todo:
                    return
                step = self.todo.pop(0)
                *terms, incoming = after(*self.terms(), self.incoming)
                if step == "split":
                    bit = self.bits[self.level]
                    sent, self.kept = stage(split_add, bit, *terms, incoming)
                    self.terms = lambda: (self.kept,)
                    self.level += 1
                    self.across(sent, bit)
                elif step in ("add", "back"):
                    self.kept = done(add_rows(terms[0], incoming))
                    mask = self.bits[1] if step == "back" else 4 << (self.level - 2)
                    self.level += 1
                    self.across(self.kept, mask)
                elif step == "join":
                    self.kept = done(join(after(scalars), self.bits[1], terms[0], incoming))
                    self.across(self.kept, self.bits[0])
                else:
                    self.result = finish(
                        after(scalars), self.bits[0], terms[0], incoming, self.outputs
                    )
                    done(*self.result)

        class MixedReduction(Reduction):
            def __init__(self, kept, extra):
                super().__init__()
                self.kept, self.extra = kept, extra
                self.todo = ["mixed"] * (len(masks) + 1) + ["end"]

            def hop(self):
                if not self.todo or self.todo[0] == "end":
                    super().hop()
                    return
                self.todo.pop(0)
                kept, extra, incoming = after(self.kept, self.extra, self.incoming)
                text, self.kept, self.extra = stage(
                    mixed_hop, kept, extra, incoming, self.level == 0
                )
                mask = masks[self.level] if self.level < len(masks) else masks[0]
                self.level += 1
                self.across(text, mask)

        class CrossReduction(Reduction):
            def __init__(self, near, near_partner, far, far_partner, bits):
                super().__init__(1, bits)
                sent, self.near, self.far = stage(
                    take_halves, bits[0], *after(near, near_partner, far, far_partner)
                )
                self.todo[0] = "cross"
                self.incoming = over_dp(after(sent), bits[0])
                if HOLD_Y:
                    hold()

            def hop(self):
                if self.todo and self.todo[0] == "cross":
                    self.todo.pop(0)
                    near, far, incoming = after(self.near, self.far, self.incoming)
                    self.kept, far = stage(add_halves, near, far, incoming)
                    self.level = 1
                    self.incoming = send(far, 2)
                    if HOLD_Z:
                        hold()
                else:
                    super().hop()

        partner = {}
        outer_parts, inner_parts, heads_parts = {}, {}, {}
        qkv_grads, qkv_bias = {}, {}

        def retreat(slot):
            attended_low, _, qkv, probs = heads[slot]
            qkv_grads[slot], qkv_bias[slot] = stage(
                attend_backward, slot, branch_low, mixers[slot], attended_low, qkv, probs
            )

        def split_step(name, slot):
            left, right = {
                "o": (activated[slot], ffn_low),
                "i": (normed_low, inner_lows[slot]),
                "m": (attended[slot], branch_low),
                "h": (qkv_grads.get(slot), tokens),
            }[name]
            share = part(left, right)
            if slot % 2:
                partner[name, slot - 1] = send(share, 1)
            else:
                own_share[name, slot] = share

        def own_sum(name, slot):
            return add_low(own_share[name, slot], partner[name, slot])

        own_share, chains = {}, {}
        for step in PLAN:
            name, slot = step[0], int(step[1])
            if name == "b":
                retreat(slot)
            elif name in "oimh":
                split_step(name, slot)
            elif name == "X":
                which = ("o", None, "h")[slot]
                chains[slot] = Reduction(3 if slot == 2 else 1).begin(own_sum(which, 2))
            elif name == "Y":
                chains[1] = CrossReduction(
                    own_share["i", 0],
                    partner["i", 0],
                    own_share["i", 2],
                    partner["i", 2],
                    (Z_BIT, Y_BIT),
                )
            elif name == "S":
                small = done(
                    jnp.concatenate(
                        [
                            sums_one,
                            sums_two,
                            inner_bias_rows,
                            qkv_bias[0] + qkv_bias[1] + qkv_bias[2] + qkv_bias[3],
                        ]
                    )
                )
                small_other = send(small, 1)
            elif name == "M":
                small = done(small + after(small_other))
                sent = done(message(own_sum("m", 2), small))
                chains[3] = MixedReduction(own_sum("m", 0), small).begin(sent)
            elif name == "B":
                tokens_grad = done(
                    input_backward(
                        after(scalars), first_grad, [qkv_grads[j] for j in range(4)], projections
                    )
                )
            else:
                if name == "H" and slot in (0, 2) and chains[slot].level == 0:
                    which = "o" if slot == 0 else "h"
                    both = (own_share[which, 0], partner[which, 0])
                    chains[slot].terms = lambda both=both: both
                chains[slot].hop()
        for chain_left in chains.values():
            while chain_left.todo:
                chain_left.hop()
        small = chains[3].extra
        outer_chain, inner_chain, heads_chain, mixer_chain = (chains[j] for j in range(4))

        totals = jnp.sum(jnp.stack([small[0], small[1], small[11]]), axis=1)
        statistics = jnp.sqrt(totals / (small[2, 0] * D))
        own_inner_bias = lax.dynamic_index_in_dim(small[24:28], place, 0, keepdims=False)
        own_qkv_bias = lax.dynamic_index_in_dim(small[32:36], place, 0, keepdims=False)
        query_grad, key_grad, value_grad = heads_chain.result
        return (
            layer_out,
            tokens_grad,
            query_grad.T,
            own_qkv_bias[:width],
            key_grad.T,
            value_grad.T,
            own_qkv_bias[2 * width : 3 * width],
            mixer_chain.result[0],
            small[18],
            small[16],
            small[17],
            inner_chain.result[0],
            own_inner_bias,
            outer_chain.result[0],
            small[10],
            small[8],
            small[9],
            statistics,
        )

    in_specs = (
        P(("dp", "tensor"), None),
        P(("dp", "tensor"), None),
        P("dp"),
        P("dp", None),
        P(None, "tensor"),
        P("tensor"),
        P(None, "tensor"),
        P(None, "tensor"),
        P("tensor"),
        P("tensor", None),
        P(),
        P(),
        P(),
        P(None, "tensor"),
        P("tensor"),
        P("tensor", None),
        P(),
        P(),
        P(),
    )
    out_specs = (
        P(("dp", "tensor"), None),
        P(("dp", "tensor"), None),
        P(None, "tensor"),
        P("tensor"),
        P(None, "tensor"),
        P(None, "tensor"),
        P("tensor"),
        P("tensor", None),
        P(),
        P(),
        P(),
        P(None, "tensor"),
        P("tensor"),
        P("tensor", None),
        P(),
        P(),
        P(),
        P(),
    )
    return jax.shard_map(body, mesh=mesh, in_specs=in_specs, out_specs=out_specs, check_vma=False)
```

```python
import jax
import jax.numpy as jnp
from jax import lax
from jax.experimental import pallas as pl
from jax.experimental.pallas import tpu as pltpu
from jax.sharding import PartitionSpec as P

D = 768
HEAD_DIM = 64
L = 512
EXTRA = 32

eps_norm = 1e-06
root_half = 0.7071067811865476
inv_root_tau = 0.3989422804014327
low_type = jnp.bfloat16
wide = jnp.float32
NN = (((1,), (0,)), ((), ()))
NT = (((1,), (1,)), ((), ()))
TN = (((0,), (0,)), ((), ()))


def product(left, right, dims):
    return lax.dot_general(left, right, dims, preferred_element_type=wide)


def shaped(shape, dtype):
    return jax.ShapeDtypeStruct(shape, dtype)


COST = 100000000000
PRICES = {
    "prepare": 100000000000,
    "attend_forward": 100000000000,
    "mix_norm": 100000000000,
    "inner_forward": 5000000000,
    "middle": 100000000000,
    "attend_backward": 100000000000,
    "input_backward": 0,
    "split_add": 0,
    "mixed_hop": 0,
    "finish": 0,
    "take_halves": 0,
    "add_halves": 0,
    "join": 0,
    "tick": 100000000000,
}
HOLD_HOPS = False
HOLD_A = True
HOLD_B = False
HOLD_C = False
HOLD_D = False
HOLD_X = True
HOLD_Y = False
HOLD_Z = False
BRANCH_LATE = False
PLAN = (
    "o3", "i3", "o2", "X0", "i1", "i2", "i0", "Y1", "b3", "h3", "b2", "h2",
    "X2", "o1", "o0", "b1", "h1", "b0", "m3", "H0", "H1", "m1", "m2", "m0",
    "S0", "h0", "M3", "H0", "H2", "H1", "H0", "H3", "H2", "H0", "H1", "B0",
    "H2", "H3", "H0", "H1", "H3", "H2", "H1", "H3", "H2", "H1", "H2", "H0",
    "H1", "H3", "H0",
)


def call(
    kernel, name, out_shape, operands, spaces, out_spaces, scratch=(), limit=14
):
    place = {"v": pltpu.VMEM, "h": pltpu.HBM}
    price = PRICES.get(name, COST)
    out_shape = tuple(
        pltpu.HBM(one.shape, one.dtype) if letter == "h" else one
        for one, letter in zip(out_shape, out_spaces)
    )
    operands = operands[:1] + [
        pltpu.with_memory_space_constraint(one, pltpu.HBM) if letter == "h" else one
        for one, letter in zip(operands[1:], spaces)
    ]
    return pl.pallas_call(
        kernel,
        out_shape=out_shape,
        in_specs=[pl.BlockSpec(memory_space=pltpu.SMEM)]
        + [pl.BlockSpec(memory_space=place[letter]) for letter in spaces],
        out_specs=tuple(pl.BlockSpec(memory_space=place[letter]) for letter in out_spaces),
        scratch_shapes=list(scratch),
        compiler_params=pltpu.CompilerParams(vmem_limit_bytes=limit << 20),
        cost_estimate=pl.CostEstimate(flops=price, transcendentals=0, bytes_accessed=price // 300),
        name=name,
    )(*operands)


def read_scalars(scalar_ref):
    place = scalar_ref[0]
    return place, scalar_ref[1], scalar_ref[3 + place]


def begin(source, target, semaphore):
    copy = pltpu.make_async_copy(source, target, semaphore)
    copy.start()
    return copy


def begin_weight(parts, odd, target, semaphores, at, first=0):
    rows = target.shape[0] // len(parts)
    first = first // len(parts)
    parts = [part.at[pl.ds(first, rows)] for part in parts]
    if len(parts) == 1:
        return [begin(parts[0], target, semaphores.at[at])]
    return [
        begin(
            part,
            target.at[pl.ds(pl.multiple_of(which * rows, rows), rows)],
            semaphores.at[at + index],
        )
        for index, (part, which) in enumerate(zip(parts, (odd, 1 - odd)))
    ]


def wait(copies):
    for copy in copies:
        copy.wait()


def unflatten(refs, slots):
    out, at = [], 0
    for parts in slots:
        out.append(refs[at : at + len(parts)])
        at += len(parts)
    return out, refs[at:]


def flat(slots):
    return [part for parts in slots for part in parts]


WIDTH = D // 4
PROJECTION_ROWS = 3 * WIDTH + EXTRA


def prepare(scalars, vectors, weights, mixer, inner, outer):
    rows = PROJECTION_ROWS + WIDTH

    def kernel(scalar_ref, vector_ref, query, key, value, mixer_in, inner_in, outer_in, *refs):
        piece_ref, inner_out, outer_out, own_out, own_ref, semaphores = refs
        odd = scalar_ref[1]
        fetches = [
            begin(source, own_ref.at[pl.ds(start, WIDTH)], semaphores.at[index])
            for index, (source, start) in enumerate(
                zip((query, key, value, mixer_in), (0, WIDTH, 2 * WIDTH, PROJECTION_ROWS))
            )
        ]
        half = D // 2
        chosen = pl.ds(pl.multiple_of(odd * half, half), half)
        passes = [
            begin(inner_in.at[chosen], inner_out, semaphores.at[4]),
            begin(outer_in.at[chosen], outer_out, semaphores.at[5]),
        ]
        own_ref[3 * WIDTH : PROJECTION_ROWS, :] = jnp.zeros((EXTRA, D), low_type)
        own_ref[3 * WIDTH : 3 * WIDTH + 8, :] = vector_ref[8:16, :]
        wait(fetches)
        copies = [begin(own_ref, own_out, semaphores.at[6])]
        half = PROJECTION_ROWS // 2
        piece_ref[:half, :] = own_ref[pl.ds(pl.multiple_of(odd * half, 16), half), :]
        half_mixer = WIDTH // 2
        piece_ref[half:, :] = own_ref[
            pl.ds(pl.multiple_of(PROJECTION_ROWS + odd * half_mixer, 16), half_mixer), :
        ]
        wait(copies + passes)

    return call(
        kernel,
        "prepare",
        (
            shaped((rows // 2, D), low_type),
            shaped((D // 2, D), low_type),
            shaped((D // 2, D), low_type),
            shaped((rows, D), low_type),
        ),
        [scalars, vectors, *weights, mixer, inner, outer],
        "vhhhhhh",
        "vvvh",
        [pltpu.VMEM((rows, D), low_type), pltpu.SemaphoreType.DMA((7,))],
    )


def tick(scalars, token):
    def kernel(scalar_ref, token_ref, out_ref):
        out_ref[...] = token_ref[...]

    return call(kernel, "tick", (shaped(token.shape, token.dtype),), [scalars, token], "v", "v")[0]


def add_rows(left, right):
    return (left.astype(wide) + right.astype(wide)).astype(low_type)


Y_BIT, Z_BIT = 1, 2


def split_add(scalars, bit, *terms):
    half = terms[0].shape[0] // 2

    def kernel(scalar_ref, *refs):
        mine = scalar_ref[bit]
        for which, out_ref in ((1 - mine, refs[-2]), (mine, refs[-1])):
            rows = pl.ds(pl.multiple_of(which * half, 16), half)
            total = refs[0][rows, :].astype(wide)
            for ref in refs[1:-2]:
                total = total + ref[rows, :].astype(wide)
            out_ref[...] = total.astype(low_type)

    return call(
        kernel,
        "split_add",
        (shaped((half, D), low_type),) * 2,
        [scalars, *terms],
        "v" * len(terms),
        "vv",
    )


def join(scalars, bit, mine, other):
    half = mine.shape[0]

    def kernel(scalar_ref, mine_ref, other_ref, out_ref):
        at = scalar_ref[bit]
        out_ref[pl.ds(pl.multiple_of(at * half, 16), half), :] = mine_ref[...]
        out_ref[pl.ds(pl.multiple_of((1 - at) * half, 16), half), :] = other_ref[...]

    return call(
        kernel, "join", (shaped((2 * half, D), low_type),), [scalars, mine, other], "vv", "v"
    )[0]


def take_halves(scalars, bit, near, near_partner, far, far_partner):
    half = near.shape[0] // 2

    def kernel(scalar_ref, near_ref, near_other, far_ref, far_other, send_ref, near_out, far_out):
        mine = scalar_ref[bit]
        theirs = pl.ds(pl.multiple_of((1 - mine) * half, 16), half)
        ours = pl.ds(pl.multiple_of(mine * half, 16), half)
        send_ref[:half, :] = add_rows(near_ref[theirs, :], near_other[theirs, :])
        send_ref[half:, :] = add_rows(far_ref[theirs, :], far_other[theirs, :])
        near_out[...] = add_rows(near_ref[ours, :], near_other[ours, :])
        far_out[...] = add_rows(far_ref[ours, :], far_other[ours, :])

    return call(
        kernel,
        "take_halves",
        (shaped((2 * half, D), low_type),) + (shaped((half, D), low_type),) * 2,
        [scalars, near, near_partner, far, far_partner],
        "vvvv",
        "vvv",
    )


def message(rows, extra):
    high = extra.astype(low_type)
    return jnp.concatenate([rows, high, (extra - high.astype(wide)).astype(low_type)], axis=0)


def mixed_hop(scalars, kept, extra, incoming, split):
    rows = kept.shape[0] // 2 if split else kept.shape[0]
    count = extra.shape[0]

    def kernel(scalar_ref, kept_ref, extra_ref, incoming_ref, message_ref, keep_ref, out_ref):
        at = kept.shape[0]
        total = extra_ref[...] + (
            incoming_ref[at : at + count, :].astype(wide)
            + incoming_ref[at + count : at + 2 * count, :].astype(wide)
        )
        out_ref[...] = total
        high = total.astype(low_type)
        message_ref[rows : rows + count, :] = high
        message_ref[rows + count :, :] = (total - high.astype(wide)).astype(low_type)
        if split:
            odd = scalar_ref[1]
            theirs = pl.ds(pl.multiple_of((1 - odd) * rows, 16), rows)
            ours = pl.ds(pl.multiple_of(odd * rows, 16), rows)
            message_ref[:rows, :] = add_rows(kept_ref[theirs, :], incoming_ref[theirs, :])
            keep_ref[...] = add_rows(kept_ref[ours, :], incoming_ref[ours, :])
        else:
            joined = add_rows(kept_ref[...], incoming_ref[:rows, :])
            message_ref[:rows, :] = joined
            keep_ref[...] = joined

    return call(
        kernel,
        "mixed_hop",
        (
            shaped((rows + 2 * count, D), low_type),
            shaped((rows, D), low_type),
            shaped((count, D), wide),
        ),
        [scalars, kept, extra, incoming],
        "vvv",
        "vvv",
    )


def finish(scalars, bit, kept, incoming, outputs):
    half = kept.shape[0]
    rows = 2 * half // outputs

    def kernel(scalar_ref, kept_ref, incoming_ref, *refs):
        outs, joined, semaphores = refs[:outputs], refs[outputs], refs[outputs + 1]
        odd = scalar_ref[bit]
        joined[pl.ds(pl.multiple_of(odd * half, 16), half), :] = kept_ref[...].astype(wide)
        joined[pl.ds(pl.multiple_of((1 - odd) * half, 16), half), :] = incoming_ref[
            :half, :
        ].astype(wide)
        wait(
            [
                begin(joined.at[pl.ds(index * rows, rows)], out, semaphores.at[index])
                for index, out in enumerate(outs)
            ]
        )

    return call(
        kernel,
        "finish",
        (shaped((rows, D), wide),) * outputs,
        [scalars, kept, incoming],
        "vv",
        "h" * outputs,
        [pltpu.VMEM((2 * half, D), wide), pltpu.SemaphoreType.DMA((outputs,))],
    )


def attend_forward(scalars, segment_ids, tokens, projection):
    width = D // 4
    heads = width // HEAD_DIM
    block = 256

    def kernel(scalar_ref, segment_ref, tokens_ref, *refs):
        (parts,), refs = unflatten(refs, [projection])
        attended_ref, bias_ref, qkv_out, probs_out, mask, weight, qkv_ref, probs_ref, semaphores = refs
        place, odd, length = read_scalars(scalar_ref)
        fetch = begin_weight(parts, odd, weight, semaphores, 0)
        query_owner = segment_ref[pl.ds(place, 1), :].astype(wide)
        key_owner = jnp.broadcast_to(query_owner, (128, L)).T
        key_at = lax.broadcasted_iota(jnp.int32, (L, 128), 0)
        key_owner = jnp.where(key_at < length, key_owner, -1.0)
        query_at = lax.broadcasted_iota(jnp.int32, (L, 128), 1)
        for start in range(0, L, 128):
            allowed = (key_owner == query_owner[:, start : start + 128]) | (
                key_at == query_at + start
            )
            mask[:, start : start + 128] = jnp.where(allowed, 0.0, -1e30)
        wait(fetch)
        bias_ref[...] = weight[3 * width : 3 * width + 16, :]
        bias = weight[3 * width : 3 * width + 1, : 3 * width].astype(wide)
        qkv_ref[...] = (product(tokens_ref[...], weight[: 3 * width, :], NT) + bias).astype(
            low_type
        )
        qkv_copy = begin(qkv_ref, qkv_out, semaphores.at[2])

        @pl.loop(0, L // block)
        def _(step):
            rows = pl.ds(pl.multiple_of(step * block, block), block)
            for head in range(heads):
                at = head * HEAD_DIM
                queries = qkv_ref[rows, at : at + HEAD_DIM] * jnp.asarray(
                    HEAD_DIM**-0.5, low_type
                )
                key_rows = qkv_ref[:, width + at : width + at + HEAD_DIM]
                values = qkv_ref[:, 2 * width + at : 2 * width + at + HEAD_DIM]
                scores = product(key_rows, queries, NT) + mask[:, rows]
                highest = jnp.max(scores, axis=0, keepdims=True)
                expanded = jnp.exp(scores - highest)
                total = jnp.sum(expanded, axis=0, keepdims=True)
                probs = (expanded * (1.0 / total)).astype(low_type)
                probs_ref[step, head] = probs
                attended_ref[rows, at : at + HEAD_DIM] = product(probs, values, TN).astype(
                    low_type
                )
            begin(probs_ref.at[step], probs_out.at[step], semaphores.at[3 + step])

        qkv_copy.wait()
        for step in range(L // block):
            pltpu.make_async_copy(
                probs_ref.at[step], probs_out.at[step], semaphores.at[3 + step]
            ).wait()

    kept = (L // block, heads, L, block)
    return call(
        kernel,
        "attend_forward",
        (
            shaped((L, width), low_type),
            shaped((16, D), low_type),
            shaped((L, 3 * width), low_type),
            shaped(kept, low_type),
        ),
        [scalars, segment_ids, tokens, *projection],
        "vv" + "h" * len(projection),
        "vvhh",
        [
            pltpu.VMEM((L, L), wide),
            pltpu.VMEM((3 * width + EXTRA, D), low_type),
            pltpu.VMEM((L, 3 * width), low_type),
            pltpu.VMEM(kept, low_type),
            pltpu.SemaphoreType.DMA((3 + L // block,)),
        ],
    )


def attend_backward(scalars, slot, branch_low, mixer, attended, qkv, probs):
    width = D // 4
    heads = width // HEAD_DIM
    block = 256

    def kernel(scalar_ref, branch_ref, attended_ref, qkv_in, probs_in, *refs):
        (parts,), refs = unflatten(refs, [mixer])
        grad_ref, bias_ref, weight, qkv_ref, probs_ref, outgoing, sums, dots, semaphores = refs
        fetch = begin_weight(parts, scalar_ref[1], weight, semaphores, 0, PROJECTION_ROWS)
        fetch_rest = [
            begin(qkv_in, qkv_ref, semaphores.at[2]),
            begin(probs_in, probs_ref, semaphores.at[3]),
        ]
        wait(fetch)
        attended_grad = product(branch_ref[...], weight[...], NT).astype(low_type)
        outgoing[...] = attended_grad
        along = (attended_ref[...].astype(wide) * attended_grad.astype(wide)).T
        for head in range(heads):
            dots[head : head + 1, :] = jnp.sum(
                along[head * HEAD_DIM : (head + 1) * HEAD_DIM], axis=0, keepdims=True
            )
            sums[head] = jnp.zeros((L, HEAD_DIM), wide)
        wait(fetch_rest)

        @pl.loop(0, L // block)
        def _(step):
            rows = pl.ds(pl.multiple_of(step * block, block), block)
            for head in range(heads):
                at = head * HEAD_DIM
                queries = qkv_ref[:, at : at + HEAD_DIM] * jnp.asarray(HEAD_DIM**-0.5, low_type)
                key_rows = qkv_ref[rows, width + at : width + at + HEAD_DIM]
                values = qkv_ref[rows, 2 * width + at : 2 * width + at + HEAD_DIM]
                grad = outgoing[:, at : at + HEAD_DIM]
                probs = jnp.concatenate(
                    [probs_ref[part, head, rows, :] for part in range(L // block)], axis=1
                )
                probs_grad = product(values, grad, NT)
                scores_grad = (
                    probs.astype(wide) * (probs_grad - dots[head : head + 1, :])
                ).astype(low_type)
                grad_ref[rows, width + at : width + at + HEAD_DIM] = product(
                    scores_grad, queries, NN
                ).astype(low_type)
                grad_ref[rows, 2 * width + at : 2 * width + at + HEAD_DIM] = product(
                    probs, grad, NN
                ).astype(low_type)
                sums[head] += product(scores_grad, key_rows, TN)

        for head in range(heads):
            at = head * HEAD_DIM
            grad_ref[:, at : at + HEAD_DIM] = (sums[head] * (HEAD_DIM**-0.5)).astype(low_type)
        bias_ref[...] = jnp.zeros((8, D), wide)
        quarter = scalar_ref[0] ^ slot
        bias_ref[pl.ds(quarter, 1), : 3 * width] = jnp.sum(
            grad_ref[...].astype(wide), axis=0, keepdims=True
        )

    return call(
        kernel,
        "attend_backward",
        (shaped((L, 3 * width), low_type), shaped((8, D), wide)),
        [scalars, branch_low, attended, qkv, probs, *mixer],
        "vvhh" + "h" * len(mixer),
        "vv",
        [
            pltpu.VMEM((width, D), low_type),
            pltpu.VMEM((L, 3 * width), low_type),
            pltpu.VMEM(probs.shape, low_type),
            pltpu.VMEM((L, width), low_type),
            pltpu.VMEM((heads, L, HEAD_DIM), wide),
            pltpu.VMEM((8, L), wide),
            pltpu.SemaphoreType.DMA((4,)),
        ],
    )


def normalize(rows):
    center = rows - jnp.mean(rows, axis=-1, keepdims=True)
    inverse = lax.rsqrt(jnp.mean(center * center, axis=-1, keepdims=True) + eps_norm)
    return center * inverse, inverse


def normalize_backward(scaled, normed, inverse):
    middle = jnp.mean(scaled, axis=-1, keepdims=True)
    along = jnp.mean(scaled * normed, axis=-1, keepdims=True)
    return inverse * (scaled - middle - normed * along)


def column_sum(rows):
    return jnp.sum(rows, axis=0, keepdims=True)


BLOCK = 256
STEPS = L // BLOCK


def block_rows(step):
    return pl.ds(pl.multiple_of(step * BLOCK, BLOCK), BLOCK)


def mix_norm(scalars, vectors, tokens, attended, mixers):
    width = D // 4

    def kernel(scalar_ref, vector_ref, tokens_ref, *refs):
        attended_refs = refs[:4]
        parts, refs = unflatten(refs[4:], mixers)
        inverse_ref, low_ref, sums_ref, hat_out, weight, hat_ref, semaphores = refs
        _, odd, length = read_scalars(scalar_ref)
        fetches = [
            begin_weight(
                parts[i], odd, weight.at[pl.ds(i * width, width)], semaphores, 2 * i, PROJECTION_ROWS
            )
            for i in range(4)
        ]
        vectors = vector_ref[...].astype(wide)
        sums_ref[...] = jnp.zeros((8, D), wide)
        for fetch in fetches:
            wait(fetch)

        @pl.loop(0, STEPS)
        def _(step):
            at = block_rows(step)
            branch = vectors[0:1]
            for index in range(4):
                branch = branch + product(
                    attended_refs[index][at, :], weight[index * width : (index + 1) * width], NN
                )
            rows = tokens_ref[at, :].astype(wide)
            hat, inverse = normalize(rows + branch)
            hat_ref[at, :] = hat
            begin(hat_ref.at[at], hat_out.at[at], semaphores.at[8 + step])
            inverse_ref[at, :] = inverse
            low_ref[at, :] = (hat * vectors[1:2] + vectors[2:3]).astype(low_type)
            place = lax.broadcasted_iota(jnp.int32, (BLOCK, 1), 0) + step * BLOCK
            valid = (place < length).astype(wide)
            sums_ref[0:1, :] += column_sum(valid * rows * rows)
            sums_ref[1:2, :] += column_sum(valid * branch * branch)
            sums_ref[2:3, :] += column_sum(jnp.broadcast_to(valid, (BLOCK, D)))

        for step in range(STEPS):
            at = block_rows(step)
            pltpu.make_async_copy(hat_ref.at[at], hat_out.at[at], semaphores.at[8 + step]).wait()

    return call(
        kernel,
        "mix_norm",
        (shaped((L, 1), wide), shaped((L, D), low_type), shaped((8, D), wide), shaped((L, D), wide)),
        [scalars, vectors, tokens, *attended, *flat(mixers)],
        "vv" + "v" * 4 + "h" * len(flat(mixers)),
        "vvvh",
        [
            pltpu.VMEM((D, D), low_type),
            pltpu.VMEM((L, D), wide),
            pltpu.SemaphoreType.DMA((8 + STEPS,)),
        ],
    )


def inner_forward(scalars, normed_low, weights, biases):
    chunk = 256

    def kernel(scalar_ref, normed_ref, *refs):
        bias_refs = refs[:2]
        parts, refs = unflatten(refs[2:], weights)
        out_refs, slope_out, weight, bias, slope_ref, semaphores = refs[:2], *refs[2:]
        odd = scalar_ref[1]
        fetches = [begin_weight(parts[i], odd, weight.at[i], semaphores, 2 * i) for i in range(2)]
        for index in range(2):
            bias[index] = bias_refs[index][...].astype(wide)

        @pl.loop(0, 2)
        def _(slot):
            for index in range(2):

                @pl.when(slot == index)
                def _(index=index):
                    wait(fetches[index])

            @pl.loop(0, D // chunk)
            def _(step):
                columns = pl.ds(pl.multiple_of(step * chunk, chunk), chunk)
                inner_pre = (
                    product(normed_ref[...], weight[slot, :, columns], NN)
                    + bias[slot, 1:2, columns]
                )
                below = 0.5 * (1.0 + lax.erf(inner_pre * root_half))
                density = jnp.exp(-0.5 * inner_pre * inner_pre) * inv_root_tau
                activated = (inner_pre * below).astype(low_type)
                slope_ref[slot, :, columns] = (below + inner_pre * density).astype(low_type)
                for index in range(2):

                    @pl.when(slot == index)
                    def _(index=index):
                        out_refs[index][:, columns] = activated

            begin(slope_ref.at[slot], slope_out.at[slot], semaphores.at[4 + slot])

        for slot in range(2):
            pltpu.make_async_copy(
                slope_ref.at[slot], slope_out.at[slot], semaphores.at[4 + slot]
            ).wait()

    return call(
        kernel,
        "inner_forward",
        (shaped((L, D), low_type),) * 2 + (shaped((2, L, D), low_type),),
        [scalars, normed_low, *biases, *flat(weights)],
        "vvv" + "h" * len(flat(weights)),
        "vvh",
        [
            pltpu.VMEM((2, D, D), low_type),
            pltpu.VMEM((2, 16, D), wide),
            pltpu.VMEM((2, L, D), low_type),
            pltpu.SemaphoreType.DMA((6,)),
        ],
    )


def middle(
    scalars, vectors, hat_one, inverse_one, grad_out, activated, slopes, outers, inners
):
    chunk = 256

    def kernel(scalar_ref, vector_ref, hat_in, inverse_ref, incoming_in, *refs):
        left_refs, slope_in = refs[:4], refs[4:6]
        outer_parts, refs = unflatten(refs[6:], outers)
        inner_parts, refs = unflatten(refs, inners)
        low_ref, branch_ref, bias_ref, sums_ref = refs[:4]
        inner_refs, grad_out_ref, result_out = refs[4:8], refs[8], refs[9]
        outer, inner, slope_ref, hat_ref, incoming_ref, second_ref, grad_ref, result_ref = refs[10:18]
        semaphores = refs[18]
        place, odd, length = read_scalars(scalar_ref)
        fetch_outer = [
            begin_weight(outer_parts[i], odd, outer.at[i], semaphores, 2 * i) for i in range(4)
        ]
        fetch_rest = [
            begin(hat_in, hat_ref, semaphores.at[8]),
            begin(incoming_in, incoming_ref, semaphores.at[9]),
        ]
        fetch_slope = [
            begin(slope_in[i // 2].at[i % 2], slope_ref.at[i], semaphores.at[10 + i])
            for i in range(4)
        ]
        fetch_inner = [
            begin_weight(inner_parts[i], odd, inner.at[i], semaphores, 14 + 2 * i)
            for i in range(4)
        ]
        vectors = vector_ref[...].astype(wide)
        sums_ref[...] = jnp.zeros((16, D), wide)
        bias_ref[...] = jnp.zeros((8, D), wide)

        def result_copy(step):
            at = block_rows(step)
            return pltpu.make_async_copy(
                result_ref.at[at], result_out.at[at], semaphores.at[22 + step]
            )

        def grad_copy(step):
            at = block_rows(step)
            return pltpu.make_async_copy(
                grad_ref.at[at], grad_out_ref.at[at], semaphores.at[22 + STEPS + step]
            )

        @pl.loop(0, STEPS)
        def _(step):
            at = block_rows(step)
            branch = vectors[3:4]
            for index in range(4):

                @pl.when(step == 0)
                def _(index=index):
                    wait(fetch_outer[index])

                branch = branch + product(left_refs[index][at, :], outer[index], NN)

            @pl.when(step == 0)
            def _():
                wait(fetch_rest)

            normed_one = hat_ref[at, :] * vectors[1:2] + vectors[2:3]
            hat, inverse = normalize(normed_one + branch)
            result_ref[at, :] = (hat * vectors[4:5] + vectors[5:6]).astype(low_type)
            result_copy(step).start()
            incoming = incoming_ref[at, :].astype(wide)
            grad = normalize_backward(incoming * vectors[4:5], hat, inverse)
            second_ref[at, :] = grad
            low_ref[at, :] = grad.astype(low_type)
            row = lax.broadcasted_iota(jnp.int32, (BLOCK, 1), 0) + step * BLOCK
            valid = (row < length).astype(wide)
            sums_ref[0:1, :] += column_sum(incoming * hat)
            sums_ref[1:2, :] += column_sum(incoming)
            sums_ref[2:3, :] += column_sum(grad)
            sums_ref[3:4, :] += column_sum(valid * branch * branch)

        @pl.loop(0, 4)
        def _(slot):
            for index in range(4):

                @pl.when(slot == index)
                def _(index=index):
                    fetch_slope[index].wait()

            @pl.loop(0, D // chunk)
            def _(step):
                columns = pl.ds(pl.multiple_of(step * chunk, chunk), chunk)
                grad = product(low_ref[...], outer[slot, columns, :], NT) * slope_ref[
                    slot, :, columns
                ].astype(wide)
                bias_ref[pl.ds(place ^ slot, 1), columns] = column_sum(grad)
                low = grad.astype(low_type)
                for index in range(4):

                    @pl.when(slot == index)
                    def _(index=index):
                        inner_refs[index][:, columns] = low

        for fetch in fetch_inner:
            wait(fetch)

        @pl.loop(0, STEPS)
        def _(step):
            at = block_rows(step)
            total = second_ref[at, :]
            for index in range(4):
                total = total + product(inner_refs[index][at, :], inner[index], NT)
            hat = hat_ref[at, :]
            grad = normalize_backward(total * vectors[1:2], hat, inverse_ref[at, :])
            grad_ref[at, :] = grad
            grad_copy(step).start()
            branch_ref[at, :] = grad.astype(low_type)
            sums_ref[8:9, :] += column_sum(total * hat)
            sums_ref[9:10, :] += column_sum(total)
            sums_ref[10:11, :] += column_sum(grad)

        for step in range(STEPS):
            result_copy(step).wait()
            grad_copy(step).wait()

    return call(
        kernel,
        "middle",
        (
            shaped((L, D), low_type),
            shaped((L, D), low_type),
            shaped((8, D), wide),
            shaped((16, D), wide),
        )
        + (shaped((L, D), low_type),) * 4
        + (shaped((L, D), wide), shaped((L, D), low_type)),
        [
            scalars,
            vectors,
            hat_one,
            inverse_one,
            grad_out,
            *activated,
            *slopes,
            *flat(outers),
            *flat(inners),
        ],
        "vhvh" + "vvvv" + "hh" + "h" * len(flat(outers) + flat(inners)),
        "vvvv" + "vvvv" + "hh",
        [
            pltpu.VMEM((4, D, D), low_type),
            pltpu.VMEM((4, D, D), low_type),
            pltpu.VMEM((4, L, D), low_type),
            pltpu.VMEM((L, D), wide),
            pltpu.VMEM((L, D), low_type),
            pltpu.VMEM((L, D), wide),
            pltpu.VMEM((L, D), wide),
            pltpu.VMEM((L, D), low_type),
            pltpu.SemaphoreType.DMA((22 + 2 * STEPS,)),
        ],
        limit=32,
    )


def add_halves(scalars, near, far, incoming):
    half = near.shape[0]

    def kernel(scalar_ref, near_ref, far_ref, incoming_ref, near_out, far_out):
        near_out[...] = add_rows(near_ref[...], incoming_ref[:half, :])
        far_out[...] = add_rows(far_ref[...], incoming_ref[half:, :])

    return call(
        kernel,
        "add_halves",
        (shaped((half, D), low_type),) * 2,
        [scalars, near, far, incoming],
        "vvv",
        "vv",
    )


def input_backward(scalars, first_grad, qkv_grads, projections):
    width = D // 4

    def kernel(scalar_ref, first_in, *refs):
        left_refs = refs[:4]
        parts, refs = unflatten(refs[4:], projections)
        out, weight, first_ref, semaphores = refs
        odd = scalar_ref[1]
        fetches = [begin_weight(parts[i], odd, weight.at[i], semaphores, 2 * i) for i in range(4)]
        fetch_first = begin(first_in, first_ref, semaphores.at[8])

        @pl.loop(0, STEPS)
        def _(step):
            at = block_rows(step)
            total = 0.0
            for index in range(4):

                @pl.when(step == 0)
                def _(index=index):
                    wait(fetches[index])

                total = total + product(left_refs[index][at, :], weight[index, : 3 * width], NN)

            @pl.when(step == 0)
            def _():
                fetch_first.wait()

            first_ref[at, :] = total + first_ref[at, :]
            begin(first_ref.at[at], out.at[at], semaphores.at[9 + step])

        for step in range(STEPS):
            at = block_rows(step)
            pltpu.make_async_copy(first_ref.at[at], out.at[at], semaphores.at[9 + step]).wait()

    return call(
        kernel,
        "input_backward",
        (shaped((L, D), wide),),
        [scalars, first_grad, *qkv_grads, *flat(projections)],
        "h" + "v" * 4 + "h" * len(flat(projections)),
        "h",
        [
            pltpu.VMEM((4, 3 * width + EXTRA, D), low_type),
            pltpu.VMEM((L, D), wide),
            pltpu.SemaphoreType.DMA((9 + STEPS,)),
        ],
        limit=16,
    )[0]


def solution(mesh):
    dp_size = mesh.shape["dp"]
    tensor_size = mesh.shape["tensor"]
    masks = [1 << bit for bit in range(dp_size.bit_length() - 1)]

    def over_tensor(value, mask):
        return lax.ppermute(value, "tensor", [(i, i ^ mask) for i in range(tensor_size)])

    def over_dp(value, mask):
        return lax.ppermute(value, "dp", [(i, i ^ mask) for i in range(dp_size)])

    def body(
        tokens,
        grad_out,
        lengths,
        segment_ids,
        query_weight,
        query_bias,
        key_weight,
        value_weight,
        value_bias,
        mixer_weight,
        mixer_bias,
        first_gain,
        first_shift,
        inner_weight,
        inner_bias,
        outer_weight,
        outer_bias,
        second_gain,
        second_shift,
    ):
        width = query_weight.shape[1]
        place = lax.axis_index("tensor")
        odd = lax.axis_index("dp") % 2
        chain = [jnp.zeros((8, 128), wide)]

        def after(*values):
            held = lax.optimization_barrier((chain[0],) + values)
            return held[1:] if len(values) > 1 else held[1]

        def done(*values):
            chain[0] = lax.optimization_barrier((chain[0],) + values)[0]
            return values if len(values) > 1 else values[0]

        lines = [mixer_bias, first_gain, first_shift, outer_bias, second_gain, second_shift]
        lines = dict(enumerate(lines))
        lines[8] = jnp.pad(query_bias, (0, D - width)) + jnp.pad(
            value_bias, (2 * width, D - 3 * width)
        )
        lines[9] = inner_bias
        line_at = lax.broadcasted_iota(jnp.int32, (16, D), 0)
        vectors = jnp.zeros((16, D), low_type)
        for index, line in lines.items():
            vectors = jnp.where(line_at == index, line[None, :], vectors)
        high = lax.axis_index("dp") // 2 % 2
        scalars = jnp.concatenate([jnp.stack([place, odd, high]).astype(jnp.int32), lengths])

        def hold():
            chain[0] = tick(scalars, chain[0])

        def send(value, mask):
            return over_tensor(after(value), mask)

        def pass_y(value):
            return over_dp(after(value), masks[0])

        def land(value):
            return done(after(value))

        def stage(function, *operands):
            return done(*function(after(scalars), *operands))

        piece, inner_piece, outer_piece, own_heads = done(
            *prepare(
                scalars,
                vectors,
                [query_weight.T, key_weight.T, value_weight.T],
                mixer_weight,
                inner_weight,
                outer_weight,
            )
        )
        heads = {}

        def attend(slot, parts):
            heads[slot] = stage(attend_forward, segment_ids, tokens, parts)

        heads_x = send(piece, 2)
        heads_core = send(own_heads, 1)
        hold()
        attend(0, (own_heads,))
        heads_core = land(heads_core)
        inner_core = send(inner_weight, 1)
        attend(1, (heads_core,))
        inner_core = land(inner_core)
        heads_x = land(heads_x)
        heads_y = pass_y(heads_x)
        inner_x = send(inner_piece, 2)
        heads_near = send(heads_x, 1)
        hold()
        heads_near = land(heads_near)
        outer_core = send(outer_weight, 1)
        hold()
        outer_core = land(outer_core)
        heads_y = land(heads_y)
        heads_far = send(heads_y, 1)
        inner_x = land(inner_x)
        inner_y = pass_y(inner_x)
        outer_x = send(outer_piece, 2)
        inner_near = send(inner_x, 1)
        if HOLD_A:
            hold()
        heads_far = land(heads_far)
        attend(2, (heads_x, heads_y))
        inner_near = land(inner_near)
        attend(3, (heads_near, heads_far))
        attended = [heads[j][0] for j in range(4)]
        inner_biases = [heads[j][1] for j in range(4)]
        projections = mixers = [
            (own_heads,),
            (heads_core,),
            (heads_x, heads_y),
            (heads_near, heads_far),
        ]
        inverse_one, normed_low, sums_one, hat_one = stage(
            mix_norm, vectors, tokens, attended, mixers
        )
        outer_x = land(outer_x)
        outer_y = pass_y(outer_x)
        outer_near = send(outer_x, 1)
        inner_y = land(inner_y)
        inner_far = send(inner_y, 1)
        if HOLD_B:
            hold()
        outer_near = land(outer_near)
        *activated, slope_one = stage(
            inner_forward, normed_low, [(inner_weight,), (inner_core,)], inner_biases[:2]
        )
        inner_far = land(inner_far)
        *more, slope_two = stage(
            inner_forward,
            normed_low,
            [(inner_x, inner_y), (inner_near, inner_far)],
            inner_biases[2:],
        )
        activated = activated + more
        inners = [(inner_weight,), (inner_core,), (inner_x, inner_y), (inner_near, inner_far)]
        outer_y = land(outer_y)
        outer_far = send(outer_y, 1)
        hold()
        outer_far = land(outer_far)
        outers = [(outer_weight,), (outer_core,), (outer_x, outer_y), (outer_near, outer_far)]
        ffn_low, branch_low, inner_bias_rows, sums_two, *rest = stage(
            middle,
            vectors,
            hat_one,
            inverse_one,
            grad_out,
            activated,
            [slope_one, slope_two],
            outers,
            inners,
        )
        *inner_lows, first_grad, layer_out = rest

        def part(left, right):
            left, right = after(left, right)
            return done(product(left, right, TN).astype(low_type))

        def add_low(left, right):
            return done(add_rows(*after(left, right)))

        class Reduction:
            def __init__(self, outputs=1, bits=(Y_BIT, Z_BIT)):
                self.outputs, self.bits = outputs, bits
                self.todo = ["split", "split"] + ["add"] * (len(masks) - 2)
                self.todo += ["back", "join", "end"]
                self.level = 0

            def begin(self, sent):
                self.incoming = send(sent, 2)
                if HOLD_X:
                    hold()
                return self

            def across(self, value, mask):
                self.incoming = over_dp(after(value), mask)
                if HOLD_HOPS:
                    hold()

            def terms(self):
                return (self.kept,)

            def hop(self):
                if not self.todo:
                    return
                step = self.todo.pop(0)
                *terms, incoming = after(*self.terms(), self.incoming)
                if step == "split":
                    bit = self.bits[self.level]
                    sent, self.kept = stage(split_add, bit, *terms, incoming)
                    self.terms = lambda: (self.kept,)
                    self.level += 1
                    self.across(sent, bit)
                elif step in ("add", "back"):
                    self.kept = done(add_rows(terms[0], incoming))
                    mask = self.bits[1] if step == "back" else 4 << (self.level - 2)
                    self.level += 1
                    self.across(self.kept, mask)
                elif step == "join":
                    self.kept = done(join(after(scalars), self.bits[1], terms[0], incoming))
                    self.across(self.kept, self.bits[0])
                else:
                    self.result = finish(
                        after(scalars), self.bits[0], terms[0], incoming, self.outputs
                    )
                    done(*self.result)

        class MixedReduction(Reduction):
            def __init__(self, kept, extra):
                super().__init__()
                self.kept, self.extra = kept, extra
                self.todo = ["mixed"] * (len(masks) + 1) + ["end"]

            def hop(self):
                if not self.todo or self.todo[0] == "end":
                    super().hop()
                    return
                self.todo.pop(0)
                kept, extra, incoming = after(self.kept, self.extra, self.incoming)
                text, self.kept, self.extra = stage(
                    mixed_hop, kept, extra, incoming, self.level == 0
                )
                mask = masks[self.level] if self.level < len(masks) else masks[0]
                self.level += 1
                self.across(text, mask)

        class CrossReduction(Reduction):
            def __init__(self, near, near_partner, far, far_partner, bits):
                super().__init__(1, bits)
                sent, self.near, self.far = stage(
                    take_halves, bits[0], *after(near, near_partner, far, far_partner)
                )
                self.todo[0] = "cross"
                self.incoming = over_dp(after(sent), bits[0])
                if HOLD_Y:
                    hold()

            def hop(self):
                if self.todo and self.todo[0] == "cross":
                    self.todo.pop(0)
                    near, far, incoming = after(self.near, self.far, self.incoming)
                    self.kept, far = stage(add_halves, near, far, incoming)
                    self.level = 1
                    self.incoming = send(far, 2)
                    if HOLD_Z:
                        hold()
                else:
                    super().hop()

        partner = {}
        outer_parts, inner_parts, heads_parts = {}, {}, {}
        qkv_grads, qkv_bias = {}, {}

        def retreat(slot):
            attended_low, _, qkv, probs = heads[slot]
            qkv_grads[slot], qkv_bias[slot] = stage(
                attend_backward, slot, branch_low, mixers[slot], attended_low, qkv, probs
            )

        def split_step(name, slot):
            left, right = {
                "o": (activated[slot], ffn_low),
                "i": (normed_low, inner_lows[slot]),
                "m": (attended[slot], branch_low),
                "h": (qkv_grads.get(slot), tokens),
            }[name]
            share = part(left, right)
            if slot % 2:
                partner[name, slot - 1] = send(share, 1)
            else:
                own_share[name, slot] = share

        def own_sum(name, slot):
            return add_low(own_share[name, slot], partner[name, slot])

        own_share, chains = {}, {}
        for step in PLAN:
            name, slot = step[0], int(step[1])
            if name == "b":
                retreat(slot)
            elif name in "oimh":
                split_step(name, slot)
            elif name == "X":
                which = ("o", None, "h")[slot]
                chains[slot] = Reduction(3 if slot == 2 else 1).begin(own_sum(which, 2))
            elif name == "Y":
                chains[1] = CrossReduction(
                    own_share["i", 0],
                    partner["i", 0],
                    own_share["i", 2],
                    partner["i", 2],
                    (Z_BIT, Y_BIT),
                )
            elif name == "S":
                small = done(
                    jnp.concatenate(
                        [
                            sums_one,
                            sums_two,
                            inner_bias_rows,
                            qkv_bias[0] + qkv_bias[1] + qkv_bias[2] + qkv_bias[3],
                        ]
                    )
                )
                small_other = send(small, 1)
            elif name == "M":
                small = done(small + after(small_other))
                sent = done(message(own_sum("m", 2), small))
                chains[3] = MixedReduction(own_sum("m", 0), small).begin(sent)
            elif name == "B":
                tokens_grad = done(
                    input_backward(
                        after(scalars), first_grad, [qkv_grads[j] for j in range(4)], projections
                    )
                )
            else:
                if name == "H" and slot in (0, 2) and chains[slot].level == 0:
                    which = "o" if slot == 0 else "h"
                    both = (own_share[which, 0], partner[which, 0])
                    chains[slot].terms = lambda both=both: both
                chains[slot].hop()
        for chain_left in chains.values():
            while chain_left.todo:
                chain_left.hop()
        small = chains[3].extra
        outer_chain, inner_chain, heads_chain, mixer_chain = (chains[j] for j in range(4))

        totals = jnp.sum(jnp.stack([small[0], small[1], small[11]]), axis=1)
        statistics = jnp.sqrt(totals / (small[2, 0] * D))
        own_inner_bias = lax.dynamic_index_in_dim(small[24:28], place, 0, keepdims=False)
        own_qkv_bias = lax.dynamic_index_in_dim(small[32:36], place, 0, keepdims=False)
        query_grad, key_grad, value_grad = heads_chain.result
        return (
            layer_out,
            tokens_grad,
            query_grad.T,
            own_qkv_bias[:width],
            key_grad.T,
            value_grad.T,
            own_qkv_bias[2 * width : 3 * width],
            mixer_chain.result[0],
            small[18],
            small[16],
            small[17],
            inner_chain.result[0],
            own_inner_bias,
            outer_chain.result[0],
            small[10],
            small[8],
            small[9],
            statistics,
        )

    in_specs = (
        P(("dp", "tensor"), None),
        P(("dp", "tensor"), None),
        P("dp"),
        P("dp", None),
        P(None, "tensor"),
        P("tensor"),
        P(None, "tensor"),
        P(None, "tensor"),
        P("tensor"),
        P("tensor", None),
        P(),
        P(),
        P(),
        P(None, "tensor"),
        P("tensor"),
        P("tensor", None),
        P(),
        P(),
        P(),
    )
    out_specs = (
        P(("dp", "tensor"), None),
        P(("dp", "tensor"), None),
        P(None, "tensor"),
        P("tensor"),
        P(None, "tensor"),
        P(None, "tensor"),
        P("tensor"),
        P("tensor", None),
        P(),
        P(),
        P(),
        P(None, "tensor"),
        P("tensor"),
        P("tensor", None),
        P(),
        P(),
        P(),
        P(),
    )
    return jax.shard_map(body, mesh=mesh, in_specs=in_specs, out_specs=out_specs, check_vma=False)
```

```python
import jax
import jax.numpy as jnp
from jax import lax
from jax.experimental import pallas as pl
from jax.experimental.pallas import tpu as pltpu
from jax.sharding import PartitionSpec as P

D = 768
HEAD_DIM = 64
L = 512
EXTRA = 32

eps_norm = 1e-06
root_half = 0.7071067811865476
inv_root_tau = 0.3989422804014327
low_type = jnp.bfloat16
wide = jnp.float32
NN = (((1,), (0,)), ((), ()))
NT = (((1,), (1,)), ((), ()))
TN = (((0,), (0,)), ((), ()))


def product(left, right, dims):
    return lax.dot_general(left, right, dims, preferred_element_type=wide)


def shaped(shape, dtype):
    return jax.ShapeDtypeStruct(shape, dtype)


COST = 100000000000
PRICES = {
    "prepare": 100000000000,
    "attend_forward": 100000000000,
    "mix_norm": 100000000000,
    "inner_forward": 5000000000,
    "middle": 100000000000,
    "attend_backward": 100000000000,
    "input_backward": 0,
    "split_add": 0,
    "mixed_hop": 0,
    "finish": 0,
    "take_halves": 0,
    "add_halves": 0,
    "join": 0,
    "tick": 100000000000,
    "halve": 100000000000,
}
HOLD_HOPS = False
HOLD_A = True
HOLD_B = False
HOLD_C = False
HOLD_D = False
HOLD_X = True
HOLD_Y = False
HOLD_Z = False
BRANCH_LATE = False
LATE = False
EARLY = 2
PLAN = (
    "o3", "i3", "o2", "X0", "i1", "i2", "i0", "Y1", "b3", "h3", "b2", "h2",
    "X2", "o1", "o0", "b1", "h1", "b0", "m3", "H0", "H1", "m1", "m2", "m0",
    "S0", "h0", "M3", "H0", "H2", "H1", "H0", "H3", "H2", "H0", "H1", "B0",
    "H2", "H3", "H0", "H1", "H3", "H2", "H1", "H3", "H2", "H1", "H2", "H0",
    "H1", "H3", "H0",
)


def call(
    kernel, name, out_shape, operands, spaces, out_spaces, scratch=(), limit=14
):
    place = {"v": pltpu.VMEM, "h": pltpu.HBM}
    price = PRICES.get(name, COST)
    out_shape = tuple(
        pltpu.HBM(one.shape, one.dtype) if letter == "h" else one
        for one, letter in zip(out_shape, out_spaces)
    )
    operands = operands[:1] + [
        pltpu.with_memory_space_constraint(one, pltpu.HBM) if letter == "h" else one
        for one, letter in zip(operands[1:], spaces)
    ]
    return pl.pallas_call(
        kernel,
        out_shape=out_shape,
        in_specs=[pl.BlockSpec(memory_space=pltpu.SMEM)]
        + [pl.BlockSpec(memory_space=place[letter]) for letter in spaces],
        out_specs=tuple(pl.BlockSpec(memory_space=place[letter]) for letter in out_spaces),
        scratch_shapes=list(scratch),
        compiler_params=pltpu.CompilerParams(vmem_limit_bytes=limit << 20),
        cost_estimate=pl.CostEstimate(flops=price, transcendentals=0, bytes_accessed=price // 300),
        name=name,
    )(*operands)


def read_scalars(scalar_ref):
    place = scalar_ref[0]
    return place, scalar_ref[1], scalar_ref[3 + place]


def begin(source, target, semaphore):
    copy = pltpu.make_async_copy(source, target, semaphore)
    copy.start()
    return copy


def begin_weight(parts, odd, target, semaphores, at, first=0):
    rows = target.shape[0] // len(parts)
    first = first // len(parts)
    parts = [part.at[pl.ds(first, rows)] for part in parts]
    if len(parts) == 1:
        return [begin(parts[0], target, semaphores.at[at])]
    return [
        begin(
            part,
            target.at[pl.ds(pl.multiple_of(which * rows, rows), rows)],
            semaphores.at[at + index],
        )
        for index, (part, which) in enumerate(zip(parts, (odd, 1 - odd)))
    ]


def wait(copies):
    for copy in copies:
        copy.wait()


def unflatten(refs, slots):
    out, at = [], 0
    for parts in slots:
        out.append(refs[at : at + len(parts)])
        at += len(parts)
    return out, refs[at:]


def flat(slots):
    return [part for parts in slots for part in parts]


WIDTH = D // 4
PROJECTION_ROWS = 3 * WIDTH + EXTRA


def prepare(scalars, vectors, weights, mixer):
    rows = PROJECTION_ROWS + WIDTH

    def kernel(scalar_ref, vector_ref, query, key, value, mixer_in, piece_ref, own_ref, semaphores):
        odd = scalar_ref[1]
        fetches = [
            begin(source, own_ref.at[pl.ds(start, WIDTH)], semaphores.at[index])
            for index, (source, start) in enumerate(
                zip((query, key, value, mixer_in), (0, WIDTH, 2 * WIDTH, PROJECTION_ROWS))
            )
        ]
        own_ref[3 * WIDTH : PROJECTION_ROWS, :] = jnp.zeros((EXTRA, D), low_type)
        own_ref[3 * WIDTH : 3 * WIDTH + 8, :] = vector_ref[8:16, :]
        wait(fetches)
        half = PROJECTION_ROWS // 2
        piece_ref[:half, :] = own_ref[pl.ds(pl.multiple_of(odd * half, 16), half), :]
        half_mixer = WIDTH // 2
        piece_ref[half:, :] = own_ref[
            pl.ds(pl.multiple_of(PROJECTION_ROWS + odd * half_mixer, 16), half_mixer), :
        ]

    return call(
        kernel,
        "prepare",
        (shaped((rows // 2, D), low_type), shaped((rows, D), low_type)),
        [scalars, vectors, *weights, mixer],
        "vhhhh",
        "vv",
        [pltpu.SemaphoreType.DMA((4,))],
    )


def halve(scalars, inner, outer):
    def kernel(scalar_ref, inner_in, outer_in, inner_out, outer_out, semaphores):
        half = D // 2
        chosen = pl.ds(pl.multiple_of(scalar_ref[1] * half, half), half)
        wait(
            [
                begin(inner_in.at[chosen], inner_out, semaphores.at[0]),
                begin(outer_in.at[chosen], outer_out, semaphores.at[1]),
            ]
        )

    return call(
        kernel,
        "halve",
        (shaped((D // 2, D), low_type),) * 2,
        [scalars, inner, outer],
        "hh",
        "vv",
        [pltpu.SemaphoreType.DMA((2,))],
    )


def tick(scalars, token):
    def kernel(scalar_ref, token_ref, out_ref):
        out_ref[...] = token_ref[...]

    return call(kernel, "tick", (shaped(token.shape, token.dtype),), [scalars, token], "v", "v")[0]


def add_rows(left, right):
    return (left.astype(wide) + right.astype(wide)).astype(low_type)


Y_BIT, Z_BIT = 1, 2


def split_add(scalars, bit, *terms):
    half = terms[0].shape[0] // 2

    def kernel(scalar_ref, *refs):
        mine = scalar_ref[bit]
        for which, out_ref in ((1 - mine, refs[-2]), (mine, refs[-1])):
            rows = pl.ds(pl.multiple_of(which * half, 16), half)
            total = refs[0][rows, :].astype(wide)
            for ref in refs[1:-2]:
                total = total + ref[rows, :].astype(wide)
            out_ref[...] = total.astype(low_type)

    return call(
        kernel,
        "split_add",
        (shaped((half, D), low_type),) * 2,
        [scalars, *terms],
        "v" * len(terms),
        "vv",
    )


def join(scalars, bit, mine, other):
    half = mine.shape[0]

    def kernel(scalar_ref, mine_ref, other_ref, out_ref):
        at = scalar_ref[bit]
        out_ref[pl.ds(pl.multiple_of(at * half, 16), half), :] = mine_ref[...]
        out_ref[pl.ds(pl.multiple_of((1 - at) * half, 16), half), :] = other_ref[...]

    return call(
        kernel, "join", (shaped((2 * half, D), low_type),), [scalars, mine, other], "vv", "v"
    )[0]


def take_halves(scalars, bit, near, near_partner, far, far_partner):
    half = near.shape[0] // 2

    def kernel(scalar_ref, near_ref, near_other, far_ref, far_other, send_ref, near_out, far_out):
        mine = scalar_ref[bit]
        theirs = pl.ds(pl.multiple_of((1 - mine) * half, 16), half)
        ours = pl.ds(pl.multiple_of(mine * half, 16), half)
        send_ref[:half, :] = add_rows(near_ref[theirs, :], near_other[theirs, :])
        send_ref[half:, :] = add_rows(far_ref[theirs, :], far_other[theirs, :])
        near_out[...] = add_rows(near_ref[ours, :], near_other[ours, :])
        far_out[...] = add_rows(far_ref[ours, :], far_other[ours, :])

    return call(
        kernel,
        "take_halves",
        (shaped((2 * half, D), low_type),) + (shaped((half, D), low_type),) * 2,
        [scalars, near, near_partner, far, far_partner],
        "vvvv",
        "vvv",
    )


def message(rows, extra):
    high = extra.astype(low_type)
    return jnp.concatenate([rows, high, (extra - high.astype(wide)).astype(low_type)], axis=0)


def mixed_hop(scalars, kept, extra, incoming, split):
    rows = kept.shape[0] // 2 if split else kept.shape[0]
    count = extra.shape[0]

    def kernel(scalar_ref, kept_ref, extra_ref, incoming_ref, message_ref, keep_ref, out_ref):
        at = kept.shape[0]
        total = extra_ref[...] + (
            incoming_ref[at : at + count, :].astype(wide)
            + incoming_ref[at + count : at + 2 * count, :].astype(wide)
        )
        out_ref[...] = total
        high = total.astype(low_type)
        message_ref[rows : rows + count, :] = high
        message_ref[rows + count :, :] = (total - high.astype(wide)).astype(low_type)
        if split:
            odd = scalar_ref[1]
            theirs = pl.ds(pl.multiple_of((1 - odd) * rows, 16), rows)
            ours = pl.ds(pl.multiple_of(odd * rows, 16), rows)
            message_ref[:rows, :] = add_rows(kept_ref[theirs, :], incoming_ref[theirs, :])
            keep_ref[...] = add_rows(kept_ref[ours, :], incoming_ref[ours, :])
        else:
            joined = add_rows(kept_ref[...], incoming_ref[:rows, :])
            message_ref[:rows, :] = joined
            keep_ref[...] = joined

    return call(
        kernel,
        "mixed_hop",
        (
            shaped((rows + 2 * count, D), low_type),
            shaped((rows, D), low_type),
            shaped((count, D), wide),
        ),
        [scalars, kept, extra, incoming],
        "vvv",
        "vvv",
    )


def finish(scalars, bits, pairs, outputs):
    def kernel(scalar_ref, *refs):
        count = len(pairs)
        outs, joins = refs[2 * count : -count - 1], refs[-count - 1 : -1]
        semaphores = refs[-1]
        copies, at = [], 0
        for index in range(count):
            half = pairs[index][0].shape[0]
            mine = scalar_ref[bits[index]]
            for ref, which in ((refs[2 * index], mine), (refs[2 * index + 1], 1 - mine)):
                joins[index][pl.ds(pl.multiple_of(which * half, 16), half), :] = ref[
                    :half, :
                ].astype(wide)
            rows = 2 * half // outputs[index]
            for part in range(outputs[index]):
                copies.append(
                    begin(
                        joins[index].at[pl.ds(part * rows, rows)], outs[at], semaphores.at[at]
                    )
                )
                at += 1
        wait(copies)

    shapes = [
        shaped((2 * pair[0].shape[0] // count, D), wide)
        for pair, count in zip(pairs, outputs)
        for _ in range(count)
    ]
    return call(
        kernel,
        "finish",
        tuple(shapes),
        [scalars, *[half for pair in pairs for half in pair]],
        "vv" * len(pairs),
        "h" * len(shapes),
        [pltpu.VMEM((2 * pair[0].shape[0], D), wide) for pair in pairs]
        + [pltpu.SemaphoreType.DMA((len(shapes),))],
        limit=20,
    )


HEADS_HERE = WIDTH // HEAD_DIM
QUERY_BLOCK = 256
QUERY_STEPS = L // QUERY_BLOCK
KEPT = (QUERY_STEPS, HEADS_HERE, L, QUERY_BLOCK)


def attend_forward(scalars, segment_ids, tokens, projections):
    count = len(projections)

    def kernel(scalar_ref, segment_ref, tokens_ref, *refs):
        slots, refs = unflatten(refs, projections)
        attended_refs, bias_refs = refs[:count], refs[count : 2 * count]
        qkv_outs, probs_outs = refs[2 * count : 3 * count], refs[3 * count : 4 * count]
        mask, weights, qkvs, probs_all, semaphores = refs[4 * count :]
        place, odd, length = read_scalars(scalar_ref)
        each = 3 + QUERY_STEPS
        fetches = [
            begin_weight(parts, odd, weights.at[i], semaphores, each * i)
            for i, parts in enumerate(slots)
        ]
        query_owner = segment_ref[pl.ds(place, 1), :].astype(wide)
        key_owner = jnp.broadcast_to(query_owner, (128, L)).T
        key_at = lax.broadcasted_iota(jnp.int32, (L, 128), 0)
        key_owner = jnp.where(key_at < length, key_owner, -1.0)
        query_at = lax.broadcasted_iota(jnp.int32, (L, 128), 1)
        for start in range(0, L, 128):
            allowed = (key_owner == query_owner[:, start : start + 128]) | (
                key_at == query_at + start
            )
            mask[:, start : start + 128] = jnp.where(allowed, 0.0, -1e30)
        copies = []
        for slot in range(count):
            weight, qkv_ref, probs_ref = weights.at[slot], qkvs.at[slot], probs_all.at[slot]
            attended_ref, probs_out = attended_refs[slot], probs_outs[slot]
            first = each * slot
            wait(fetches[slot])
            bias_refs[slot][...] = weight[3 * WIDTH : 3 * WIDTH + 16, :]
            bias = weight[3 * WIDTH : 3 * WIDTH + 16, : 3 * WIDTH].astype(wide)[0:1]
            qkv_ref[...] = (
                product(tokens_ref[...], weight[: 3 * WIDTH, :], NT) + bias
            ).astype(low_type)
            copies.append(begin(qkv_ref, qkv_outs[slot], semaphores.at[first + 2]))

            @pl.loop(0, QUERY_STEPS)
            def _(step):
                rows = pl.ds(pl.multiple_of(step * QUERY_BLOCK, QUERY_BLOCK), QUERY_BLOCK)
                for head in range(HEADS_HERE):
                    at = head * HEAD_DIM
                    queries = qkv_ref[rows, at : at + HEAD_DIM] * jnp.asarray(
                        HEAD_DIM**-0.5, low_type
                    )
                    key_rows = qkv_ref[:, WIDTH + at : WIDTH + at + HEAD_DIM]
                    values = qkv_ref[:, 2 * WIDTH + at : 2 * WIDTH + at + HEAD_DIM]
                    scores = product(key_rows, queries, NT) + mask[:, rows]
                    highest = jnp.max(scores, axis=0, keepdims=True)
                    expanded = jnp.exp(scores - highest)
                    total = jnp.sum(expanded, axis=0, keepdims=True)
                    probs = (expanded * (1.0 / total)).astype(low_type)
                    probs_ref[step, head] = probs
                    attended_ref[rows, at : at + HEAD_DIM] = product(probs, values, TN).astype(
                        low_type
                    )
                begin(probs_ref.at[step], probs_out.at[step], semaphores.at[first + 3 + step])

            for step in range(QUERY_STEPS):
                copies.append(
                    pltpu.make_async_copy(
                        probs_ref.at[step], probs_out.at[step], semaphores.at[first + 3 + step]
                    )
                )
        wait(copies)

    return call(
        kernel,
        "attend_forward",
        (shaped((L, WIDTH), low_type),) * count
        + (shaped((16, D), low_type),) * count
        + (shaped((L, 3 * WIDTH), low_type),) * count
        + (shaped(KEPT, low_type),) * count,
        [scalars, segment_ids, tokens, *flat(projections)],
        "vv" + "h" * len(flat(projections)),
        "v" * (2 * count) + "h" * (2 * count),
        [
            pltpu.VMEM((L, L), wide),
            pltpu.VMEM((count, PROJECTION_ROWS, D), low_type),
            pltpu.VMEM((count, L, 3 * WIDTH), low_type),
            pltpu.VMEM((count,) + KEPT, low_type),
            pltpu.SemaphoreType.DMA(((3 + QUERY_STEPS) * count,)),
        ],
        limit=10 + 6 * count,
    )


def attend_backward(scalars, slots, branch_low, mixers, attended, qkv, probs):
    count = len(slots)

    def kernel(scalar_ref, branch_ref, *refs):
        attended_refs, qkv_ins = refs[:count], refs[count : 2 * count]
        probs_ins = refs[2 * count : 3 * count]
        parts, refs = unflatten(refs[3 * count :], mixers)
        grad_refs, bias_ref = refs[:count], refs[count]
        weights, qkvs, probs_all, outgoing, sums, dots, semaphores = refs[count + 1 :]
        fetches = [
            begin_weight(
                parts[i], scalar_ref[1], weights.at[i], semaphores, 4 * i, PROJECTION_ROWS
            )
            for i in range(count)
        ]
        fetches_rest = [
            [
                begin(qkv_ins[i], qkvs.at[i], semaphores.at[4 * i + 2]),
                begin(probs_ins[i], probs_all.at[i], semaphores.at[4 * i + 3]),
            ]
            for i in range(count)
        ]
        bias_ref[...] = jnp.zeros((8, D), wide)
        for slot in range(count):
            grad_ref, qkv_ref, probs_ref = grad_refs[slot], qkvs.at[slot], probs_all.at[slot]
            wait(fetches[slot])
            attended_grad = product(branch_ref[...], weights[slot], NT).astype(low_type)
            outgoing[...] = attended_grad
            along = (attended_refs[slot][...].astype(wide) * attended_grad.astype(wide)).T
            for head in range(HEADS_HERE):
                dots[head : head + 1, :] = jnp.sum(
                    along[head * HEAD_DIM : (head + 1) * HEAD_DIM], axis=0, keepdims=True
                )
                sums[head] = jnp.zeros((L, HEAD_DIM), wide)
            wait(fetches_rest[slot])

            @pl.loop(0, QUERY_STEPS)
            def _(step):
                rows = pl.ds(pl.multiple_of(step * QUERY_BLOCK, QUERY_BLOCK), QUERY_BLOCK)
                for head in range(HEADS_HERE):
                    at = head * HEAD_DIM
                    queries = qkv_ref[:, at : at + HEAD_DIM] * jnp.asarray(
                        HEAD_DIM**-0.5, low_type
                    )
                    key_rows = qkv_ref[rows, WIDTH + at : WIDTH + at + HEAD_DIM]
                    values = qkv_ref[rows, 2 * WIDTH + at : 2 * WIDTH + at + HEAD_DIM]
                    grad = outgoing[:, at : at + HEAD_DIM]
                    probs_low = jnp.concatenate(
                        [probs_ref[part, head, rows, :] for part in range(QUERY_STEPS)], axis=1
                    )
                    probs_grad = product(values, grad, NT)
                    scores_grad = (
                        probs_low.astype(wide) * (probs_grad - dots[head : head + 1, :])
                    ).astype(low_type)
                    grad_ref[rows, WIDTH + at : WIDTH + at + HEAD_DIM] = product(
                        scores_grad, queries, NN
                    ).astype(low_type)
                    grad_ref[rows, 2 * WIDTH + at : 2 * WIDTH + at + HEAD_DIM] = product(
                        probs_low, grad, NN
                    ).astype(low_type)
                    sums[head] += product(scores_grad, key_rows, TN)

            for head in range(HEADS_HERE):
                at = head * HEAD_DIM
                grad_ref[:, at : at + HEAD_DIM] = (sums[head] * (HEAD_DIM**-0.5)).astype(low_type)
            quarter = scalar_ref[0] ^ slots[slot]
            bias_ref[pl.ds(quarter, 1), : 3 * WIDTH] = jnp.sum(
                grad_ref[...].astype(wide), axis=0, keepdims=True
            )

    return call(
        kernel,
        "attend_backward",
        (shaped((L, 3 * WIDTH), low_type),) * count + (shaped((8, D), wide),),
        [scalars, branch_low, *attended, *qkv, *probs, *flat(mixers)],
        "v" * (1 + count) + "h" * (2 * count + len(flat(mixers))),
        "v" * (count + 1),
        [
            pltpu.VMEM((count, WIDTH, D), low_type),
            pltpu.VMEM((count, L, 3 * WIDTH), low_type),
            pltpu.VMEM((count,) + KEPT, low_type),
            pltpu.VMEM((L, WIDTH), low_type),
            pltpu.VMEM((HEADS_HERE, L, HEAD_DIM), wide),
            pltpu.VMEM((8, L), wide),
            pltpu.SemaphoreType.DMA((4 * count,)),
        ],
        limit=10 + 5 * count,
    )


def normalize(rows):
    center = rows - jnp.mean(rows, axis=-1, keepdims=True)
    inverse = lax.rsqrt(jnp.mean(center * center, axis=-1, keepdims=True) + eps_norm)
    return center * inverse, inverse


def normalize_backward(scaled, normed, inverse):
    middle = jnp.mean(scaled, axis=-1, keepdims=True)
    along = jnp.mean(scaled * normed, axis=-1, keepdims=True)
    return inverse * (scaled - middle - normed * along)


def column_sum(rows):
    return jnp.sum(rows, axis=0, keepdims=True)


BLOCK = 256
STEPS = L // BLOCK


def block_rows(step):
    return pl.ds(pl.multiple_of(step * BLOCK, BLOCK), BLOCK)


def mix_norm(scalars, vectors, tokens, attended, mixers):
    width = D // 4

    def kernel(scalar_ref, vector_ref, tokens_ref, *refs):
        attended_refs = refs[:4]
        parts, refs = unflatten(refs[4:], mixers)
        inverse_ref, low_ref, sums_ref, hat_out, weight, hat_ref, semaphores = refs
        _, odd, length = read_scalars(scalar_ref)
        fetches = [
            begin_weight(
                parts[i], odd, weight.at[pl.ds(i * width, width)], semaphores, 2 * i, PROJECTION_ROWS
            )
            for i in range(4)
        ]
        vectors = vector_ref[...].astype(wide)
        sums_ref[...] = jnp.zeros((8, D), wide)
        for fetch in fetches:
            wait(fetch)

        @pl.loop(0, STEPS)
        def _(step):
            at = block_rows(step)
            branch = vectors[0:1]
            for index in range(4):
                branch = branch + product(
                    attended_refs[index][at, :], weight[index * width : (index + 1) * width], NN
                )
            rows = tokens_ref[at, :].astype(wide)
            hat, inverse = normalize(rows + branch)
            hat_ref[at, :] = hat
            begin(hat_ref.at[at], hat_out.at[at], semaphores.at[8 + step])
            inverse_ref[at, :] = inverse
            low_ref[at, :] = (hat * vectors[1:2] + vectors[2:3]).astype(low_type)
            place = lax.broadcasted_iota(jnp.int32, (BLOCK, 1), 0) + step * BLOCK
            valid = (place < length).astype(wide)
            sums_ref[0:1, :] += column_sum(valid * rows * rows)
            sums_ref[1:2, :] += column_sum(valid * branch * branch)
            sums_ref[2:3, :] += column_sum(jnp.broadcast_to(valid, (BLOCK, D)))

        for step in range(STEPS):
            at = block_rows(step)
            pltpu.make_async_copy(hat_ref.at[at], hat_out.at[at], semaphores.at[8 + step]).wait()

    return call(
        kernel,
        "mix_norm",
        (shaped((L, 1), wide), shaped((L, D), low_type), shaped((8, D), wide), shaped((L, D), wide)),
        [scalars, vectors, tokens, *attended, *flat(mixers)],
        "vv" + "v" * 4 + "h" * len(flat(mixers)),
        "vvvh",
        [
            pltpu.VMEM((D, D), low_type),
            pltpu.VMEM((L, D), wide),
            pltpu.SemaphoreType.DMA((8 + STEPS,)),
        ],
    )


def inner_forward(scalars, normed_low, weights, biases):
    chunk = 256

    def kernel(scalar_ref, normed_ref, *refs):
        bias_refs = refs[:2]
        parts, refs = unflatten(refs[2:], weights)
        out_refs, slope_out, weight, bias, slope_ref, semaphores = refs[:2], *refs[2:]
        odd = scalar_ref[1]
        fetches = [begin_weight(parts[i], odd, weight.at[i], semaphores, 2 * i) for i in range(2)]
        for index in range(2):
            bias[index] = bias_refs[index][...].astype(wide)

        @pl.loop(0, 2)
        def _(slot):
            for index in range(2):

                @pl.when(slot == index)
                def _(index=index):
                    wait(fetches[index])

            @pl.loop(0, D // chunk)
            def _(step):
                columns = pl.ds(pl.multiple_of(step * chunk, chunk), chunk)
                inner_pre = (
                    product(normed_ref[...], weight[slot, :, columns], NN)
                    + bias[slot, 1:2, columns]
                )
                below = 0.5 * (1.0 + lax.erf(inner_pre * root_half))
                density = jnp.exp(-0.5 * inner_pre * inner_pre) * inv_root_tau
                activated = (inner_pre * below).astype(low_type)
                slope_ref[slot, :, columns] = (below + inner_pre * density).astype(low_type)
                for index in range(2):

                    @pl.when(slot == index)
                    def _(index=index):
                        out_refs[index][:, columns] = activated

            begin(slope_ref.at[slot], slope_out.at[slot], semaphores.at[4 + slot])

        for slot in range(2):
            pltpu.make_async_copy(
                slope_ref.at[slot], slope_out.at[slot], semaphores.at[4 + slot]
            ).wait()

    return call(
        kernel,
        "inner_forward",
        (shaped((L, D), low_type),) * 2 + (shaped((2, L, D), low_type),),
        [scalars, normed_low, *biases, *flat(weights)],
        "vvv" + "h" * len(flat(weights)),
        "vvh",
        [
            pltpu.VMEM((2, D, D), low_type),
            pltpu.VMEM((2, 16, D), wide),
            pltpu.VMEM((2, L, D), low_type),
            pltpu.SemaphoreType.DMA((6,)),
        ],
    )


def middle(
    scalars, vectors, hat_one, inverse_one, grad_out, activated, slopes, outers, inners
):
    chunk = 256

    def kernel(scalar_ref, vector_ref, hat_in, inverse_ref, incoming_in, *refs):
        left_refs, slope_in = refs[:4], refs[4:6]
        outer_parts, refs = unflatten(refs[6:], outers)
        inner_parts, refs = unflatten(refs, inners)
        low_ref, branch_ref, bias_ref, sums_ref = refs[:4]
        inner_refs, grad_out_ref, result_out = refs[4:8], refs[8], refs[9]
        outer, inner, slope_ref, hat_ref, incoming_ref, second_ref, grad_ref, result_ref = refs[10:18]
        semaphores = refs[18]
        place, odd, length = read_scalars(scalar_ref)
        fetch_outer = [
            begin_weight(outer_parts[i], odd, outer.at[i], semaphores, 2 * i) for i in range(4)
        ]
        fetch_rest = [
            begin(hat_in, hat_ref, semaphores.at[8]),
            begin(incoming_in, incoming_ref, semaphores.at[9]),
        ]
        fetch_slope = [
            begin(slope_in[i // 2].at[i % 2], slope_ref.at[i], semaphores.at[10 + i])
            for i in range(4)
        ]
        fetch_inner = [
            begin_weight(inner_parts[i], odd, inner.at[i], semaphores, 14 + 2 * i)
            for i in range(4)
        ]
        vectors = vector_ref[...].astype(wide)
        sums_ref[...] = jnp.zeros((16, D), wide)
        bias_ref[...] = jnp.zeros((8, D), wide)

        def result_copy(step):
            at = block_rows(step)
            return pltpu.make_async_copy(
                result_ref.at[at], result_out.at[at], semaphores.at[22 + step]
            )

        def grad_copy(step):
            at = block_rows(step)
            return pltpu.make_async_copy(
                grad_ref.at[at], grad_out_ref.at[at], semaphores.at[22 + STEPS + step]
            )

        @pl.loop(0, STEPS)
        def _(step):
            at = block_rows(step)
            branch = vectors[3:4]
            for index in range(4):

                @pl.when(step == 0)
                def _(index=index):
                    wait(fetch_outer[index])

                branch = branch + product(left_refs[index][at, :], outer[index], NN)

            @pl.when(step == 0)
            def _():
                wait(fetch_rest)

            normed_one = hat_ref[at, :] * vectors[1:2] + vectors[2:3]
            hat, inverse = normalize(normed_one + branch)
            result_ref[at, :] = (hat * vectors[4:5] + vectors[5:6]).astype(low_type)
            result_copy(step).start()
            incoming = incoming_ref[at, :].astype(wide)
            grad = normalize_backward(incoming * vectors[4:5], hat, inverse)
            second_ref[at, :] = grad
            low_ref[at, :] = grad.astype(low_type)
            row = lax.broadcasted_iota(jnp.int32, (BLOCK, 1), 0) + step * BLOCK
            valid = (row < length).astype(wide)
            sums_ref[0:1, :] += column_sum(incoming * hat)
            sums_ref[1:2, :] += column_sum(incoming)
            sums_ref[2:3, :] += column_sum(grad)
            sums_ref[3:4, :] += column_sum(valid * branch * branch)

        @pl.loop(0, 4)
        def _(slot):
            for index in range(4):

                @pl.when(slot == index)
                def _(index=index):
                    fetch_slope[index].wait()

            @pl.loop(0, D // chunk)
            def _(step):
                columns = pl.ds(pl.multiple_of(step * chunk, chunk), chunk)
                grad = product(low_ref[...], outer[slot, columns, :], NT) * slope_ref[
                    slot, :, columns
                ].astype(wide)
                bias_ref[pl.ds(place ^ slot, 1), columns] = column_sum(grad)
                low = grad.astype(low_type)
                for index in range(4):

                    @pl.when(slot == index)
                    def _(index=index):
                        inner_refs[index][:, columns] = low

        for fetch in fetch_inner:
            wait(fetch)

        @pl.loop(0, STEPS)
        def _(step):
            at = block_rows(step)
            total = second_ref[at, :]
            for index in range(4):
                total = total + product(inner_refs[index][at, :], inner[index], NT)
            hat = hat_ref[at, :]
            grad = normalize_backward(total * vectors[1:2], hat, inverse_ref[at, :])
            grad_ref[at, :] = grad
            grad_copy(step).start()
            branch_ref[at, :] = grad.astype(low_type)
            sums_ref[8:9, :] += column_sum(total * hat)
            sums_ref[9:10, :] += column_sum(total)
            sums_ref[10:11, :] += column_sum(grad)

        for step in range(STEPS):
            result_copy(step).wait()
            grad_copy(step).wait()

    return call(
        kernel,
        "middle",
        (
            shaped((L, D), low_type),
            shaped((L, D), low_type),
            shaped((8, D), wide),
            shaped((16, D), wide),
        )
        + (shaped((L, D), low_type),) * 4
        + (shaped((L, D), wide), shaped((L, D), low_type)),
        [
            scalars,
            vectors,
            hat_one,
            inverse_one,
            grad_out,
            *activated,
            *slopes,
            *flat(outers),
            *flat(inners),
        ],
        "vhvh" + "vvvv" + "hh" + "h" * len(flat(outers) + flat(inners)),
        "vvvv" + "vvvv" + "hh",
        [
            pltpu.VMEM((4, D, D), low_type),
            pltpu.VMEM((4, D, D), low_type),
            pltpu.VMEM((4, L, D), low_type),
            pltpu.VMEM((L, D), wide),
            pltpu.VMEM((L, D), low_type),
            pltpu.VMEM((L, D), wide),
            pltpu.VMEM((L, D), wide),
            pltpu.VMEM((L, D), low_type),
            pltpu.SemaphoreType.DMA((22 + 2 * STEPS,)),
        ],
        limit=32,
    )


def add_halves(scalars, near, far, incoming):
    half = near.shape[0]

    def kernel(scalar_ref, near_ref, far_ref, incoming_ref, near_out, far_out):
        near_out[...] = add_rows(near_ref[...], incoming_ref[:half, :])
        far_out[...] = add_rows(far_ref[...], incoming_ref[half:, :])

    return call(
        kernel,
        "add_halves",
        (shaped((half, D), low_type),) * 2,
        [scalars, near, far, incoming],
        "vvv",
        "vv",
    )


def input_backward(scalars, first_grad, qkv_grads, projections):
    width = D // 4

    def kernel(scalar_ref, first_in, *refs):
        left_refs = refs[:4]
        parts, refs = unflatten(refs[4:], projections)
        out, weight, first_ref, semaphores = refs
        odd = scalar_ref[1]
        fetches = [begin_weight(parts[i], odd, weight.at[i], semaphores, 2 * i) for i in range(4)]
        fetch_first = begin(first_in, first_ref, semaphores.at[8])

        @pl.loop(0, STEPS)
        def _(step):
            at = block_rows(step)
            total = 0.0
            for index in range(4):

                @pl.when(step == 0)
                def _(index=index):
                    wait(fetches[index])

                total = total + product(left_refs[index][at, :], weight[index, : 3 * width], NN)

            @pl.when(step == 0)
            def _():
                fetch_first.wait()

            first_ref[at, :] = total + first_ref[at, :]
            begin(first_ref.at[at], out.at[at], semaphores.at[9 + step])

        for step in range(STEPS):
            at = block_rows(step)
            pltpu.make_async_copy(first_ref.at[at], out.at[at], semaphores.at[9 + step]).wait()

    return call(
        kernel,
        "input_backward",
        (shaped((L, D), wide),),
        [scalars, first_grad, *qkv_grads, *flat(projections)],
        "h" + "v" * 4 + "h" * len(flat(projections)),
        "h",
        [
            pltpu.VMEM((4, 3 * width + EXTRA, D), low_type),
            pltpu.VMEM((L, D), wide),
            pltpu.SemaphoreType.DMA((9 + STEPS,)),
        ],
        limit=16,
    )[0]


def solution(mesh):
    dp_size = mesh.shape["dp"]
    tensor_size = mesh.shape["tensor"]
    masks = [1 << bit for bit in range(dp_size.bit_length() - 1)]

    def over_tensor(value, mask):
        return lax.ppermute(value, "tensor", [(i, i ^ mask) for i in range(tensor_size)])

    def over_dp(value, mask):
        return lax.ppermute(value, "dp", [(i, i ^ mask) for i in range(dp_size)])

    def body(
        tokens,
        grad_out,
        lengths,
        segment_ids,
        query_weight,
        query_bias,
        key_weight,
        value_weight,
        value_bias,
        mixer_weight,
        mixer_bias,
        first_gain,
        first_shift,
        inner_weight,
        inner_bias,
        outer_weight,
        outer_bias,
        second_gain,
        second_shift,
    ):
        width = query_weight.shape[1]
        place = lax.axis_index("tensor")
        odd = lax.axis_index("dp") % 2
        chain = [jnp.zeros((8, 128), wide)]

        def after(*values):
            held = lax.optimization_barrier((chain[0],) + values)
            return held[1:] if len(values) > 1 else held[1]

        def done(*values):
            chain[0] = lax.optimization_barrier((chain[0],) + values)[0]
            return values if len(values) > 1 else values[0]

        lines = [mixer_bias, first_gain, first_shift, outer_bias, second_gain, second_shift]
        lines = dict(enumerate(lines))
        lines[8] = jnp.pad(query_bias, (0, D - width)) + jnp.pad(
            value_bias, (2 * width, D - 3 * width)
        )
        lines[9] = inner_bias
        line_at = lax.broadcasted_iota(jnp.int32, (16, D), 0)
        vectors = jnp.zeros((16, D), low_type)
        for index, line in lines.items():
            vectors = jnp.where(line_at == index, line[None, :], vectors)
        high = lax.axis_index("dp") // 2 % 2
        scalars = jnp.concatenate([jnp.stack([place, odd, high]).astype(jnp.int32), lengths])

        def hold():
            chain[0] = tick(scalars, chain[0])

        def send(value, mask):
            return over_tensor(after(value), mask)

        def pass_y(value):
            return over_dp(after(value), masks[0])

        def land(value):
            return done(after(value))

        def stage(function, *operands):
            return done(*function(after(scalars), *operands))

        piece, own_heads = done(
            *prepare(
                scalars,
                vectors,
                [query_weight.T, key_weight.T, value_weight.T],
                mixer_weight,
            )
        )
        heads = {}

        def attend(slots, projections):
            outs = stage(attend_forward, segment_ids, tokens, projections)
            for index, slot in enumerate(slots):
                heads[slot] = outs[index :: len(slots)]

        heads_x = send(piece, 2)
        heads_core = send(own_heads, 1)
        hold()
        inner_piece, outer_piece = stage(halve, inner_weight, outer_weight)
        attend((0,), [(own_heads,)])
        heads_core = land(heads_core)
        if not LATE:
            inner_core = send(inner_weight, 1)
            attend((1,), [(heads_core,)])
            inner_core = land(inner_core)
        heads_x = land(heads_x)
        heads_y = pass_y(heads_x)
        inner_x = send(inner_piece, 2)
        heads_near = send(heads_x, 1)
        hold()
        if LATE:
            inner_core = send(inner_weight, 1)
            attend((1,), [(heads_core,)])
            inner_core = land(inner_core)
        heads_near = land(heads_near)
        outer_core = send(outer_weight, 1)
        hold()
        outer_core = land(outer_core)
        heads_y = land(heads_y)
        heads_far = send(heads_y, 1)
        inner_x = land(inner_x)
        inner_y = pass_y(inner_x)
        outer_x = send(outer_piece, 2)
        inner_near = send(inner_x, 1)
        if HOLD_A:
            hold()
        heads_far = land(heads_far)
        attend((2, 3), [(heads_x, heads_y), (heads_near, heads_far)])
        inner_near = land(inner_near)
        attended = [heads[j][0] for j in range(4)]
        inner_biases = [heads[j][1] for j in range(4)]
        projections = mixers = [
            (own_heads,),
            (heads_core,),
            (heads_x, heads_y),
            (heads_near, heads_far),
        ]
        inverse_one, normed_low, sums_one, hat_one = stage(
            mix_norm, vectors, tokens, attended, mixers
        )
        outer_x = land(outer_x)
        outer_y = pass_y(outer_x)
        outer_near = send(outer_x, 1)
        inner_y = land(inner_y)
        inner_far = send(inner_y, 1)
        if HOLD_B:
            hold()
        outer_near = land(outer_near)
        *activated, slope_one = stage(
            inner_forward, normed_low, [(inner_weight,), (inner_core,)], inner_biases[:2]
        )
        inner_far = land(inner_far)
        *more, slope_two = stage(
            inner_forward,
            normed_low,
            [(inner_x, inner_y), (inner_near, inner_far)],
            inner_biases[2:],
        )
        activated = activated + more
        inners = [(inner_weight,), (inner_core,), (inner_x, inner_y), (inner_near, inner_far)]
        outer_y = land(outer_y)
        outer_far = send(outer_y, 1)
        hold()
        outer_far = land(outer_far)
        outers = [(outer_weight,), (outer_core,), (outer_x, outer_y), (outer_near, outer_far)]
        ffn_low, branch_low, inner_bias_rows, sums_two, *rest = stage(
            middle,
            vectors,
            hat_one,
            inverse_one,
            grad_out,
            activated,
            [slope_one, slope_two],
            outers,
            inners,
        )
        *inner_lows, first_grad, layer_out = rest

        def part(left, right):
            left, right = after(left, right)
            return done(product(left, right, TN).astype(low_type))

        def add_low(left, right):
            return done(add_rows(*after(left, right)))

        waiting = []

        def flush():
            results = done(
                *finish(
                    after(scalars),
                    [one.bits[0] for one in waiting],
                    [one.pair for one in waiting],
                    [one.outputs for one in waiting],
                )
            )
            results = list(results) if isinstance(results, tuple) else [results]
            for one in waiting:
                one.result, results = results[: one.outputs], results[one.outputs :]
            waiting.clear()

        class Reduction:
            def __init__(self, outputs=1, bits=(Y_BIT, Z_BIT)):
                self.outputs, self.bits = outputs, bits
                self.todo = ["split", "split"] + ["add"] * (len(masks) - 2)
                self.todo += ["back", "join", "end"]
                self.level = 0

            def begin(self, sent):
                self.incoming = send(sent, 2)
                if HOLD_X:
                    hold()
                return self

            def across(self, value, mask):
                self.incoming = over_dp(after(value), mask)
                if HOLD_HOPS:
                    hold()

            def terms(self):
                return (self.kept,)

            def hop(self):
                if not self.todo:
                    return
                step = self.todo.pop(0)
                *terms, incoming = after(*self.terms(), self.incoming)
                if step == "split":
                    bit = self.bits[self.level]
                    sent, self.kept = stage(split_add, bit, *terms, incoming)
                    self.terms = lambda: (self.kept,)
                    self.level += 1
                    self.across(sent, bit)
                elif step in ("add", "back"):
                    self.kept = done(add_rows(terms[0], incoming))
                    mask = self.bits[1] if step == "back" else 4 << (self.level - 2)
                    self.level += 1
                    self.across(self.kept, mask)
                elif step == "join":
                    self.kept = done(join(after(scalars), self.bits[1], terms[0], incoming))
                    self.across(self.kept, self.bits[0])
                else:
                    self.pair = (terms[0], incoming)
                    waiting.append(self)
                    if len(waiting) == 4 or (len(waiting) == EARLY and len(chains) == 4):
                        flush()

        class MixedReduction(Reduction):
            def __init__(self, kept, extra):
                super().__init__()
                self.kept, self.extra = kept, extra
                self.todo = ["mixed"] * (len(masks) + 1) + ["end"]

            def hop(self):
                if not self.todo or self.todo[0] == "end":
                    super().hop()
                    return
                self.todo.pop(0)
                kept, extra, incoming = after(self.kept, self.extra, self.incoming)
                text, self.kept, self.extra = stage(
                    mixed_hop, kept, extra, incoming, self.level == 0
                )
                mask = masks[self.level] if self.level < len(masks) else masks[0]
                self.level += 1
                self.across(text, mask)

        class CrossReduction(Reduction):
            def __init__(self, near, near_partner, far, far_partner, bits):
                super().__init__(1, bits)
                sent, self.near, self.far = stage(
                    take_halves, bits[0], *after(near, near_partner, far, far_partner)
                )
                self.todo[0] = "cross"
                self.incoming = over_dp(after(sent), bits[0])
                if HOLD_Y:
                    hold()

            def hop(self):
                if self.todo and self.todo[0] == "cross":
                    self.todo.pop(0)
                    near, far, incoming = after(self.near, self.far, self.incoming)
                    self.kept, far = stage(add_halves, near, far, incoming)
                    self.level = 1
                    self.incoming = send(far, 2)
                    if HOLD_Z:
                        hold()
                else:
                    super().hop()

        partner = {}
        outer_parts, inner_parts, heads_parts = {}, {}, {}
        qkv_grads, qkv_bias = {}, {}

        def retreat(slots):
            kept = [heads[slot] for slot in slots]
            *grads, bias = stage(
                attend_backward,
                slots,
                branch_low,
                [mixers[slot] for slot in slots],
                [one[0] for one in kept],
                [one[2] for one in kept],
                [one[3] for one in kept],
            )
            qkv_grads.update(zip(slots, grads))
            qkv_bias[slots] = bias

        def split_step(name, slot):
            left, right = {
                "o": (activated[slot], ffn_low),
                "i": (normed_low, inner_lows[slot]),
                "m": (attended[slot], branch_low),
                "h": (qkv_grads.get(slot), tokens),
            }[name]
            share = part(left, right)
            if slot % 2:
                partner[name, slot - 1] = send(share, 1)
            else:
                own_share[name, slot] = share

        def own_sum(name, slot):
            return add_low(own_share[name, slot], partner[name, slot])

        own_share, chains = {}, {}
        for step in PLAN:
            name, slot = step[0], int(step[1])
            if name == "b":
                retreat(tuple(int(digit) for digit in step[1:]))
            elif name in "oimh":
                split_step(name, slot)
            elif name == "X":
                which = ("o", None, "h")[slot]
                chains[slot] = Reduction(3 if slot == 2 else 1).begin(own_sum(which, 2))
            elif name == "Y":
                chains[1] = CrossReduction(
                    own_share["i", 0],
                    partner["i", 0],
                    own_share["i", 2],
                    partner["i", 2],
                    (Z_BIT, Y_BIT),
                )
            elif name == "S":
                small = done(
                    jnp.concatenate(
                        [
                            sums_one,
                            sums_two,
                            inner_bias_rows,
                            sum(qkv_bias.values()),
                        ]
                    )
                )
                small_other = send(small, 1)
            elif name == "M":
                small = done(small + after(small_other))
                sent = done(message(own_sum("m", 2), small))
                chains[3] = MixedReduction(own_sum("m", 0), small).begin(sent)
            elif name == "B":
                tokens_grad = done(
                    input_backward(
                        after(scalars), first_grad, [qkv_grads[j] for j in range(4)], projections
                    )
                )
            else:
                if name == "H" and slot in (0, 2) and chains[slot].level == 0:
                    which = "o" if slot == 0 else "h"
                    both = (own_share[which, 0], partner[which, 0])
                    chains[slot].terms = lambda both=both: both
                chains[slot].hop()
        for chain_left in chains.values():
            while chain_left.todo:
                chain_left.hop()
        if waiting:
            flush()
        small = chains[3].extra
        outer_chain, inner_chain, heads_chain, mixer_chain = (chains[j] for j in range(4))

        totals = jnp.sum(jnp.stack([small[0], small[1], small[11]]), axis=1)
        statistics = jnp.sqrt(totals / (small[2, 0] * D))
        own_inner_bias = lax.dynamic_index_in_dim(small[24:28], place, 0, keepdims=False)
        own_qkv_bias = lax.dynamic_index_in_dim(small[32:36], place, 0, keepdims=False)
        query_grad, key_grad, value_grad = heads_chain.result
        return (
            layer_out,
            tokens_grad,
            query_grad.T,
            own_qkv_bias[:width],
            key_grad.T,
            value_grad.T,
            own_qkv_bias[2 * width : 3 * width],
            mixer_chain.result[0],
            small[18],
            small[16],
            small[17],
            inner_chain.result[0],
            own_inner_bias,
            outer_chain.result[0],
            small[10],
            small[8],
            small[9],
            statistics,
        )

    in_specs = (
        P(("dp", "tensor"), None),
        P(("dp", "tensor"), None),
        P("dp"),
        P("dp", None),
        P(None, "tensor"),
        P("tensor"),
        P(None, "tensor"),
        P(None, "tensor"),
        P("tensor"),
        P("tensor", None),
        P(),
        P(),
        P(),
        P(None, "tensor"),
        P("tensor"),
        P("tensor", None),
        P(),
        P(),
        P(),
    )
    out_specs = (
        P(("dp", "tensor"), None),
        P(("dp", "tensor"), None),
        P(None, "tensor"),
        P("tensor"),
        P(None, "tensor"),
        P(None, "tensor"),
        P("tensor"),
        P("tensor", None),
        P(),
        P(),
        P(),
        P(None, "tensor"),
        P("tensor"),
        P("tensor", None),
        P(),
        P(),
        P(),
        P(),
    )
    return jax.shard_map(body, mesh=mesh, in_specs=in_specs, out_specs=out_specs, check_vma=False)
```

```python
import jax
import jax.numpy as jnp
from jax import lax
from jax.experimental import pallas as pl
from jax.experimental.pallas import tpu as pltpu
from jax.sharding import PartitionSpec as P

D = 768
HEAD_DIM = 64
L = 512
EXTRA = 32

eps_norm = 1e-06
root_half = 0.7071067811865476
inv_root_tau = 0.3989422804014327
low_type = jnp.bfloat16
wide = jnp.float32
NN = (((1,), (0,)), ((), ()))
NT = (((1,), (1,)), ((), ()))
TN = (((0,), (0,)), ((), ()))


def product(left, right, dims):
    return lax.dot_general(left, right, dims, preferred_element_type=wide)


def shaped(shape, dtype):
    return jax.ShapeDtypeStruct(shape, dtype)


COST = 100000000000
PRICES = {
    "prepare": 100000000000,
    "attend_forward": 100000000000,
    "mix_norm": 100000000000,
    "inner_forward": 5000000000,
    "middle": 100000000000,
    "attend_backward": 100000000000,
    "input_backward": 0,
    "split_add": 0,
    "mixed_hop": 0,
    "finish": 0,
    "take_halves": 0,
    "add_halves": 0,
    "join": 0,
    "tick": 100000000000,
    "halve": 100000000000,
}
HOLD_HOPS = False
HOLD_A = True
HOLD_B = False
HOLD_C = False
HOLD_D = False
HOLD_X = True
HOLD_Y = False
HOLD_Z = False
BRANCH_LATE = False
LATE = False
EARLY = 2
PLAN = (
    "o3", "i3", "o2", "X0", "i1", "i2", "i0", "Y1", "b3", "h3", "b2", "h2",
    "o1", "X2", "o0", "b1", "h1", "H0", "b0", "m3", "H1", "m1", "m2", "m0",
    "S0", "h0", "M3", "H0", "H2", "H1", "H0", "H3", "H2", "H0", "H1", "B0",
    "H2", "H3", "H0", "H1", "H3", "H2", "H1", "H3", "H2", "H1", "H2", "H0",
    "H1", "H3", "H0",
)


def call(
    kernel, name, out_shape, operands, spaces, out_spaces, scratch=(), limit=14
):
    place = {"v": pltpu.VMEM, "h": pltpu.HBM, "a": pl.ANY}
    price = PRICES.get(name, COST)
    out_shape = tuple(
        pltpu.HBM(one.shape, one.dtype) if letter == "h" else one
        for one, letter in zip(out_shape, out_spaces)
    )
    operands = operands[:1] + [
        pltpu.with_memory_space_constraint(one, pltpu.HBM) if letter == "h" else one
        for one, letter in zip(operands[1:], spaces)
    ]
    return pl.pallas_call(
        kernel,
        out_shape=out_shape,
        in_specs=[pl.BlockSpec(memory_space=pltpu.SMEM)]
        + [pl.BlockSpec(memory_space=place[letter]) for letter in spaces],
        out_specs=tuple(pl.BlockSpec(memory_space=place[letter]) for letter in out_spaces),
        scratch_shapes=list(scratch),
        compiler_params=pltpu.CompilerParams(vmem_limit_bytes=limit << 20),
        cost_estimate=pl.CostEstimate(flops=price, transcendentals=0, bytes_accessed=price // 300),
        name=name,
    )(*operands)


def read_scalars(scalar_ref):
    place = scalar_ref[0]
    return place, scalar_ref[1], scalar_ref[3 + place]


def begin(source, target, semaphore):
    copy = pltpu.make_async_copy(source, target, semaphore)
    copy.start()
    return copy


def begin_weight(parts, odd, target, semaphores, at, first=0):
    rows = target.shape[0] // len(parts)
    first = first // len(parts)
    parts = [part.at[pl.ds(first, rows)] for part in parts]
    if len(parts) == 1:
        return [begin(parts[0], target, semaphores.at[at])]
    return [
        begin(
            part,
            target.at[pl.ds(pl.multiple_of(which * rows, rows), rows)],
            semaphores.at[at + index],
        )
        for index, (part, which) in enumerate(zip(parts, (odd, 1 - odd)))
    ]


def wait(copies):
    for copy in copies:
        copy.wait()


def unflatten(refs, slots):
    out, at = [], 0
    for parts in slots:
        out.append(refs[at : at + len(parts)])
        at += len(parts)
    return out, refs[at:]


def flat(slots):
    return [part for parts in slots for part in parts]


WIDTH = D // 4
PROJECTION_ROWS = 3 * WIDTH + EXTRA


def prepare(scalars, vectors, weights, mixer):
    rows = PROJECTION_ROWS + WIDTH

    def kernel(scalar_ref, vector_ref, query, key, value, mixer_in, piece_ref, own_ref, semaphores):
        odd = scalar_ref[1]
        fetches = [
            begin(source, own_ref.at[pl.ds(start, WIDTH)], semaphores.at[index])
            for index, (source, start) in enumerate(
                zip((query, key, value, mixer_in), (0, WIDTH, 2 * WIDTH, PROJECTION_ROWS))
            )
        ]
        own_ref[3 * WIDTH : PROJECTION_ROWS, :] = jnp.zeros((EXTRA, D), low_type)
        own_ref[3 * WIDTH : 3 * WIDTH + 8, :] = vector_ref[8:16, :]
        wait(fetches)
        half = PROJECTION_ROWS // 2
        piece_ref[:half, :] = own_ref[pl.ds(pl.multiple_of(odd * half, 16), half), :]
        half_mixer = WIDTH // 2
        piece_ref[half:, :] = own_ref[
            pl.ds(pl.multiple_of(PROJECTION_ROWS + odd * half_mixer, 16), half_mixer), :
        ]

    return call(
        kernel,
        "prepare",
        (shaped((rows // 2, D), low_type), shaped((rows, D), low_type)),
        [scalars, vectors, *weights, mixer],
        "vhhhh",
        "vv",
        [pltpu.SemaphoreType.DMA((4,))],
    )


def halve(scalars, inner, outer):
    def kernel(scalar_ref, inner_in, outer_in, inner_out, outer_out, semaphores):
        half = D // 2
        chosen = pl.ds(pl.multiple_of(scalar_ref[1] * half, half), half)
        wait(
            [
                begin(inner_in.at[chosen], inner_out, semaphores.at[0]),
                begin(outer_in.at[chosen], outer_out, semaphores.at[1]),
            ]
        )

    return call(
        kernel,
        "halve",
        (shaped((D // 2, D), low_type),) * 2,
        [scalars, inner, outer],
        "hh",
        "vv",
        [pltpu.SemaphoreType.DMA((2,))],
    )


def tick(scalars, token):
    def kernel(scalar_ref, token_ref, out_ref):
        out_ref[...] = token_ref[...]

    return call(kernel, "tick", (shaped(token.shape, token.dtype),), [scalars, token], "v", "v")[0]


def add_rows(left, right):
    return (left.astype(wide) + right.astype(wide)).astype(low_type)


Y_BIT, Z_BIT = 1, 2


def split_add(scalars, bit, *terms):
    half = terms[0].shape[0] // 2

    def kernel(scalar_ref, *refs):
        mine = scalar_ref[bit]
        for which, out_ref in ((1 - mine, refs[-2]), (mine, refs[-1])):
            rows = pl.ds(pl.multiple_of(which * half, 16), half)
            total = refs[0][rows, :].astype(wide)
            for ref in refs[1:-2]:
                total = total + ref[rows, :].astype(wide)
            out_ref[...] = total.astype(low_type)

    return call(
        kernel,
        "split_add",
        (shaped((half, D), low_type),) * 2,
        [scalars, *terms],
        "v" * len(terms),
        "vv",
    )


def join(scalars, bit, mine, other):
    half = mine.shape[0]

    def kernel(scalar_ref, mine_ref, other_ref, out_ref):
        at = scalar_ref[bit]
        out_ref[pl.ds(pl.multiple_of(at * half, 16), half), :] = mine_ref[...]
        out_ref[pl.ds(pl.multiple_of((1 - at) * half, 16), half), :] = other_ref[...]

    return call(
        kernel, "join", (shaped((2 * half, D), low_type),), [scalars, mine, other], "vv", "v"
    )[0]


def take_halves(scalars, bit, near, near_partner, far, far_partner):
    half = near.shape[0] // 2

    def kernel(scalar_ref, near_ref, near_other, far_ref, far_other, send_ref, near_out, far_out):
        mine = scalar_ref[bit]
        theirs = pl.ds(pl.multiple_of((1 - mine) * half, 16), half)
        ours = pl.ds(pl.multiple_of(mine * half, 16), half)
        send_ref[:half, :] = add_rows(near_ref[theirs, :], near_other[theirs, :])
        send_ref[half:, :] = add_rows(far_ref[theirs, :], far_other[theirs, :])
        near_out[...] = add_rows(near_ref[ours, :], near_other[ours, :])
        far_out[...] = add_rows(far_ref[ours, :], far_other[ours, :])

    return call(
        kernel,
        "take_halves",
        (shaped((2 * half, D), low_type),) + (shaped((half, D), low_type),) * 2,
        [scalars, near, near_partner, far, far_partner],
        "vvvv",
        "vvv",
    )


def message(rows, extra):
    high = extra.astype(low_type)
    return jnp.concatenate([rows, high, (extra - high.astype(wide)).astype(low_type)], axis=0)


def mixed_hop(scalars, kept, extra, incoming, split):
    rows = kept.shape[0] // 2 if split else kept.shape[0]
    count = extra.shape[0]

    def kernel(scalar_ref, kept_ref, extra_ref, incoming_ref, message_ref, keep_ref, out_ref):
        at = kept.shape[0]
        total = extra_ref[...] + (
            incoming_ref[at : at + count, :].astype(wide)
            + incoming_ref[at + count : at + 2 * count, :].astype(wide)
        )
        out_ref[...] = total
        high = total.astype(low_type)
        message_ref[rows : rows + count, :] = high
        message_ref[rows + count :, :] = (total - high.astype(wide)).astype(low_type)
        if split:
            odd = scalar_ref[1]
            theirs = pl.ds(pl.multiple_of((1 - odd) * rows, 16), rows)
            ours = pl.ds(pl.multiple_of(odd * rows, 16), rows)
            message_ref[:rows, :] = add_rows(kept_ref[theirs, :], incoming_ref[theirs, :])
            keep_ref[...] = add_rows(kept_ref[ours, :], incoming_ref[ours, :])
        else:
            joined = add_rows(kept_ref[...], incoming_ref[:rows, :])
            message_ref[:rows, :] = joined
            keep_ref[...] = joined

    return call(
        kernel,
        "mixed_hop",
        (
            shaped((rows + 2 * count, D), low_type),
            shaped((rows, D), low_type),
            shaped((count, D), wide),
        ),
        [scalars, kept, extra, incoming],
        "vvv",
        "vvv",
    )


def finish(scalars, bits, pairs, outputs):
    def kernel(scalar_ref, *refs):
        count = len(pairs)
        outs, joins = refs[2 * count : -count - 1], refs[-count - 1 : -1]
        semaphores = refs[-1]
        copies, at = [], 0
        for index in range(count):
            half = pairs[index][0].shape[0]
            mine = scalar_ref[bits[index]]
            for ref, which in ((refs[2 * index], mine), (refs[2 * index + 1], 1 - mine)):
                joins[index][pl.ds(pl.multiple_of(which * half, 16), half), :] = ref[
                    :half, :
                ].astype(wide)
            rows = 2 * half // outputs[index]
            for part in range(outputs[index]):
                copies.append(
                    begin(
                        joins[index].at[pl.ds(part * rows, rows)], outs[at], semaphores.at[at]
                    )
                )
                at += 1
        wait(copies)

    shapes = [
        shaped((2 * pair[0].shape[0] // count, D), wide)
        for pair, count in zip(pairs, outputs)
        for _ in range(count)
    ]
    return call(
        kernel,
        "finish",
        tuple(shapes),
        [scalars, *[half for pair in pairs for half in pair]],
        "vv" * len(pairs),
        "h" * len(shapes),
        [pltpu.VMEM((2 * pair[0].shape[0], D), wide) for pair in pairs]
        + [pltpu.SemaphoreType.DMA((len(shapes),))],
        limit=20,
    )


HEADS_HERE = WIDTH // HEAD_DIM
QUERY_BLOCK = 256
QUERY_STEPS = L // QUERY_BLOCK
KEPT = (QUERY_STEPS, HEADS_HERE, L, QUERY_BLOCK)


def attend_forward(scalars, segment_ids, tokens, projections):
    count = len(projections)

    def kernel(scalar_ref, segment_ref, tokens_ref, *refs):
        slots, refs = unflatten(refs, projections)
        attended_refs, bias_refs = refs[:count], refs[count : 2 * count]
        qkv_outs, probs_outs = refs[2 * count : 3 * count], refs[3 * count : 4 * count]
        mask, weights, qkvs, probs_all, semaphores = refs[4 * count :]
        place, odd, length = read_scalars(scalar_ref)
        each = 3 + QUERY_STEPS
        fetches = [
            begin_weight(parts, odd, weights.at[i], semaphores, each * i)
            for i, parts in enumerate(slots)
        ]
        query_owner = segment_ref[pl.ds(place, 1), :].astype(wide)
        key_owner = jnp.broadcast_to(query_owner, (128, L)).T
        key_at = lax.broadcasted_iota(jnp.int32, (L, 128), 0)
        key_owner = jnp.where(key_at < length, key_owner, -1.0)
        query_at = lax.broadcasted_iota(jnp.int32, (L, 128), 1)
        for start in range(0, L, 128):
            allowed = (key_owner == query_owner[:, start : start + 128]) | (
                key_at == query_at + start
            )
            mask[:, start : start + 128] = jnp.where(allowed, 0.0, -1e30)
        copies = []
        for slot in range(count):
            weight, qkv_ref, probs_ref = weights.at[slot], qkvs.at[slot], probs_all.at[slot]
            attended_ref, probs_out = attended_refs[slot], probs_outs[slot]
            first = each * slot
            wait(fetches[slot])
            bias_refs[slot][...] = weight[3 * WIDTH : 3 * WIDTH + 16, :]
            bias = weight[3 * WIDTH : 3 * WIDTH + 16, : 3 * WIDTH].astype(wide)[0:1]
            qkv_ref[...] = (
                product(tokens_ref[...], weight[: 3 * WIDTH, :], NT) + bias
            ).astype(low_type)
            copies.append(begin(qkv_ref, qkv_outs[slot], semaphores.at[first + 2]))

            @pl.loop(0, QUERY_STEPS)
            def _(step):
                rows = pl.ds(pl.multiple_of(step * QUERY_BLOCK, QUERY_BLOCK), QUERY_BLOCK)
                for head in range(HEADS_HERE):
                    at = head * HEAD_DIM
                    queries = qkv_ref[rows, at : at + HEAD_DIM] * jnp.asarray(
                        HEAD_DIM**-0.5, low_type
                    )
                    key_rows = qkv_ref[:, WIDTH + at : WIDTH + at + HEAD_DIM]
                    values = qkv_ref[:, 2 * WIDTH + at : 2 * WIDTH + at + HEAD_DIM]
                    scores = product(key_rows, queries, NT) + mask[:, rows]
                    highest = jnp.max(scores, axis=0, keepdims=True)
                    expanded = jnp.exp(scores - highest)
                    total = jnp.sum(expanded, axis=0, keepdims=True)
                    probs = (expanded * (1.0 / total)).astype(low_type)
                    probs_ref[step, head] = probs
                    attended_ref[rows, at : at + HEAD_DIM] = product(probs, values, TN).astype(
                        low_type
                    )
                begin(probs_ref.at[step], probs_out.at[step], semaphores.at[first + 3 + step])

            for step in range(QUERY_STEPS):
                copies.append(
                    pltpu.make_async_copy(
                        probs_ref.at[step], probs_out.at[step], semaphores.at[first + 3 + step]
                    )
                )
        wait(copies)

    return call(
        kernel,
        "attend_forward",
        (shaped((L, WIDTH), low_type),) * count
        + (shaped((16, D), low_type),) * count
        + (shaped((L, 3 * WIDTH), low_type),) * count
        + (shaped(KEPT, low_type),) * count,
        [scalars, segment_ids, tokens, *flat(projections)],
        "vv" + "h" * (len(flat(projections)) - 1) + "a",
        "v" * (2 * count) + "h" * (2 * count),
        [
            pltpu.VMEM((L, L), wide),
            pltpu.VMEM((count, PROJECTION_ROWS, D), low_type),
            pltpu.VMEM((count, L, 3 * WIDTH), low_type),
            pltpu.VMEM((count,) + KEPT, low_type),
            pltpu.SemaphoreType.DMA(((3 + QUERY_STEPS) * count,)),
        ],
        limit=10 + 6 * count,
    )


def attend_backward(scalars, slots, branch_low, mixers, attended, qkv, probs):
    count = len(slots)

    def kernel(scalar_ref, branch_ref, *refs):
        attended_refs, qkv_ins = refs[:count], refs[count : 2 * count]
        probs_ins = refs[2 * count : 3 * count]
        parts, refs = unflatten(refs[3 * count :], mixers)
        grad_refs, bias_ref = refs[:count], refs[count]
        weights, qkvs, probs_all, outgoing, sums, dots, semaphores = refs[count + 1 :]
        fetches = [
            begin_weight(
                parts[i], scalar_ref[1], weights.at[i], semaphores, 4 * i, PROJECTION_ROWS
            )
            for i in range(count)
        ]
        fetches_rest = [
            [
                begin(qkv_ins[i], qkvs.at[i], semaphores.at[4 * i + 2]),
                begin(probs_ins[i], probs_all.at[i], semaphores.at[4 * i + 3]),
            ]
            for i in range(count)
        ]
        bias_ref[...] = jnp.zeros((8, D), wide)
        for slot in range(count):
            grad_ref, qkv_ref, probs_ref = grad_refs[slot], qkvs.at[slot], probs_all.at[slot]
            wait(fetches[slot])
            attended_grad = product(branch_ref[...], weights[slot], NT).astype(low_type)
            outgoing[...] = attended_grad
            along = (attended_refs[slot][...].astype(wide) * attended_grad.astype(wide)).T
            for head in range(HEADS_HERE):
                dots[head : head + 1, :] = jnp.sum(
                    along[head * HEAD_DIM : (head + 1) * HEAD_DIM], axis=0, keepdims=True
                )
                sums[head] = jnp.zeros((L, HEAD_DIM), wide)
            wait(fetches_rest[slot])

            @pl.loop(0, QUERY_STEPS)
            def _(step):
                rows = pl.ds(pl.multiple_of(step * QUERY_BLOCK, QUERY_BLOCK), QUERY_BLOCK)
                for head in range(HEADS_HERE):
                    at = head * HEAD_DIM
                    queries = qkv_ref[:, at : at + HEAD_DIM] * jnp.asarray(
                        HEAD_DIM**-0.5, low_type
                    )
                    key_rows = qkv_ref[rows, WIDTH + at : WIDTH + at + HEAD_DIM]
                    values = qkv_ref[rows, 2 * WIDTH + at : 2 * WIDTH + at + HEAD_DIM]
                    grad = outgoing[:, at : at + HEAD_DIM]
                    probs_low = jnp.concatenate(
                        [probs_ref[part, head, rows, :] for part in range(QUERY_STEPS)], axis=1
                    )
                    probs_grad = product(values, grad, NT)
                    scores_grad = (
                        probs_low.astype(wide) * (probs_grad - dots[head : head + 1, :])
                    ).astype(low_type)
                    grad_ref[rows, WIDTH + at : WIDTH + at + HEAD_DIM] = product(
                        scores_grad, queries, NN
                    ).astype(low_type)
                    grad_ref[rows, 2 * WIDTH + at : 2 * WIDTH + at + HEAD_DIM] = product(
                        probs_low, grad, NN
                    ).astype(low_type)
                    sums[head] += product(scores_grad, key_rows, TN)

            for head in range(HEADS_HERE):
                at = head * HEAD_DIM
                grad_ref[:, at : at + HEAD_DIM] = (sums[head] * (HEAD_DIM**-0.5)).astype(low_type)
            quarter = scalar_ref[0] ^ slots[slot]
            bias_ref[pl.ds(quarter, 1), : 3 * WIDTH] = jnp.sum(
                grad_ref[...].astype(wide), axis=0, keepdims=True
            )

    return call(
        kernel,
        "attend_backward",
        (shaped((L, 3 * WIDTH), low_type),) * count + (shaped((8, D), wide),),
        [scalars, branch_low, *attended, *qkv, *probs, *flat(mixers)],
        "v" * (1 + count) + "h" * (2 * count + len(flat(mixers))),
        "v" * (count + 1),
        [
            pltpu.VMEM((count, WIDTH, D), low_type),
            pltpu.VMEM((count, L, 3 * WIDTH), low_type),
            pltpu.VMEM((count,) + KEPT, low_type),
            pltpu.VMEM((L, WIDTH), low_type),
            pltpu.VMEM((HEADS_HERE, L, HEAD_DIM), wide),
            pltpu.VMEM((8, L), wide),
            pltpu.SemaphoreType.DMA((4 * count,)),
        ],
        limit=10 + 5 * count,
    )


def normalize(rows):
    center = rows - jnp.mean(rows, axis=-1, keepdims=True)
    inverse = lax.rsqrt(jnp.mean(center * center, axis=-1, keepdims=True) + eps_norm)
    return center * inverse, inverse


def normalize_backward(scaled, normed, inverse):
    middle = jnp.mean(scaled, axis=-1, keepdims=True)
    along = jnp.mean(scaled * normed, axis=-1, keepdims=True)
    return inverse * (scaled - middle - normed * along)


def column_sum(rows):
    return jnp.sum(rows, axis=0, keepdims=True)


BLOCK = 256
STEPS = L // BLOCK


def block_rows(step):
    return pl.ds(pl.multiple_of(step * BLOCK, BLOCK), BLOCK)


def mix_norm(scalars, vectors, tokens, attended, mixers):
    width = D // 4

    def kernel(scalar_ref, vector_ref, tokens_ref, *refs):
        attended_refs = refs[:4]
        parts, refs = unflatten(refs[4:], mixers)
        inverse_ref, low_ref, sums_ref, hat_out, weight, hat_ref, semaphores = refs
        _, odd, length = read_scalars(scalar_ref)
        fetches = [
            begin_weight(
                parts[i], odd, weight.at[pl.ds(i * width, width)], semaphores, 2 * i, PROJECTION_ROWS
            )
            for i in range(4)
        ]
        vectors = vector_ref[...].astype(wide)
        sums_ref[...] = jnp.zeros((8, D), wide)
        for fetch in fetches:
            wait(fetch)

        @pl.loop(0, STEPS)
        def _(step):
            at = block_rows(step)
            branch = vectors[0:1]
            for index in range(4):
                branch = branch + product(
                    attended_refs[index][at, :], weight[index * width : (index + 1) * width], NN
                )
            rows = tokens_ref[at, :].astype(wide)
            hat, inverse = normalize(rows + branch)
            hat_ref[at, :] = hat
            begin(hat_ref.at[at], hat_out.at[at], semaphores.at[8 + step])
            inverse_ref[at, :] = inverse
            low_ref[at, :] = (hat * vectors[1:2] + vectors[2:3]).astype(low_type)
            place = lax.broadcasted_iota(jnp.int32, (BLOCK, 1), 0) + step * BLOCK
            valid = (place < length).astype(wide)
            sums_ref[0:1, :] += column_sum(valid * rows * rows)
            sums_ref[1:2, :] += column_sum(valid * branch * branch)
            sums_ref[2:3, :] += column_sum(jnp.broadcast_to(valid, (BLOCK, D)))

        for step in range(STEPS):
            at = block_rows(step)
            pltpu.make_async_copy(hat_ref.at[at], hat_out.at[at], semaphores.at[8 + step]).wait()

    return call(
        kernel,
        "mix_norm",
        (shaped((L, 1), wide), shaped((L, D), low_type), shaped((8, D), wide), shaped((L, D), wide)),
        [scalars, vectors, tokens, *attended, *flat(mixers)],
        "vv" + "v" * 4 + "h" * len(flat(mixers)),
        "vvvh",
        [
            pltpu.VMEM((D, D), low_type),
            pltpu.VMEM((L, D), wide),
            pltpu.SemaphoreType.DMA((8 + STEPS,)),
        ],
    )


def inner_forward(scalars, normed_low, weights, biases):
    chunk = 256

    def kernel(scalar_ref, normed_ref, *refs):
        bias_refs = refs[:2]
        parts, refs = unflatten(refs[2:], weights)
        out_refs, slope_out, weight, bias, slope_ref, semaphores = refs[:2], *refs[2:]
        odd = scalar_ref[1]
        fetches = [begin_weight(parts[i], odd, weight.at[i], semaphores, 2 * i) for i in range(2)]
        for index in range(2):
            bias[index] = bias_refs[index][...].astype(wide)

        @pl.loop(0, 2)
        def _(slot):
            for index in range(2):

                @pl.when(slot == index)
                def _(index=index):
                    wait(fetches[index])

            @pl.loop(0, D // chunk)
            def _(step):
                columns = pl.ds(pl.multiple_of(step * chunk, chunk), chunk)
                inner_pre = (
                    product(normed_ref[...], weight[slot, :, columns], NN)
                    + bias[slot, 1:2, columns]
                )
                below = 0.5 * (1.0 + lax.erf(inner_pre * root_half))
                density = jnp.exp(-0.5 * inner_pre * inner_pre) * inv_root_tau
                activated = (inner_pre * below).astype(low_type)
                slope_ref[slot, :, columns] = (below + inner_pre * density).astype(low_type)
                for index in range(2):

                    @pl.when(slot == index)
                    def _(index=index):
                        out_refs[index][:, columns] = activated

            begin(slope_ref.at[slot], slope_out.at[slot], semaphores.at[4 + slot])

        for slot in range(2):
            pltpu.make_async_copy(
                slope_ref.at[slot], slope_out.at[slot], semaphores.at[4 + slot]
            ).wait()

    return call(
        kernel,
        "inner_forward",
        (shaped((L, D), low_type),) * 2 + (shaped((2, L, D), low_type),),
        [scalars, normed_low, *biases, *flat(weights)],
        "vvv" + "h" * (len(flat(weights)) - 1) + "a",
        "vvh",
        [
            pltpu.VMEM((2, D, D), low_type),
            pltpu.VMEM((2, 16, D), wide),
            pltpu.VMEM((2, L, D), low_type),
            pltpu.SemaphoreType.DMA((6,)),
        ],
    )


def middle(
    scalars, vectors, hat_one, inverse_one, grad_out, activated, slopes, outers, inners
):
    chunk = 256

    def kernel(scalar_ref, vector_ref, hat_in, inverse_ref, incoming_in, *refs):
        left_refs, slope_in = refs[:4], refs[4:6]
        outer_parts, refs = unflatten(refs[6:], outers)
        inner_parts, refs = unflatten(refs, inners)
        low_ref, branch_ref, bias_ref, sums_ref = refs[:4]
        inner_refs, grad_out_ref, result_out = refs[4:8], refs[8], refs[9]
        outer, inner, slope_ref, hat_ref, incoming_ref, second_ref, grad_ref, result_ref = refs[10:18]
        semaphores = refs[18]
        place, odd, length = read_scalars(scalar_ref)
        fetch_outer = [
            begin_weight(outer_parts[i], odd, outer.at[i], semaphores, 2 * i) for i in range(4)
        ]
        fetch_rest = [
            begin(hat_in, hat_ref, semaphores.at[8]),
            begin(incoming_in, incoming_ref, semaphores.at[9]),
        ]
        fetch_slope = [
            begin(slope_in[i // 2].at[i % 2], slope_ref.at[i], semaphores.at[10 + i])
            for i in range(4)
        ]
        fetch_inner = [
            begin_weight(inner_parts[i], odd, inner.at[i], semaphores, 14 + 2 * i)
            for i in range(4)
        ]
        vectors = vector_ref[...].astype(wide)
        sums_ref[...] = jnp.zeros((16, D), wide)
        bias_ref[...] = jnp.zeros((8, D), wide)

        def result_copy(step):
            at = block_rows(step)
            return pltpu.make_async_copy(
                result_ref.at[at], result_out.at[at], semaphores.at[22 + step]
            )

        def grad_copy(step):
            at = block_rows(step)
            return pltpu.make_async_copy(
                grad_ref.at[at], grad_out_ref.at[at], semaphores.at[22 + STEPS + step]
            )

        @pl.loop(0, STEPS)
        def _(step):
            at = block_rows(step)
            branch = vectors[3:4]
            for index in range(4):

                @pl.when(step == 0)
                def _(index=index):
                    wait(fetch_outer[index])

                branch = branch + product(left_refs[index][at, :], outer[index], NN)

            @pl.when(step == 0)
            def _():
                wait(fetch_rest)

            normed_one = hat_ref[at, :] * vectors[1:2] + vectors[2:3]
            hat, inverse = normalize(normed_one + branch)
            result_ref[at, :] = (hat * vectors[4:5] + vectors[5:6]).astype(low_type)
            result_copy(step).start()
            incoming = incoming_ref[at, :].astype(wide)
            grad = normalize_backward(incoming * vectors[4:5], hat, inverse)
            second_ref[at, :] = grad
            low_ref[at, :] = grad.astype(low_type)
            row = lax.broadcasted_iota(jnp.int32, (BLOCK, 1), 0) + step * BLOCK
            valid = (row < length).astype(wide)
            sums_ref[0:1, :] += column_sum(incoming * hat)
            sums_ref[1:2, :] += column_sum(incoming)
            sums_ref[2:3, :] += column_sum(grad)
            sums_ref[3:4, :] += column_sum(valid * branch * branch)

        @pl.loop(0, 4)
        def _(slot):
            for index in range(4):

                @pl.when(slot == index)
                def _(index=index):
                    fetch_slope[index].wait()

            @pl.loop(0, D // chunk)
            def _(step):
                columns = pl.ds(pl.multiple_of(step * chunk, chunk), chunk)
                grad = product(low_ref[...], outer[slot, columns, :], NT) * slope_ref[
                    slot, :, columns
                ].astype(wide)
                bias_ref[pl.ds(place ^ slot, 1), columns] = column_sum(grad)
                low = grad.astype(low_type)
                for index in range(4):

                    @pl.when(slot == index)
                    def _(index=index):
                        inner_refs[index][:, columns] = low

        for fetch in fetch_inner:
            wait(fetch)

        @pl.loop(0, STEPS)
        def _(step):
            at = block_rows(step)
            total = second_ref[at, :]
            for index in range(4):
                total = total + product(inner_refs[index][at, :], inner[index], NT)
            hat = hat_ref[at, :]
            grad = normalize_backward(total * vectors[1:2], hat, inverse_ref[at, :])
            grad_ref[at, :] = grad
            grad_copy(step).start()
            branch_ref[at, :] = grad.astype(low_type)
            sums_ref[8:9, :] += column_sum(total * hat)
            sums_ref[9:10, :] += column_sum(total)
            sums_ref[10:11, :] += column_sum(grad)

        for step in range(STEPS):
            result_copy(step).wait()
            grad_copy(step).wait()

    return call(
        kernel,
        "middle",
        (
            shaped((L, D), low_type),
            shaped((L, D), low_type),
            shaped((8, D), wide),
            shaped((16, D), wide),
        )
        + (shaped((L, D), low_type),) * 4
        + (shaped((L, D), wide), shaped((L, D), low_type)),
        [
            scalars,
            vectors,
            hat_one,
            inverse_one,
            grad_out,
            *activated,
            *slopes,
            *flat(outers),
            *flat(inners),
        ],
        "vhvh" + "vvvv" + "hh" + "h" * (len(flat(outers)) - 1) + "a" + "h" * len(flat(inners)),
        "vvvv" + "vvvv" + "hh",
        [
            pltpu.VMEM((4, D, D), low_type),
            pltpu.VMEM((4, D, D), low_type),
            pltpu.VMEM((4, L, D), low_type),
            pltpu.VMEM((L, D), wide),
            pltpu.VMEM((L, D), low_type),
            pltpu.VMEM((L, D), wide),
            pltpu.VMEM((L, D), wide),
            pltpu.VMEM((L, D), low_type),
            pltpu.SemaphoreType.DMA((22 + 2 * STEPS,)),
        ],
        limit=32,
    )


def add_halves(scalars, near, far, incoming):
    half = near.shape[0]

    def kernel(scalar_ref, near_ref, far_ref, incoming_ref, near_out, far_out):
        near_out[...] = add_rows(near_ref[...], incoming_ref[:half, :])
        far_out[...] = add_rows(far_ref[...], incoming_ref[half:, :])

    return call(
        kernel,
        "add_halves",
        (shaped((half, D), low_type),) * 2,
        [scalars, near, far, incoming],
        "vvv",
        "vv",
    )


def input_backward(scalars, first_grad, qkv_grads, projections):
    width = D // 4

    def kernel(scalar_ref, first_in, *refs):
        left_refs = refs[:4]
        parts, refs = unflatten(refs[4:], projections)
        out, weight, first_ref, semaphores = refs
        odd = scalar_ref[1]
        fetches = [begin_weight(parts[i], odd, weight.at[i], semaphores, 2 * i) for i in range(4)]
        fetch_first = begin(first_in, first_ref, semaphores.at[8])

        @pl.loop(0, STEPS)
        def _(step):
            at = block_rows(step)
            total = 0.0
            for index in range(4):

                @pl.when(step == 0)
                def _(index=index):
                    wait(fetches[index])

                total = total + product(left_refs[index][at, :], weight[index, : 3 * width], NN)

            @pl.when(step == 0)
            def _():
                fetch_first.wait()

            first_ref[at, :] = total + first_ref[at, :]
            begin(first_ref.at[at], out.at[at], semaphores.at[9 + step])

        for step in range(STEPS):
            at = block_rows(step)
            pltpu.make_async_copy(first_ref.at[at], out.at[at], semaphores.at[9 + step]).wait()

    return call(
        kernel,
        "input_backward",
        (shaped((L, D), wide),),
        [scalars, first_grad, *qkv_grads, *flat(projections)],
        "h" + "v" * 4 + "h" * len(flat(projections)),
        "h",
        [
            pltpu.VMEM((4, 3 * width + EXTRA, D), low_type),
            pltpu.VMEM((L, D), wide),
            pltpu.SemaphoreType.DMA((9 + STEPS,)),
        ],
        limit=16,
    )[0]


def solution(mesh):
    dp_size = mesh.shape["dp"]
    tensor_size = mesh.shape["tensor"]
    masks = [1 << bit for bit in range(dp_size.bit_length() - 1)]

    def over_tensor(value, mask):
        return lax.ppermute(value, "tensor", [(i, i ^ mask) for i in range(tensor_size)])

    def over_dp(value, mask):
        return lax.ppermute(value, "dp", [(i, i ^ mask) for i in range(dp_size)])

    def body(
        tokens,
        grad_out,
        lengths,
        segment_ids,
        query_weight,
        query_bias,
        key_weight,
        value_weight,
        value_bias,
        mixer_weight,
        mixer_bias,
        first_gain,
        first_shift,
        inner_weight,
        inner_bias,
        outer_weight,
        outer_bias,
        second_gain,
        second_shift,
    ):
        width = query_weight.shape[1]
        place = lax.axis_index("tensor")
        odd = lax.axis_index("dp") % 2
        chain = [jnp.zeros((8, 128), wide)]

        def after(*values):
            held = lax.optimization_barrier((chain[0],) + values)
            return held[1:] if len(values) > 1 else held[1]

        def done(*values):
            chain[0] = lax.optimization_barrier((chain[0],) + values)[0]
            return values if len(values) > 1 else values[0]

        lines = [mixer_bias, first_gain, first_shift, outer_bias, second_gain, second_shift]
        lines = dict(enumerate(lines))
        lines[8] = jnp.pad(query_bias, (0, D - width)) + jnp.pad(
            value_bias, (2 * width, D - 3 * width)
        )
        lines[9] = inner_bias
        line_at = lax.broadcasted_iota(jnp.int32, (16, D), 0)
        vectors = jnp.zeros((16, D), low_type)
        for index, line in lines.items():
            vectors = jnp.where(line_at == index, line[None, :], vectors)
        high = lax.axis_index("dp") // 2 % 2
        scalars = jnp.concatenate([jnp.stack([place, odd, high]).astype(jnp.int32), lengths])

        def hold():
            chain[0] = tick(scalars, chain[0])

        def send(value, mask):
            return over_tensor(after(value), mask)

        def pass_y(value):
            return over_dp(after(value), masks[0])

        def land(value):
            return done(after(value))

        def stage(function, *operands):
            return done(*function(after(scalars), *operands))

        piece, own_heads = done(
            *prepare(
                scalars,
                vectors,
                [query_weight.T, key_weight.T, value_weight.T],
                mixer_weight,
            )
        )
        heads = {}

        def attend(slots, projections):
            outs = stage(attend_forward, segment_ids, tokens, projections)
            for index, slot in enumerate(slots):
                heads[slot] = outs[index :: len(slots)]

        heads_x = send(piece, 2)
        heads_core = send(own_heads, 1)
        hold()
        inner_piece, outer_piece = stage(halve, inner_weight, outer_weight)
        attend((0,), [(own_heads,)])
        heads_core = land(heads_core)
        if not LATE:
            inner_core = send(inner_weight, 1)
            attend((1,), [(heads_core,)])
        heads_x = land(heads_x)
        heads_y = pass_y(heads_x)
        inner_x = send(inner_piece, 2)
        heads_near = send(heads_x, 1)
        hold()
        if LATE:
            inner_core = send(inner_weight, 1)
            attend((1,), [(heads_core,)])
            inner_core = land(inner_core)
        if not LATE:
            inner_core = land(inner_core)
        heads_near = land(heads_near)
        outer_core = send(outer_weight, 1)
        hold()
        outer_core = land(outer_core)
        heads_y = land(heads_y)
        heads_far = send(heads_y, 1)
        inner_x = land(inner_x)
        inner_y = pass_y(inner_x)
        outer_x = send(outer_piece, 2)
        inner_near = send(inner_x, 1)
        if HOLD_A:
            hold()
        heads_far = land(heads_far)
        attend((2, 3), [(heads_x, heads_y), (heads_near, heads_far)])
        inner_near = land(inner_near)
        attended = [heads[j][0] for j in range(4)]
        inner_biases = [heads[j][1] for j in range(4)]
        projections = mixers = [
            (own_heads,),
            (heads_core,),
            (heads_x, heads_y),
            (heads_near, heads_far),
        ]
        inverse_one, normed_low, sums_one, hat_one = stage(
            mix_norm, vectors, tokens, attended, mixers
        )
        outer_x = land(outer_x)
        outer_y = pass_y(outer_x)
        outer_near = send(outer_x, 1)
        inner_y = land(inner_y)
        inner_far = send(inner_y, 1)
        if HOLD_B:
            hold()
        outer_near = land(outer_near)
        *activated, slope_one = stage(
            inner_forward, normed_low, [(inner_weight,), (inner_core,)], inner_biases[:2]
        )
        inner_far = land(inner_far)
        *more, slope_two = stage(
            inner_forward,
            normed_low,
            [(inner_x, inner_y), (inner_near, inner_far)],
            inner_biases[2:],
        )
        activated = activated + more
        inners = [(inner_weight,), (inner_core,), (inner_x, inner_y), (inner_near, inner_far)]
        outer_y = land(outer_y)
        outer_far = send(outer_y, 1)
        hold()
        outer_far = land(outer_far)
        outers = [(outer_weight,), (outer_core,), (outer_x, outer_y), (outer_near, outer_far)]
        ffn_low, branch_low, inner_bias_rows, sums_two, *rest = stage(
            middle,
            vectors,
            hat_one,
            inverse_one,
            grad_out,
            activated,
            [slope_one, slope_two],
            outers,
            inners,
        )
        *inner_lows, first_grad, layer_out = rest

        def part(left, right):
            left, right = after(left, right)
            return done(product(left, right, TN).astype(low_type))

        def add_low(left, right):
            return done(add_rows(*after(left, right)))

        waiting = []

        def flush():
            results = done(
                *finish(
                    after(scalars),
                    [one.bits[0] for one in waiting],
                    [one.pair for one in waiting],
                    [one.outputs for one in waiting],
                )
            )
            results = list(results) if isinstance(results, tuple) else [results]
            for one in waiting:
                one.result, results = results[: one.outputs], results[one.outputs :]
            waiting.clear()

        class Reduction:
            def __init__(self, outputs=1, bits=(Y_BIT, Z_BIT)):
                self.outputs, self.bits = outputs, bits
                self.todo = ["split", "split"] + ["add"] * (len(masks) - 2)
                self.todo += ["back", "join", "end"]
                self.level = 0

            def begin(self, sent):
                self.incoming = send(sent, 2)
                if HOLD_X:
                    hold()
                return self

            def across(self, value, mask):
                self.incoming = over_dp(after(value), mask)
                if HOLD_HOPS:
                    hold()

            def terms(self):
                return (self.kept,)

            def hop(self):
                if not self.todo:
                    return
                step = self.todo.pop(0)
                *terms, incoming = after(*self.terms(), self.incoming)
                if step == "split":
                    bit = self.bits[self.level]
                    sent, self.kept = stage(split_add, bit, *terms, incoming)
                    self.terms = lambda: (self.kept,)
                    self.level += 1
                    self.across(sent, bit)
                elif step in ("add", "back"):
                    self.kept = done(add_rows(terms[0], incoming))
                    mask = self.bits[1] if step == "back" else 4 << (self.level - 2)
                    self.level += 1
                    self.across(self.kept, mask)
                elif step == "join":
                    self.kept = done(join(after(scalars), self.bits[1], terms[0], incoming))
                    self.across(self.kept, self.bits[0])
                else:
                    self.pair = (terms[0], incoming)
                    waiting.append(self)
                    if len(waiting) == 4 or (len(waiting) == EARLY and len(chains) == 4):
                        flush()

        class MixedReduction(Reduction):
            def __init__(self, kept, extra):
                super().__init__()
                self.kept, self.extra = kept, extra
                self.todo = ["mixed"] * (len(masks) + 1) + ["end"]

            def hop(self):
                if not self.todo or self.todo[0] == "end":
                    super().hop()
                    return
                self.todo.pop(0)
                kept, extra, incoming = after(self.kept, self.extra, self.incoming)
                text, self.kept, self.extra = stage(
                    mixed_hop, kept, extra, incoming, self.level == 0
                )
                mask = masks[self.level] if self.level < len(masks) else masks[0]
                self.level += 1
                self.across(text, mask)

        class CrossReduction(Reduction):
            def __init__(self, near, near_partner, far, far_partner, bits):
                super().__init__(1, bits)
                sent, self.near, self.far = stage(
                    take_halves, bits[0], *after(near, near_partner, far, far_partner)
                )
                self.todo[0] = "cross"
                self.incoming = over_dp(after(sent), bits[0])
                if HOLD_Y:
                    hold()

            def hop(self):
                if self.todo and self.todo[0] == "cross":
                    self.todo.pop(0)
                    near, far, incoming = after(self.near, self.far, self.incoming)
                    self.kept, far = stage(add_halves, near, far, incoming)
                    self.level = 1
                    self.incoming = send(far, 2)
                    if HOLD_Z:
                        hold()
                else:
                    super().hop()

        partner = {}
        outer_parts, inner_parts, heads_parts = {}, {}, {}
        qkv_grads, qkv_bias = {}, {}

        def retreat(slots):
            kept = [heads[slot] for slot in slots]
            *grads, bias = stage(
                attend_backward,
                slots,
                branch_low,
                [mixers[slot] for slot in slots],
                [one[0] for one in kept],
                [one[2] for one in kept],
                [one[3] for one in kept],
            )
            qkv_grads.update(zip(slots, grads))
            qkv_bias[slots] = bias

        def split_step(name, slot):
            left, right = {
                "o": (activated[slot], ffn_low),
                "i": (normed_low, inner_lows[slot]),
                "m": (attended[slot], branch_low),
                "h": (qkv_grads.get(slot), tokens),
            }[name]
            share = part(left, right)
            if slot % 2:
                partner[name, slot - 1] = send(share, 1)
            else:
                own_share[name, slot] = share

        def own_sum(name, slot):
            return add_low(own_share[name, slot], partner[name, slot])

        own_share, chains = {}, {}
        for step in PLAN:
            name, slot = step[0], int(step[1])
            if name == "b":
                retreat(tuple(int(digit) for digit in step[1:]))
            elif name in "oimh":
                split_step(name, slot)
            elif name == "X":
                which = ("o", None, "h")[slot]
                chains[slot] = Reduction(3 if slot == 2 else 1).begin(own_sum(which, 2))
            elif name == "Y":
                chains[1] = CrossReduction(
                    own_share["i", 0],
                    partner["i", 0],
                    own_share["i", 2],
                    partner["i", 2],
                    (Z_BIT, Y_BIT),
                )
            elif name == "S":
                small = done(
                    jnp.concatenate(
                        [
                            sums_one,
                            sums_two,
                            inner_bias_rows,
                            sum(qkv_bias.values()),
                        ]
                    )
                )
                small_other = send(small, 1)
            elif name == "M":
                small = done(small + after(small_other))
                sent = done(message(own_sum("m", 2), small))
                chains[3] = MixedReduction(own_sum("m", 0), small).begin(sent)
            elif name == "B":
                tokens_grad = done(
                    input_backward(
                        after(scalars), first_grad, [qkv_grads[j] for j in range(4)], projections
                    )
                )
            else:
                if name == "H" and slot in (0, 2) and chains[slot].level == 0:
                    which = "o" if slot == 0 else "h"
                    both = (own_share[which, 0], partner[which, 0])
                    chains[slot].terms = lambda both=both: both
                chains[slot].hop()
        for chain_left in chains.values():
            while chain_left.todo:
                chain_left.hop()
        if waiting:
            flush()
        small = chains[3].extra
        outer_chain, inner_chain, heads_chain, mixer_chain = (chains[j] for j in range(4))

        totals = jnp.sum(jnp.stack([small[0], small[1], small[11]]), axis=1)
        statistics = jnp.sqrt(totals / (small[2, 0] * D))
        own_inner_bias = lax.dynamic_index_in_dim(small[24:28], place, 0, keepdims=False)
        own_qkv_bias = lax.dynamic_index_in_dim(small[32:36], place, 0, keepdims=False)
        query_grad, key_grad, value_grad = heads_chain.result
        return (
            layer_out,
            tokens_grad,
            query_grad.T,
            own_qkv_bias[:width],
            key_grad.T,
            value_grad.T,
            own_qkv_bias[2 * width : 3 * width],
            mixer_chain.result[0],
            small[18],
            small[16],
            small[17],
            inner_chain.result[0],
            own_inner_bias,
            outer_chain.result[0],
            small[10],
            small[8],
            small[9],
            statistics,
        )

    in_specs = (
        P(("dp", "tensor"), None),
        P(("dp", "tensor"), None),
        P("dp"),
        P("dp", None),
        P(None, "tensor"),
        P("tensor"),
        P(None, "tensor"),
        P(None, "tensor"),
        P("tensor"),
        P("tensor", None),
        P(),
        P(),
        P(),
        P(None, "tensor"),
        P("tensor"),
        P("tensor", None),
        P(),
        P(),
        P(),
    )
    out_specs = (
        P(("dp", "tensor"), None),
        P(("dp", "tensor"), None),
        P(None, "tensor"),
        P("tensor"),
        P(None, "tensor"),
        P(None, "tensor"),
        P("tensor"),
        P("tensor", None),
        P(),
        P(),
        P(),
        P(None, "tensor"),
        P("tensor"),
        P("tensor", None),
        P(),
        P(),
        P(),
        P(),
    )
    return jax.shard_map(body, mesh=mesh, in_specs=in_specs, out_specs=out_specs, check_vma=False)
```
